128 devices in a mesh: dp: 32 (over x, z, core), enc: 4 (over y).
Axes of the slice: x: 4, y: 4, z: 4, core: 2. Of those that a mesh axis runs over, the one named last changes fastest.
Arguments:
- hidden: bfloat16 [16384, 4096], P('dp', 'enc'), may hold values from -6 to 6
- norm_gain: float32 [4096], replicated, may hold values from 0.25 to 1.75
- w_query: bfloat16 [4096, 2048], P('dp', 'enc'), may hold values from -0.09375 to 0.09375
- w_key: bfloat16 [896, 2048], P('dp', 'enc'), may hold values from -0.1875 to 0.1875
- w_value: bfloat16 [896, 2048], P('dp', 'enc'), may hold values from -0.1875 to 0.1875
- w_out: bfloat16 [2048, 4096], P('enc', 'dp'), may hold values from -0.125 to 0.125
- w_cond: bfloat16 [4096, 896], P('dp', 'enc'), may hold values from -0.75 to 0.75
- enc_gain: float32 [896], replicated, may hold values from 0.25 to 1.75
- store: bfloat16 [1024, 128, 896], P(('dp', 'enc')), may hold values from -6 to 6
- neighbour_ids: int32 [512], P(('dp', 'enc')), may hold values from 0 to 1023, as said below
- out_grad: bfloat16 [16384, 4096], P('dp', 'enc'), may hold values from -6 to 6
Outputs:
- layer_out: bfloat16 [16384, 4096], P('dp', 'enc')
- hidden_grad: float32 [16384, 4096], P('dp', 'enc')
- query_grad: float32 [4096, 2048], P('dp', 'enc')
- key_grad: float32 [896, 2048], P('dp', 'enc')
- value_grad: float32 [896, 2048], P('dp', 'enc')
- out_weight_grad: float32 [2048, 4096], P('enc', 'dp')
- cond_grad: float32 [4096, 896], P('dp', 'enc')
The draws below stay inside these ranges and needn't reach their ends.
Inputs may be any that keep to these rules, and one draw needn't show every extreme that they name: `neighbour_ids`: slot n names a neighbour stored on a device of the same data index as the device holding slot n (device k holds rows k * 8 to (k + 1) * 8 - 1). Among the 4 slots of one device at most 2 name rows of one device, and for every data index one device is named by exactly 2 slots of each of the 4 devices.
All inputs are finite; a program needn't handle non-finite values.
Results may differ from the reference program's by a relative error of at most 0.019.
Values may be sent and summed in bfloat16 or wider, within the bound.
A program may use at most 192 MiB of HBM per device.

```python
import jax
import jax.numpy as jnp
from jax import lax

D = 4096
HEADS = 16
HSZ = 128
DE = 896
SPAN = 64
NBR = 2
NL = 128
STORE_DEV = 8
HD = 2048
TOKENS = 16384
SPANS = 256
NEIGHBOURS = 512
RQ = 4
CAP = 2
STORE = 1024
N_DP = 32
N_ENC = 4


def draw_neighbour_ids(key, part):
    hot_key, offset_key, row_key, order_key = jax.random.split(key, 4)
    device_count = NEIGHBOURS // RQ
    group_count = device_count // N_ENC
    hot_owner = jax.random.randint(hot_key, (group_count,), 0, N_ENC)
    hot_device = jnp.repeat(hot_owner, N_ENC)
    orders = jax.vmap(lambda subkey: jax.random.permutation(subkey, RQ))(jax.random.split(order_key, device_count))
    offset_draw = jax.random.randint(offset_key, (device_count, RQ), 1, N_ENC)
    owner_of = jnp.where(orders < CAP, hot_device[:, None], (hot_device[:, None] + offset_draw) % N_ENC)
    row_index = jax.random.randint(row_key, (device_count, RQ), 0, STORE_DEV)
    group_of = jnp.arange(device_count) // N_ENC
    drawn_ids = (group_of[:, None] * N_ENC + owner_of) * STORE_DEV + row_index
    return drawn_ids.reshape(NEIGHBOURS).astype(jnp.int32)


def block_levels(key, extent, cuts, least, high):
    def one(dim, shards_of):
        steps = jax.random.uniform(jax.random.fold_in(jax.random.fold_in(key, 6), dim), (shards_of,), jnp.float32, least / len(cuts), high / len(cuts))
        return jnp.repeat(jnp.exp(steps), extent[dim] // shards_of).reshape((-1,) + (1,) * (len(extent) - dim - 1))

    factor_of = one(*cuts[0])
    for cut in cuts[1:]:
        factor_of = factor_of * one(*cut)
    return factor_of


def centred(own_key, dims, deviation, bound, cuts=(), kind=jnp.bfloat16):
    level = block_levels(own_key, dims, cuts, -0.22, 0.18) if cuts else 1.0
    result = jax.random.normal(own_key, dims, jnp.float32) * deviation * level
    return jnp.minimum(jnp.maximum(result, -bound), bound).astype(kind)


def setup_inputs(seed: int = 0) -> dict:
    seeds = jax.random.split(jax.random.key(seed), 12)
    hidden = centred(seeds[0], (TOKENS, D), 1.0, 6.0, ((0, 32), (1, 4)))
    norm_gain = jnp.clip(1.0 + 0.15 * jax.random.normal(seeds[1], (D,), jnp.float32), 0.25, 1.75)
    w_query = centred(seeds[2], (D, HD), D ** -0.5, 0.09375, ((0, 32), (1, 4)))
    w_key = centred(seeds[3], (DE, HD), DE ** -0.5, 0.1875, ((0, 32), (1, 4)))
    w_value = centred(seeds[4], (DE, HD), DE ** -0.5, 0.1875, ((0, 32), (1, 4)))
    w_out = centred(seeds[5], (HD, D), HD ** -0.5, 0.125, ((0, 4), (1, 32)))
    w_cond = centred(seeds[6], (D, DE), (D // SPAN) ** -0.5, 0.75, ((0, 32), (1, 4)))
    enc_gain = jnp.clip(1.0 + 0.15 * jax.random.normal(seeds[7], (DE,), jnp.float32), 0.25, 1.75)
    store = centred(seeds[8], (STORE, NL, DE), 1.0, 6.0, ((0, 128),))
    neighbour_ids = draw_neighbour_ids(jax.random.fold_in(seeds[11], 71), 0)
    out_grad = centred(seeds[10], (TOKENS, D), 1.0, 6.0, ((0, 32), (1, 4)))
    return dict(hidden=hidden, norm_gain=norm_gain, w_query=w_query, w_key=w_key, w_value=w_value, w_out=w_out, w_cond=w_cond, enc_gain=enc_gain, store=store, neighbour_ids=neighbour_ids, out_grad=out_grad)


epsilon = 1e-05

def group_sum(left, right, groups):
    left_blocks = left.reshape(groups, -1, left.shape[-1])
    right_blocks = right.reshape(groups, -1, right.shape[-1])

    def accumulate(running, operands):
        product = lax.dot_general(operands[0], operands[1], (((0,), (0,)), ((), ())), preferred_element_type=jnp.float32)
        rounded = lax.optimization_barrier(product.astype(jnp.bfloat16))
        return (running + rounded.astype(jnp.float32), None)
    initial = jnp.zeros((left.shape[-1], right.shape[-1]), jnp.float32)
    return lax.scan(accumulate, initial, (left_blocks, right_blocks))[0]

def rounded_part(product):
    return lax.optimization_barrier(product.astype(jnp.bfloat16)).astype(jnp.float32)

def reference(hidden, norm_gain, w_query, w_key, w_value, w_out, w_cond, enc_gain, store, neighbour_ids, out_grad):
    head_cols = HD // N_ENC
    enc_cols = DE // N_ENC
    keys_len = NBR * NL
    score_scale = HSZ ** (-0.5)
    inputs = hidden.astype(jnp.float32)
    row_rstd = lax.rsqrt(lax.optimization_barrier(jnp.mean(inputs * inputs, axis=-1, keepdims=True)) + epsilon)
    normed = (inputs * row_rstd * norm_gain).astype(jnp.bfloat16)
    queries = jnp.dot(normed, w_query, preferred_element_type=jnp.float32).astype(jnp.bfloat16)
    summary = lax.optimization_barrier(jnp.mean(inputs.reshape(SPANS, SPAN, D), axis=1)).astype(jnp.bfloat16)
    condition = jnp.dot(summary, w_cond, preferred_element_type=jnp.float32).astype(jnp.bfloat16)
    span_of = (jnp.arange(NEIGHBOURS) // NBR).astype(jnp.int32)
    raw_rows = jnp.take(store, neighbour_ids, axis=0).astype(jnp.float32)
    cond_rows = jnp.take(condition, span_of, axis=0).astype(jnp.float32)
    enc_in = raw_rows + cond_rows[:, None, :]
    enc_rstd = lax.rsqrt(lax.optimization_barrier(jnp.mean(enc_in * enc_in, axis=-1, keepdims=True)) + epsilon)
    encoded = (enc_in * enc_rstd * enc_gain).astype(jnp.bfloat16)
    flat_enc = encoded.reshape(NEIGHBOURS * NL, DE)
    keys_proj = jnp.dot(flat_enc, w_key, preferred_element_type=jnp.float32).astype(jnp.bfloat16)
    values_proj = jnp.dot(flat_enc, w_value, preferred_element_type=jnp.float32).astype(jnp.bfloat16)
    query_heads = queries.reshape(SPANS, SPAN, HEADS, HSZ).astype(jnp.float32)
    key_heads = keys_proj.reshape(SPANS, keys_len, HEADS, HSZ).astype(jnp.float32)
    value_heads = values_proj.reshape(SPANS, keys_len, HEADS, HSZ).astype(jnp.float32)
    scores = jnp.einsum('cqhd,ckhd->chqk', query_heads, key_heads) * score_scale
    attn_full = jax.nn.softmax(scores, axis=-1)
    attn_weights = attn_full.astype(jnp.bfloat16)
    attended = jnp.einsum('chqk,ckhd->cqhd', attn_weights.astype(jnp.float32), value_heads).astype(jnp.bfloat16).reshape(TOKENS, HD)
    running = jnp.zeros((TOKENS, D), jnp.float32)
    for member in range(N_ENC):
        lower = member * head_cols
        upper = lower + head_cols
        running = running + rounded_part(jnp.dot(attended[:, lower:upper], w_out[lower:upper], preferred_element_type=jnp.float32))
    layer_out = (inputs + running).astype(jnp.bfloat16)
    attended_grad = jnp.dot(out_grad, w_out.T, preferred_element_type=jnp.float32).astype(jnp.bfloat16)
    out_weight_grad = group_sum(attended, out_grad, N_DP)
    grad_heads = attended_grad.reshape(SPANS, SPAN, HEADS, HSZ).astype(jnp.float32)
    prob_grad = jnp.einsum('cqhd,ckhd->chqk', grad_heads, value_heads)
    score_grad = (attn_full * (prob_grad - lax.optimization_barrier(jnp.sum(attn_full * prob_grad, axis=-1, keepdims=True))) * score_scale).astype(jnp.bfloat16)
    score_float = score_grad.astype(jnp.float32)
    query_act_grad = jnp.einsum('chqk,ckhd->cqhd', score_float, key_heads).astype(jnp.bfloat16).reshape(TOKENS, HD)
    key_act_grad = jnp.einsum('chqk,cqhd->ckhd', score_float, query_heads).astype(jnp.bfloat16).reshape(NEIGHBOURS * NL, HD)
    value_act_grad = jnp.einsum('chqk,cqhd->ckhd', attn_weights.astype(jnp.float32), grad_heads).astype(jnp.bfloat16).reshape(NEIGHBOURS * NL, HD)
    query_grad = group_sum(normed, query_act_grad, N_DP)
    key_grad = group_sum(flat_enc, key_act_grad, N_DP)
    value_grad = group_sum(flat_enc, value_act_grad, N_DP)
    enc_running = jnp.zeros((NEIGHBOURS * NL, DE), jnp.float32)
    for member in range(N_ENC):
        lower = member * head_cols
        upper = lower + head_cols
        partial_value = jnp.dot(key_act_grad[:, lower:upper], w_key[:, lower:upper].T, preferred_element_type=jnp.float32)
        partial_value = partial_value + jnp.dot(value_act_grad[:, lower:upper], w_value[:, lower:upper].T, preferred_element_type=jnp.float32)
        enc_running = enc_running + rounded_part(partial_value)
    encoded_grad = enc_running.astype(jnp.bfloat16).reshape(NEIGHBOURS, NL, DE)
    scaled_enc = enc_gain * encoded_grad.astype(jnp.float32)
    enc_mean = lax.optimization_barrier(jnp.mean(enc_in * scaled_enc, axis=-1, keepdims=True))
    slot_cond_grad = lax.optimization_barrier(jnp.sum(enc_rstd * scaled_enc - enc_in * enc_rstd ** 3 * enc_mean, axis=1))
    cond_delta = lax.optimization_barrier(jnp.sum(slot_cond_grad.reshape(SPANS, NBR, DE), axis=1)).astype(jnp.bfloat16)
    cond_grad = group_sum(summary, cond_delta, N_DP)
    summary_grad = jnp.zeros((SPANS, D), jnp.float32)
    for member in range(N_ENC):
        lower = member * enc_cols
        upper = lower + enc_cols
        summary_grad = summary_grad + rounded_part(jnp.dot(cond_delta[:, lower:upper], w_cond[:, lower:upper].T, preferred_element_type=jnp.float32))
    normed_grad = jnp.zeros((TOKENS, D), jnp.float32)
    for member in range(N_ENC):
        lower = member * head_cols
        upper = lower + head_cols
        normed_grad = normed_grad + rounded_part(jnp.dot(query_act_grad[:, lower:upper], w_query[:, lower:upper].T, preferred_element_type=jnp.float32))
    scaled = normed_grad * norm_gain
    row_mean = lax.optimization_barrier(jnp.mean(inputs * scaled, axis=-1, keepdims=True))
    hidden_grad = out_grad.astype(jnp.float32) + (row_rstd * scaled - inputs * row_rstd ** 3 * row_mean) + jnp.repeat(summary_grad / SPAN, SPAN, axis=0)
    return (layer_out, hidden_grad, query_grad, key_grad, value_grad, out_weight_grad, cond_grad)
```

```python
import functools

import jax
import jax.numpy as jnp
from jax import lax
from jax.experimental import pallas as pl
from jax.experimental.pallas import tpu as pltpu
from jax.sharding import PartitionSpec as P

MESH = pl.DeviceIdType.MESH
F32 = jnp.float32
BF16 = jnp.bfloat16
HSZ = 128
SPAN = 64
NL = 128
DE = 896
PE = 1024
EPS = 1e-05
ANY = pl.BlockSpec(memory_space=pl.ANY)
VM = pl.BlockSpec(memory_space=pltpu.VMEM)
DMA = pltpu.SemaphoreType.DMA


def place():
    d = lax.axis_index("dp")
    return d // 8, (d // 2) % 4, d % 2, lax.axis_index("enc")


def at(x, z, c, y):
    return ((x * 4 + z) * 2 + c, y)


def around(v, k):
    return (v + k) % 4


def remote(src, dst, send, recv, device):
    copy = pltpu.make_async_remote_copy(
        src, dst, send, recv, device_id=device, device_id_type=MESH
    )
    copy.start()
    return copy


def meet(peers, partner=None, has_partner=None):
    barrier = pltpu.get_barrier_semaphore()
    for peer in peers:
        pl.semaphore_signal(barrier, inc=1, device_id=peer, device_id_type=MESH)
    if partner is not None:

        @pl.when(has_partner)
        def _():
            pl.semaphore_signal(barrier, inc=1, device_id=partner, device_id_type=MESH)

        pl.semaphore_wait(barrier, jnp.where(has_partner, len(peers) + 1, len(peers)))
    else:
        pl.semaphore_wait(barrier, len(peers))


def sum_rows(out, terms, step=16):
    rows = out.shape[0]

    def body(i, carry):
        at_row = pl.ds(pl.multiple_of(i * step, step), step)
        total = terms[0][at_row].astype(F32)
        for t in terms[1:]:
            total = total + t[at_row].astype(F32)
        out[at_row] = total.astype(out.dtype)
        return carry

    lax.fori_loop(0, rows // step, body, 0)


def cols(i, n):
    return pl.ds(pl.multiple_of(i * n, n), n)


def gather_kernel(
    ids, sq, store, wq, wo, wc,
    raw, sq_all, gq, go, gc,
    ids_all, ids_s, out_rows, in_rows, tq, to, tc,
    s_small, r_small, s_row, r_row, s_t, r_t, s_x, r_x, s_z, r_z, s_c, r_c, s_loc,
):
    x, z, c, y = place()
    yp = [at(x, z, c, around(y, k)) for k in (1, 2, 3)]
    xp = [at(around(x, k), z, c, y) for k in (1, 2, 3)]
    zp = [at(x, around(z, k), c, y) for k in (1, 2, 3)]
    sib = at(x, z, 1 - c, y)
    partner = at(y, z, c, x)
    meet(yp + xp + zp + [sib], partner, x != y)

    small = []
    for k in (1, 2, 3):
        small.append(remote(ids, ids_all.at[y], s_small.at[0, k], r_small.at[0, k], yp[k - 1]))
        small.append(remote(sq, sq_all.at[y], s_small.at[1, k], r_small.at[1, k], yp[k - 1]))
    keep_ids = pltpu.make_async_copy(ids, ids_all.at[y], s_loc.at[0])
    keep_sq = pltpu.make_async_copy(sq, sq_all.at[y], s_loc.at[1])
    keep_ids.start()
    keep_sq.start()

    @pl.when(x != y)
    def _():
        for n, (w, t) in enumerate(((wq, tq), (wo, to), (wc, tc))):
            remote(w, t, s_t.at[n], r_t.at[n], partner)

    @pl.when(x == y)
    def _():
        for n, (w, t) in enumerate(((wq, tq), (wo, to), (wc, tc))):
            pltpu.make_async_copy(w, t, r_t.at[n]).start()

    keep_ids.wait()
    keep_sq.wait()
    for copy in small:
        copy.wait_recv()
    to_s = pltpu.make_async_copy(ids_all, ids_s, s_loc.at[2])
    to_s.start()
    to_s.wait()

    def picks(r):
        every = [ids_s[r, 0, k] for k in range(4)]
        owner = [(v // 8) % 4 for v in every]
        row = [v % 8 for v in every]
        rank = []
        for k in range(4):
            n = jnp.int32(0)
            for j in range(k):
                n = n + jnp.where(owner[j] == owner[k], 1, 0)
            rank.append(n)
        return owner, row, rank

    row_copies = []
    for k in (2, 1, 3):
        r = around(y, k)
        owner, row, rank = picks(r)
        for q in range(2):
            pick = jnp.int32(0)
            for j in range(4):
                pick = pick + jnp.where((owner[j] == y) & (rank[j] == q), row[j], 0)
            out_rows[k, q] = store[pick]
        row_copies.append(
            remote(out_rows.at[k], in_rows.at[y], s_row.at[k], r_row.at[k], yp[k - 1])
        )
    owner, row, rank = picks(y)
    for q in range(2):
        pick = jnp.int32(0)
        for j in range(4):
            pick = pick + jnp.where((owner[j] == y) & (rank[j] == q), row[j], 0)
        in_rows[y, q] = store[pick]

    triples = ((tq, gq, 512), (to, go, 512), (tc, gc, 256))
    first, keep = [], []
    for n, (t, g, w) in enumerate(triples):
        pltpu.make_async_copy(t, t, r_t.at[n]).wait()
        mine = g.at[z, c, :, cols(x, w)]
        local = pltpu.make_async_copy(t, mine, s_loc.at[3 + n])
        local.start()
        keep.append(local)
        for k in (2, 1, 3):
            peer = zp[k - 1] if n == 1 else xp[k - 1]
            first.append(remote(t, mine, s_x.at[n, k], r_x.at[n, k], peer))
    second = []
    for n, (t, g, w) in enumerate(triples):
        keep[n].wait()
        for copy in first[3 * n : 3 * n + 3]:
            copy.wait_recv()
        block = g.at[:, c, :, cols(x, w)] if n == 1 else g.at[z, c]
        for k in (2, 1, 3):
            peer = xp[k - 1] if n == 1 else zp[k - 1]
            second.append(remote(block, block, s_z.at[n, k], r_z.at[n, k], peer))
    third = []
    for n, (t, g, w) in enumerate(triples):
        for copy in second[3 * n : 3 * n + 3]:
            copy.wait_recv()
        third.append(remote(g.at[:, c], g.at[:, c], s_c.at[n], r_c.at[n], sib))

    for copy in row_copies:
        copy.wait_recv()
    for k in range(4):
        raw[k] = in_rows[owner[k], jnp.minimum(rank[k], 1)]
    for copy in third:
        copy.wait_recv()
    for copy in small + row_copies + first + second + third:
        copy.wait_send()

    @pl.when(x != y)
    def _():
        for n, (t, _, _) in enumerate(triples):
            pltpu.make_async_copy(t, t, s_t.at[n]).wait()


def gather_weights(ids, sq, store, wq, wo, wc):
    return pl.pallas_call(
        gather_kernel,
        out_shape=(
            jax.ShapeDtypeStruct((4, NL, DE), BF16),
            jax.ShapeDtypeStruct((4, 8, 128), F32),
            jax.ShapeDtypeStruct((4, 2, 128, 2048), BF16),
            jax.ShapeDtypeStruct((4, 2, 128, 2048), BF16),
            jax.ShapeDtypeStruct((4, 2, 128, 1024), BF16),
        ),
        in_specs=[VM] * 6,
        out_specs=(VM, VM, ANY, ANY, ANY),
        scratch_shapes=[
            pltpu.VMEM((4, 8, 128), jnp.int32),
            pltpu.SMEM((4, 8, 128), jnp.int32),
            pltpu.VMEM((4, 2, NL, DE), BF16),
            pltpu.VMEM((4, 2, NL, DE), BF16),
            pltpu.VMEM((128, 512), BF16),
            pltpu.VMEM((128, 512), BF16),
            pltpu.VMEM((128, 256), BF16),
            DMA((2, 4)), DMA((2, 4)),
            DMA((4,)), DMA((4,)),
            DMA((3,)), DMA((3,)),
            DMA((3, 4)), DMA((3, 4)),
            DMA((3, 4)), DMA((3, 4)),
            DMA((3,)), DMA((3,)),
            DMA((6,)),
        ],
        compiler_params=pltpu.CompilerParams(
            collective_id=0, has_side_effects=True, vmem_limit_bytes=32 << 20
        ),
        name="gather_weights",
    )(ids, sq, store, wq, wo, wc)


def scatter_kernel(
    qp, ap, cp, wk, wv,
    q, a, cond, gk, gv,
    rq, ra, rc, yk, yv,
    s_y, r_y, s_w, r_w, s_x, r_x, s_z, r_z, s_c, r_c, s_loc,
):
    x, z, c, y = place()
    yp = [at(x, z, c, around(y, k)) for k in (1, 2, 3)]
    xp = [at(around(x, k), z, c, y) for k in (1, 2, 3)]
    zp = [at(x, around(z, k), c, y) for k in (1, 2, 3)]
    sib = at(x, z, 1 - c, y)
    meet(yp + xp + zp + [sib])
    across = []
    for n, (w, t) in enumerate(((wk, yk), (wv, yv))):
        local = pltpu.make_async_copy(w, t.at[:, cols(y, 512)], s_loc.at[n])
        local.start()
        for k in (2, 1, 3):
            across.append(
                remote(w, t.at[:, cols(y, 512)], s_w.at[n, k], r_w.at[n, k], yp[k - 1])
            )
        local.wait()
    parts = []
    for n, (p, r) in enumerate(((cp, rc), (qp, rq), (ap, ra))):
        for k in (2, 1, 3):
            parts.append(
                remote(p.at[around(y, k)], r.at[k], s_y.at[n, k], r_y.at[n, k], yp[k - 1])
            )
    pairs = ((yk, gk), (yv, gv))
    first, keep = [], []
    for n, (t, g) in enumerate(pairs):
        for copy in across[3 * n : 3 * n + 3]:
            copy.wait_recv()
        mine = g.at[x, z, c]
        local = pltpu.make_async_copy(t, mine, s_loc.at[2 + n])
        local.start()
        keep.append(local)
        for k in (2, 1, 3):
            peer = zp[k - 1] if n else xp[k - 1]
            first.append(remote(t, mine, s_x.at[n, k], r_x.at[n, k], peer))
    second = []
    for n, (t, g) in enumerate(pairs):
        keep[n].wait()
        for copy in first[3 * n : 3 * n + 3]:
            copy.wait_recv()
        block = g.at[x, :, c] if n else g.at[:, z, c]
        for k in (2, 1, 3):
            peer = xp[k - 1] if n else zp[k - 1]
            second.append(remote(block, block, s_z.at[n, k], r_z.at[n, k], peer))
    for copy in parts[:6]:
        copy.wait_recv()
    cond[...] = cp[y] + rc[1] + rc[2] + rc[3]
    sum_rows(q, [qp.at[y], rq.at[1], rq.at[2], rq.at[3]])
    third = []
    for n, (t, g) in enumerate(pairs):
        for copy in second[3 * n : 3 * n + 3]:
            copy.wait_recv()
        third.append(remote(g.at[:, :, c], g.at[:, :, c], s_c.at[n], r_c.at[n], sib))
    for copy in parts[6:]:
        copy.wait_recv()
    sum_rows(a, [ap.at[y], ra.at[1], ra.at[2], ra.at[3]])
    for copy in third:
        copy.wait_recv()
    for copy in across + parts + first + second + third:
        copy.wait_send()


def scatter_partials(qp, ap, cp, wk, wv):
    return pl.pallas_call(
        scatter_kernel,
        out_shape=(
            jax.ShapeDtypeStruct((128, 2048), BF16),
            jax.ShapeDtypeStruct((128, 2048), BF16),
            jax.ShapeDtypeStruct((2, 1024), F32),
            jax.ShapeDtypeStruct((4, 4, 2, 32, 2048), BF16),
            jax.ShapeDtypeStruct((4, 4, 2, 32, 2048), BF16),
        ),
        in_specs=[VM] * 5,
        out_specs=(VM, VM, VM, ANY, ANY),
        scratch_shapes=[
            pltpu.VMEM((4, 128, 2048), BF16),
            pltpu.VMEM((4, 128, 2048), BF16),
            pltpu.VMEM((4, 2, 1024), F32),
            pltpu.VMEM((32, 2048), BF16),
            pltpu.VMEM((32, 2048), BF16),
            DMA((3, 4)), DMA((3, 4)),
            DMA((2, 4)), DMA((2, 4)),
            DMA((2, 4)), DMA((2, 4)),
            DMA((2, 4)), DMA((2, 4)),
            DMA((2,)), DMA((2,)),
            DMA((4,)),
        ],
        compiler_params=pltpu.CompilerParams(
            collective_id=1, has_side_effects=True, vmem_limit_bytes=32 << 20
        ),
        name="scatter_partials",
    )(qp, ap, cp, wk, wv)


def ring_kernel(
    att, qag, cd, kp, vp,
    att_all, qag_all, cd_all, ko, vo,
    b_k, b_v, t_k, t_v, u_k, u_v, w_k, w_v, x_k, x_v, p_k, p_v,
    s_y, r_y, s_d, r_d, s_c, r_c, s_1, r_1, s_2, r_2, s_3, r_3, s_loc,
):
    x, z, c, y = place()
    yp = [at(x, z, c, around(y, k)) for k in (1, 2, 3)]
    xp = [at(around(x, k), z, c, y) for k in (1, 2, 3)]
    zp = [at(x, around(z, k), c, y) for k in (1, 2, 3)]
    sib = at(x, z, 1 - c, y)
    meet(yp + xp + zp + [sib])
    swaps = [
        remote(p.at[:, :, 1 - c], b, s_c.at[n], r_c.at[n], sib)
        for n, (p, b) in enumerate(((kp, b_k), (vp, b_v)))
    ]
    keep = []
    small, ring = [], []
    for k in (1, 2, 3):
        small.append(remote(cd, cd_all.at[y], s_d.at[k], r_d.at[k], yp[k - 1]))
    for n, (src, dst) in enumerate(((att, att_all), (qag, qag_all))):
        local = pltpu.make_async_copy(src, dst.at[y], s_loc.at[n])
        local.start()
        keep.append(local)
        ring.append(remote(src, dst.at[y], s_y.at[n, 0], r_y.at[n, 0], yp[0]))
        ring.append(remote(src, dst.at[y], s_y.at[n, 1], r_y.at[n, 1], yp[2]))
    cd_all[y] = cd[...]

    sent = []
    halves = ((kp, b_k, t_k, u_k), (vp, b_v, t_v, u_v))
    for n, (p, b, t, u) in enumerate(halves):
        swaps[n].wait_recv()

        def fold(i, carry, p=p, b=b, t=t):
            t[i // 4, i % 4] = (
                p[i // 4, i % 4, c].astype(F32) + b[i // 4, i % 4].astype(F32)
            ).astype(BF16)
            return carry

        lax.fori_loop(0, 16, fold, 0)
        for k in (2, 1, 3):
            if n:
                src, peer = t.at[around(x, k)], xp[k - 1]
            else:
                src, peer = t.at[:, around(z, k)], zp[k - 1]
            sent.append(remote(src, u.at[k], s_1.at[n, k], r_1.at[n, k], peer))

    passed = []
    for n, dst in enumerate((att_all, qag_all)):
        left, right = around(y, 3), around(y, 1)
        ring[2 * n].wait_recv()
        block = dst.at[left, pl.ds(0, 64)]
        passed.append(remote(block, block, s_y.at[n, 2], r_y.at[n, 2], yp[0]))
        ring[2 * n + 1].wait_recv()
        block = dst.at[right, pl.ds(64, 64)]
        passed.append(remote(block, block, s_y.at[n, 3], r_y.at[n, 3], yp[2]))

    sent2 = []
    for n, (t, u, w, v) in enumerate(((t_k, u_k, w_k, x_k), (t_v, u_v, w_v, x_v))):
        for copy in sent[3 * n : 3 * n + 3]:
            copy.wait_recv()

        def fold(i, carry, t=t, u=u, w=w, n=n):
            own = t[x, i] if n else t[i, z]
            w[i] = (
                own.astype(F32) + u[1, i].astype(F32) + u[2, i].astype(F32) + u[3, i].astype(F32)
            ).astype(BF16)
            return carry

        lax.fori_loop(0, 4, fold, 0)
        for k in (2, 1, 3):
            if n:
                src, peer = w.at[around(z, k)], zp[k - 1]
            else:
                src, peer = w.at[around(x, k)], xp[k - 1]
            sent2.append(remote(src, v.at[k], s_2.at[n, k], r_2.at[n, k], peer))
    sent3 = []
    ends = ((w_k, x_k, p_k), (w_v, x_v, p_v))
    for n, (w, v, p) in enumerate(ends):
        for copy in sent2[3 * n : 3 * n + 3]:
            copy.wait_recv()
        own = w[z] if n else w[x]
        p[0] = (
            own.astype(F32) + v[1].astype(F32) + v[2].astype(F32) + v[3].astype(F32)
        ).astype(BF16)
        for k in (2, 1, 3):
            sent3.append(
                remote(
                    p.at[0, :, cols(around(y, k), 512)],
                    p.at[k, :, pl.ds(0, 512)],
                    s_3.at[n, k],
                    r_3.at[n, k],
                    yp[k - 1],
                )
            )
    for n, (out, p) in enumerate(((ko, p_k), (vo, p_v))):
        for copy in sent3[3 * n : 3 * n + 3]:
            copy.wait_recv()
        out[...] = (
            p[0, :, cols(y, 512)].astype(F32)
            + p[1, :, pl.ds(0, 512)].astype(F32)
            + p[2, :, pl.ds(0, 512)].astype(F32)
            + p[3, :, pl.ds(0, 512)].astype(F32)
        )
    for copy in keep:
        copy.wait()
    for copy in small + passed:
        copy.wait_recv()
    for copy in swaps + small + ring + sent + passed + sent2 + sent3:
        copy.wait_send()


def ring_gather(att, qag, cd, kp, vp):
    return pl.pallas_call(
        ring_kernel,
        out_shape=(
            jax.ShapeDtypeStruct((4, 128, 2048), BF16),
            jax.ShapeDtypeStruct((4, 128, 2048), BF16),
            jax.ShapeDtypeStruct((4, 2, 1024), F32),
            jax.ShapeDtypeStruct((32, 512), F32),
            jax.ShapeDtypeStruct((32, 512), F32),
        ),
        in_specs=[VM] * 5,
        out_specs=(VM,) * 5,
        scratch_shapes=[pltpu.VMEM((4, 4, 32, 2048), BF16)] * 4
        + [pltpu.VMEM((4, 4, 32, 2048), BF16)] * 2
        + [pltpu.VMEM((4, 32, 2048), BF16)] * 6
        + [
            DMA((2, 4)), DMA((2, 4)),
            DMA((4,)), DMA((4,)),
            DMA((2,)), DMA((2,)),
            DMA((2, 4)), DMA((2, 4)),
            DMA((2, 4)), DMA((2, 4)),
            DMA((2, 4)), DMA((2, 4)),
            DMA((2,)),
        ],
        compiler_params=pltpu.CompilerParams(
            collective_id=2, has_side_effects=True, vmem_limit_bytes=56 << 20
        ),
        name="ring_gather",
    )(att, qag, cd, kp, vp)


def reduce_kernel(
    qp, op, cp, rs,
    qo, oo, co, rs_all,
    b_q, b_o, b_c, u_q, u_o, u_c, w_q, w_o, w_c, v_q, v_o, v_c, f_q, f_o, f_c,
    s_d, r_d, s_c, r_c, s_1, r_1, s_2, r_2, s_t, r_t,
):
    x, z, c, y = place()
    yp = [at(x, z, c, around(y, k)) for k in (1, 2, 3)]
    xp = [at(around(x, k), z, c, y) for k in (1, 2, 3)]
    zp = [at(x, around(z, k), c, y) for k in (1, 2, 3)]
    sib = at(x, z, 1 - c, y)
    partner = at(y, z, c, x)
    meet(yp + xp + zp + [sib], partner, x != y)
    parts = (qp, op, cp)
    swaps = [
        remote(p.at[:, 1 - c], b, s_c.at[n], r_c.at[n], sib)
        for n, (p, b) in enumerate(zip(parts, (b_q, b_o, b_c)))
    ]
    small = [
        remote(rs, rs_all.at[y], s_d.at[k], r_d.at[k], yp[k - 1]) for k in (1, 2, 3)
    ]
    rs_all[y] = rs[...]
    widths = (512, 512, 256)
    sent = []
    for n, (p, b, u, wd) in enumerate(zip(parts, (b_q, b_o, b_c), (u_q, u_o, u_c), widths)):
        swaps[n].wait_recv()

        def fold(i, carry, p=p, b=b):
            r = pl.ds(pl.multiple_of((i % 8) * 16, 16), 16)
            b[i // 8, r] = (p[i // 8, c, r].astype(F32) + b[i // 8, r].astype(F32)).astype(BF16)
            return carry

        lax.fori_loop(0, 32, fold, 0)
        for k in (2, 1, 3):
            if n == 1:
                src, peer = b.at[:, :, cols(around(x, k), wd)], xp[k - 1]
            else:
                src, peer = b.at[around(z, k)], zp[k - 1]
            sent.append(remote(src, u.at[k], s_1.at[n, k], r_1.at[n, k], peer))
    sent2 = []
    for n, (b, u, w, v, wd) in enumerate(
        zip((b_q, b_o, b_c), (u_q, u_o, u_c), (w_q, w_o, w_c), (v_q, v_o, v_c), widths)
    ):
        for copy in sent[3 * n : 3 * n + 3]:
            copy.wait_recv()

        if n == 1:

            def fold(i, carry, b=b, u=u, w=w, wd=wd):
                r = pl.ds(pl.multiple_of((i % 8) * 16, 16), 16)
                w[i // 8, r] = (
                    b[i // 8, r, cols(x, wd)].astype(F32)
                    + u[1, i // 8, r].astype(F32)
                    + u[2, i // 8, r].astype(F32)
                    + u[3, i // 8, r].astype(F32)
                ).astype(BF16)
                return carry

            lax.fori_loop(0, 32, fold, 0)
        else:
            sum_rows(w, [b.at[z], u.at[1], u.at[2], u.at[3]])
        for k in (2, 1, 3):
            if n == 1:
                src, peer = w.at[around(z, k)], zp[k - 1]
            else:
                src, peer = w.at[:, cols(around(x, k), wd)], xp[k - 1]
            sent2.append(remote(src, v.at[k], s_2.at[n, k], r_2.at[n, k], peer))
    lasts = tuple(zip((w_q, w_o, w_c), (v_q, v_o, v_c), (f_q, f_o, f_c), (qo, oo, co), widths))
    for n, (w, v, f, out, wd) in enumerate(lasts):
        for copy in sent2[3 * n : 3 * n + 3]:
            copy.wait_recv()
        own = w.at[z] if n == 1 else w.at[:, cols(x, wd)]
        sum_rows(f, [own, v.at[1], v.at[2], v.at[3]])

        @pl.when(x != y)
        def _(f=f, out=out, n=n):
            remote(f, out, s_t.at[n], r_t.at[n], partner)

        @pl.when(x == y)
        def _(f=f, out=out, n=n):
            pltpu.make_async_copy(f, out, r_t.at[n]).start()

    for n, (w, v, f, out, wd) in enumerate(lasts):
        pltpu.make_async_copy(f, out, r_t.at[n]).wait()
    for copy in small:
        copy.wait_recv()
    for copy in swaps + small + sent + sent2:
        copy.wait_send()

    @pl.when(x != y)
    def _():
        for n, (w, v, f, out, wd) in enumerate(lasts):
            pltpu.make_async_copy(f, out, s_t.at[n]).wait()


def reduce_weights(qp, op, cp, rs):
    wide, slim = (4, 128, 2048), (4, 128, 1024)
    return pl.pallas_call(
        reduce_kernel,
        out_shape=(
            jax.ShapeDtypeStruct((128, 512), BF16),
            jax.ShapeDtypeStruct((128, 512), BF16),
            jax.ShapeDtypeStruct((128, 256), BF16),
            jax.ShapeDtypeStruct((4, 8, 128), F32),
        ),
        in_specs=[VM] * 4,
        out_specs=(VM,) * 4,
        scratch_shapes=[
            pltpu.VMEM(wide, BF16), pltpu.VMEM(wide, BF16), pltpu.VMEM(slim, BF16),
            pltpu.VMEM(wide, BF16), pltpu.VMEM((4, 4, 128, 512), BF16), pltpu.VMEM(slim, BF16),
            pltpu.VMEM((128, 2048), BF16), pltpu.VMEM((4, 128, 512), BF16),
            pltpu.VMEM((128, 1024), BF16),
            pltpu.VMEM((4, 128, 512), BF16), pltpu.VMEM((4, 128, 512), BF16),
            pltpu.VMEM((4, 128, 256), BF16),
            pltpu.VMEM((128, 512), BF16), pltpu.VMEM((128, 512), BF16),
            pltpu.VMEM((128, 256), BF16),
            DMA((4,)), DMA((4,)),
            DMA((3,)), DMA((3,)),
            DMA((3, 4)), DMA((3, 4)),
            DMA((3, 4)), DMA((3, 4)),
            DMA((3,)), DMA((3,)),
        ],
        compiler_params=pltpu.CompilerParams(
            collective_id=3, has_side_effects=True, vmem_limit_bytes=56 << 20
        ),
        name="reduce_weights",
    )(qp, op, cp, rs)


def dot_nn(a, b):
    return jnp.dot(a, b, preferred_element_type=F32)


def dot_nt(a, b):
    return lax.dot_general(a, b, (((1,), (1,)), ((), ())), preferred_element_type=F32)


def dot_tn(a, b):
    return lax.dot_general(a, b, (((0,), (0,)), ((), ())), preferred_element_type=F32)


def attention_kernel(q_ref, g_ref, k_ref, v_ref, att_ref, qag_ref, kag_ref, vag_ref):
    scale = HSZ ** (-0.5)
    for h in range(q_ref.shape[1] // HSZ):
        lanes = slice(h * HSZ, (h + 1) * HSZ)
        for s in range(2):
            rows, keys = slice(s * SPAN, (s + 1) * SPAN), slice(s * 2 * NL, (s + 1) * 2 * NL)
            q, g = q_ref[rows, lanes], g_ref[rows, lanes]
            k, v = k_ref[keys, lanes], v_ref[keys, lanes]
            score = dot_nt(q, k) * scale
            e = jnp.exp(score - jnp.max(score, axis=-1, keepdims=True))
            full = e / jnp.sum(e, axis=-1, keepdims=True)
            weights = full.astype(BF16)
            att_ref[rows, lanes] = dot_nn(weights, v).astype(BF16)
            pg = dot_nt(g, v)
            sg = (full * (pg - jnp.sum(full * pg, axis=-1, keepdims=True)) * scale).astype(BF16)
            qag_ref[rows, lanes] = dot_nn(sg, k).astype(BF16)
            kag_ref[keys, lanes] = dot_tn(sg, q).astype(BF16)
            vag_ref[keys, lanes] = dot_tn(weights, g).astype(BF16)


def attention(q, g, k, v):
    few = pl.BlockSpec((128, 256), lambda h: (0, h))
    many = pl.BlockSpec((512, 256), lambda h: (0, h))
    return pl.pallas_call(
        attention_kernel,
        grid=(8,),
        out_shape=(
            jax.ShapeDtypeStruct((128, 2048), BF16),
            jax.ShapeDtypeStruct((128, 2048), BF16),
            jax.ShapeDtypeStruct((512, 2048), BF16),
            jax.ShapeDtypeStruct((512, 2048), BF16),
        ),
        in_specs=[few, few, many, many],
        out_specs=(few, few, many, many),
        name="attention",
    )(q, g, k, v)


def wide_columns(n):
    r = lax.broadcasted_iota(jnp.int32, (28 * n, 32 * n), 0)
    s = lax.broadcasted_iota(jnp.int32, (28 * n, 32 * n), 1)
    return ((r // 28 == s // 32) & (r % 28 == s % 32)).astype(BF16)


def lines(v):
    return jnp.pad(v.reshape(4, 128), ((0, 4), (0, 0)))


def shards(
    hidden, norm_gain, w_query, w_key, w_value, w_out, w_cond, enc_gain, store, neighbour_ids,
    out_grad,
):
    y = lax.axis_index("enc")
    xf = hidden.astype(F32)
    gain = lax.dynamic_slice_in_dim(norm_gain, y * 1024, 1024)
    sq = lines(jnp.sum(xf * xf, axis=-1))
    summary = jnp.mean(xf.reshape(8, SPAN, 1024), axis=1).astype(BF16)
    ids = jnp.pad(neighbour_ids.reshape(1, 4), ((0, 7), (0, 124)))
    wc = dot_nn(w_cond, wide_columns(8)).astype(BF16)
    raw, sq_all, gq, go, gc = gather_weights(ids, sq, store, w_query, w_out.T, wc)
    gq, go, gc = gq.reshape(1024, 2048), go.reshape(1024, 2048), gc.reshape(1024, 1024)

    rstd = lax.rsqrt(jnp.sum(sq_all, axis=0)[:4].reshape(512, 1) / 4096 + EPS)
    normed = (xf * rstd * gain).astype(BF16)
    qp = dot_nn(normed, gq).astype(BF16).reshape(4, 128, 2048)
    ap = dot_nn(out_grad, go).astype(BF16).reshape(4, 128, 2048)
    cp = dot_nn(summary, gc).reshape(4, 2, 1024)
    wk = jnp.pad(w_key, ((0, 4), (0, 0)))
    wv = jnp.pad(w_value, ((0, 4), (0, 0)))
    q, ag, cond, gk, gv = scatter_partials(qp, ap, cp, wk, wv)
    gk, gv = gk.reshape(PE, 2048), gv.reshape(PE, 2048)

    egain = jnp.pad(enc_gain.reshape(32, 28), ((0, 0), (0, 4))).reshape(PE)
    rawp = dot_nn(raw.reshape(512, DE), wide_columns(32))
    cond_rows = cond.astype(BF16).astype(F32)
    enc_in = (rawp.reshape(2, 256, PE) + cond_rows[:, None, :]).reshape(512, PE)
    enc_rstd = lax.rsqrt(jnp.sum(enc_in * enc_in, axis=-1, keepdims=True) / DE + EPS)
    encoded = (enc_in * enc_rstd * egain).astype(BF16)
    keys = dot_nn(encoded, gk).astype(BF16)
    values = dot_nn(encoded, gv).astype(BF16)
    att, qag, kag, vag = attention(q, ag, keys, values)
    kp = dot_tn(encoded, kag).astype(BF16).reshape(4, 4, 2, 32, 2048)
    vp = dot_tn(encoded, vag).astype(BF16).reshape(4, 4, 2, 32, 2048)
    eg = (dot_nt(kag, gk) + dot_nt(vag, gv)).astype(BF16).astype(F32)
    ey = egain * eg
    emean = jnp.sum(enc_in * ey, axis=-1, keepdims=True) / DE
    slot = jnp.sum(
        (enc_rstd * ey - enc_in * enc_rstd**3 * emean).reshape(2, 256, PE), axis=1
    )
    cd = slot.astype(BF16).astype(F32)
    att_all, qag_all, cd_all, kg, vg = ring_gather(att, qag, cd, kp, vp)
    att_all, qag_all = att_all.reshape(512, 2048), qag_all.reshape(512, 2048)
    cd_all = cd_all.reshape(8, PE).astype(BF16)

    layer_out = (xf + dot_nt(att_all, go)).astype(BF16)
    op = dot_tn(out_grad, att_all).astype(BF16).reshape(4, 2, 128, 2048)
    gp = dot_tn(normed, qag_all).astype(BF16).reshape(4, 2, 128, 2048)
    hp = dot_tn(summary, cd_all).astype(BF16).reshape(4, 2, 128, 1024)
    scaled = dot_nt(qag_all, gq) * gain
    rs = lines(jnp.sum(xf * scaled, axis=-1))
    summary_grad = dot_nt(cd_all, gc)
    qo, oo, co, rs_all = reduce_weights(gp, op, hp, rs)

    row_mean = jnp.sum(rs_all, axis=0)[:4].reshape(512, 1) / 4096
    hidden_grad = (
        out_grad.astype(F32)
        + (rstd * scaled - xf * rstd**3 * row_mean)
        + jnp.repeat(summary_grad / SPAN, SPAN, axis=0)
    )
    cond_grad = co.astype(F32).reshape(128, 8, 32)[:, :, :28].reshape(128, 224)
    return (
        layer_out,
        hidden_grad,
        qo.astype(F32),
        kg[:28],
        vg[:28],
        oo.T.astype(F32),
        cond_grad,
    )


def solution(mesh):
    placed = (
        P("dp", "enc"), P(), P("dp", "enc"), P("dp", "enc"), P("dp", "enc"), P("enc", "dp"),
        P("dp", "enc"), P(), P(("dp", "enc"), None, None), P(("dp", "enc")), P("dp", "enc"),
    )
    return jax.shard_map(
        shards,
        mesh=mesh,
        in_specs=placed,
        out_specs=(
            P("dp", "enc"), P("dp", "enc"), P("dp", "enc"), P("dp", "enc"), P("dp", "enc"),
            P("enc", "dp"), P("dp", "enc"),
        ),
        check_vma=False,
    )
```

```python
import functools

import jax
import jax.numpy as jnp
from jax import lax
from jax.experimental import pallas as pl
from jax.experimental.pallas import tpu as pltpu
from jax.sharding import PartitionSpec as P

MESH = pl.DeviceIdType.MESH
F32 = jnp.float32
BF16 = jnp.bfloat16
HSZ = 128
SPAN = 64
NL = 128
DE = 896
PE = 1024
EPS = 1e-05
ANY = pl.BlockSpec(memory_space=pl.ANY)
VM = pl.BlockSpec(memory_space=pltpu.VMEM)
DMA = pltpu.SemaphoreType.DMA


def place():
    d = lax.axis_index("dp")
    return d // 8, (d // 2) % 4, d % 2, lax.axis_index("enc")


def at(x, z, c, y):
    return ((x * 4 + z) * 2 + c, y)


def around(v, k):
    return (v + k) % 4


def remote(src, dst, send, recv, device):
    copy = pltpu.make_async_remote_copy(
        src, dst, send, recv, device_id=device, device_id_type=MESH
    )
    copy.start()
    return copy


def meet(peers, partner=None, has_partner=None):
    barrier = pltpu.get_barrier_semaphore()
    for peer in peers:
        pl.semaphore_signal(barrier, inc=1, device_id=peer, device_id_type=MESH)
    if partner is not None:

        @pl.when(has_partner)
        def _():
            pl.semaphore_signal(barrier, inc=1, device_id=partner, device_id_type=MESH)

        pl.semaphore_wait(barrier, jnp.where(has_partner, len(peers) + 1, len(peers)))
    else:
        pl.semaphore_wait(barrier, len(peers))


def sum_rows(out, terms, step=16):
    rows = out.shape[0]

    def body(i, carry):
        at_row = pl.ds(pl.multiple_of(i * step, step), step)
        total = terms[0][at_row].astype(F32)
        for t in terms[1:]:
            total = total + t[at_row].astype(F32)
        out[at_row] = total.astype(out.dtype)
        return carry

    lax.fori_loop(0, rows // step, body, 0)


def cols(i, n):
    return pl.ds(pl.multiple_of(i * n, n), n)


def pick_rows(ids_s, r):
    every = [ids_s[r, 0, k] for k in range(4)]
    owner = [(v // 8) % 4 for v in every]
    row = [v % 8 for v in every]
    rank = []
    for k in range(4):
        n = jnp.int32(0)
        for j in range(k):
            n = n + jnp.where(owner[j] == owner[k], 1, 0)
        rank.append(n)
    return owner, row, rank


class Plane:
    def __init__(self, put, line, cut, whole, axes, sems):
        self.put, self.line, self.cut, self.whole = put, line, cut, whole
        self.x, self.z, self.xp, self.zp, self.sib = axes
        self.s, self.r = sems
        self.one, self.two, self.on, self.last = [[], []], [[], []], [[], []], None

    def first(self):
        for h in range(2):
            src, dst, keep = self.put(h)
            for k in (2, 1, 3):
                peer = (self.zp if h else self.xp)[k - 1]
                self.one[h].append(remote(src, dst, self.s.at[h, k], self.r.at[h, k], peer))
            if keep is not None:
                copy = pltpu.make_async_copy(src, dst, self.s.at[h, 0])
                copy.start()
                copy.wait()

    def second(self):
        for h in range(2):
            for copy in self.one[h]:
                copy.wait_recv()
            block = self.line(h, self.x if h else self.z)
            for k in (1, 3):
                peer = (self.xp if h else self.zp)[k - 1]
                self.two[h].append(
                    remote(block, block, self.s.at[h, 3 + k], self.r.at[h, 3 + k], peer)
                )

    def relay(self):
        for h in range(2):
            place = self.x if h else self.z
            for j, k in ((0, 1), (1, 3)):
                self.two[h][j].wait_recv()
                block = self.cut(h, around(place, 4 - k), j)
                peer = (self.xp if h else self.zp)[k - 1]
                self.on[h].append(
                    remote(block, block, self.s.at[h, 7 + k], self.r.at[h, 7 + k], peer)
                )

    def swap(self):
        for copy in self.on[0] + self.on[1]:
            copy.wait_recv()
        self.last = remote(self.whole, self.whole, self.s.at[0, 5], self.r.at[0, 5], self.sib)

    def sent(self):
        every = self.one[0] + self.one[1] + self.two[0] + self.two[1]
        for copy in every + self.on[0] + self.on[1] + [self.last]:
            copy.wait_send()


def forward_kernel(
    ids, sq, gain, xs, og, sm, store, wq, wo, wc, wk, wv,
    raw, sq_all, q, a, cond, nt, ogt, hq, ho, hc, gk, gv,
    ids_all, ids_s, out_rows, in_rows, tq, to, tc, yk, yv, gq, go, gc,
    normed, qp, ap, cp, rq, ra, rc,
    s_small, r_small, s_row, r_row, s_t, r_t, s_p, r_p, s_w, r_w, s_y, r_y, s_loc, s_out,
):
    x, z, c, y = place()
    yp = [at(x, z, c, around(y, k)) for k in (1, 2, 3)]
    xp = [at(around(x, k), z, c, y) for k in (1, 2, 3)]
    zp = [at(x, around(z, k), c, y) for k in (1, 2, 3)]
    sib = at(x, z, 1 - c, y)
    partner = at(y, z, c, x)
    axes = (x, z, xp, zp, sib)
    meet(yp + xp + zp + [sib], partner, x != y)

    moves = ((wq, tq), (wo, to), (wc, tc))

    @pl.when(x != y)
    def _():
        for n, (w, t) in enumerate(moves):
            remote(w, t, s_t.at[n], r_t.at[n], partner)

    @pl.when(x == y)
    def _():
        for n, (w, t) in enumerate(moves):
            pltpu.make_async_copy(w, t, r_t.at[n]).start()

    small = []
    for k in (1, 2, 3):
        small.append(remote(ids, ids_all.at[y], s_small.at[0, k], r_small.at[0, k], yp[k - 1]))
    for k in (1, 2, 3):
        small.append(remote(sq, sq_all.at[y], s_small.at[1, k], r_small.at[1, k], yp[k - 1]))
    across = []
    for n, (w, t) in enumerate(((wk, yk), (wv, yv))):
        for k in (2, 1, 3):
            across.append(
                remote(w, t.at[:, cols(y, 512)], s_w.at[n, k], r_w.at[n, k], yp[k - 1])
            )
        t[:, cols(y, 512)] = w[...]
    ids_all[y] = ids[...]
    sq_all[y] = sq[...]
    for copy in small[:3]:
        copy.wait_recv()
    to_s = pltpu.make_async_copy(ids_all, ids_s, s_loc.at[0])
    to_s.start()
    to_s.wait()

    row_copies = []
    for k in (2, 1, 3, 0):
        owner, row, rank = pick_rows(ids_s, around(y, k))
        for n in range(2):
            pick = jnp.int32(0)
            for j in range(4):
                pick = pick + jnp.where((owner[j] == y) & (rank[j] == n), row[j], 0)
            if k:
                out_rows[k, n] = store[pick]
            else:
                in_rows[y, n] = store[pick]
        if k:
            row_copies.append(
                remote(out_rows.at[k], in_rows.at[y], s_row.at[k], r_row.at[k], yp[k - 1])
            )

    def weight(n, t, g, w):
        def put(h):
            rows = pl.ds(64 * h, 64)
            return t.at[rows], g.at[z, c, rows, cols(x, w)], True

        def line(h, i):
            if h:
                return g.at[:, c, pl.ds(64, 64), cols(i, w)]
            return g.at[i, c, pl.ds(0, 64)]

        def cut(h, i, j):
            if h:
                return g.at[:, c, pl.ds(64 + 32 * j, 32), cols(i, w)]
            return g.at[i, c, pl.ds(32 * j, 32)]

        return Plane(put, line, cut, g.at[:, c], axes, (s_p.at[n], r_p.at[n]))

    pq, po, pc = weight(0, tq, gq, 512), weight(1, to, go, 512), weight(2, tc, gc, 256)

    def kv_put(h):
        return (yv, gv.at[x, z, c], True) if h else (yk, gk.at[x, z, c], True)

    def kv_line(h, i):
        return gv.at[i, :, c] if h else gk.at[:, i, c]

    def kv_cut(h, i, j):
        if h:
            return gv.at[i, pl.ds(2 * j, 2), c]
        return gk.at[pl.ds(2 * j, 2), i, c]

    def arrived(n, w, t):
        pltpu.make_async_copy(w, t, r_t.at[n]).wait()

    arrived(0, wq, tq)
    pq.first()
    arrived(1, wo, to)
    po.first()
    pq.second()
    arrived(2, wc, tc)
    pc.first()
    for copy in small[3:]:
        copy.wait_recv()
    total = sq_all[0] + sq_all[1] + sq_all[2] + sq_all[3]
    rstd = lax.rsqrt(total / 4096 + EPS).T
    for j in range(4):
        rows = slice(128 * j, 128 * (j + 1))
        normed[rows] = (xs[rows].astype(F32) * rstd[:, j : j + 1] * gain[...]).astype(BF16)
    po.second()
    pq.relay()
    for copy in across:
        copy.wait_recv()
    pk = KeyPlane(kv_put, kv_line, kv_cut, (gk.at[:, :, c], gv.at[:, :, c]), axes, (s_p.at[3], r_p.at[3]))
    pk.first()
    pc.second()
    pq.swap()
    po.relay()

    parts, outs = [], []

    def partial(n, act, g, h, p, r, plane):
        plane.last.wait_recv()
        keep = pltpu.make_async_copy(g, h, s_out.at[n])
        keep.start()
        outs.append(keep)

        def tile(i, carry):
            lanes = cols(i, 256)
            w = g[:, :, :, lanes].reshape(1024, 256)
            p[:, :, lanes] = dot_nn(act[...], w).astype(BF16).reshape(4, 128, 256)
            return carry

        lax.fori_loop(0, 8, tile, 0)
        for k in (2, 1, 3):
            parts.append(
                remote(p.at[around(y, k)], r.at[k], s_y.at[n, k], r_y.at[n, k], yp[k - 1])
            )

    partial(0, normed, gq, hq, qp, rq, pq)
    pk.second()
    po.swap()
    pc.relay()
    partial(1, og, go, ho, ap, ra, po)
    pk.relay()
    pc.swap()
    for j in range(4):
        rows = slice(128 * j, 128 * (j + 1))
        nt[:, rows] = normed[rows].T
        ogt[:, rows] = og[rows].T
    pc.last.wait_recv()
    keep = pltpu.make_async_copy(gc, hc, s_out.at[2])
    keep.start()
    outs.append(keep)
    for i in range(4):
        lanes = slice(256 * i, 256 * (i + 1))
        w = gc[:, :, :, lanes].reshape(1024, 256)
        cp[:, lanes] = dot_nn(sm[...], w)
    for j in range(4):
        rc[j + 4] = cp[2 * j : 2 * j + 2]
    for k in (2, 1, 3):
        parts.append(
            remote(rc.at[4 + around(y, k)], rc.at[k], s_y.at[2, k], r_y.at[2, k], yp[k - 1])
        )
    for copy in row_copies:
        copy.wait_recv()
    owner, row, rank = pick_rows(ids_s, y)
    for k in range(4):
        raw[k] = in_rows[owner[k], jnp.minimum(rank[k], 1)]
    pk.swap()
    for copy in parts[:3]:
        copy.wait_recv()
    sum_rows(q, [qp.at[y], rq.at[1], rq.at[2], rq.at[3]])
    for copy in parts[3:]:
        copy.wait_recv()
    sum_rows(a, [ap.at[y], ra.at[1], ra.at[2], ra.at[3]])
    cond[...] = rc[4 + y] + rc[1] + rc[2] + rc[3]
    for copy in pk.last:
        copy.wait_recv()
    for copy in outs:
        copy.wait()
    for copy in small + across + row_copies + parts:
        copy.wait_send()
    for plane in (pq, po, pc, pk):
        plane.sent()

    @pl.when(x != y)
    def _():
        for n, (w, t) in enumerate(moves):
            pltpu.make_async_copy(w, t, s_t.at[n]).wait()


class KeyPlane(Plane):
    def swap(self):
        for copy in self.on[0] + self.on[1]:
            copy.wait_recv()
        self.last = [
            remote(ref, ref, self.s.at[n, 5], self.r.at[n, 5], self.sib)
            for n, ref in enumerate(self.whole)
        ]

    def sent(self):
        every = self.one[0] + self.one[1] + self.two[0] + self.two[1]
        for copy in every + self.on[0] + self.on[1] + self.last:
            copy.wait_send()


def forward(ids, sq, gain, xs, og, sm, store, wq, wo, wc, wk, wv):
    wide, slim, keys = (4, 2, 128, 2048), (4, 2, 128, 1024), (4, 4, 2, 32, 2048)
    shape = jax.ShapeDtypeStruct
    return pl.pallas_call(
        forward_kernel,
        out_shape=(
            shape((4, NL, DE), BF16),
            shape((4, 8, 128), F32),
            shape((128, 2048), BF16),
            shape((128, 2048), BF16),
            shape((2, 1024), F32),
            shape((1024, 512), BF16),
            shape((1024, 512), BF16),
            shape(wide, BF16),
            shape(wide, BF16),
            shape(slim, BF16),
            shape(keys, BF16),
            shape(keys, BF16),
        ),
        in_specs=[VM] * 12,
        out_specs=(VM,) * 7 + (ANY,) * 5,
        scratch_shapes=[
            pltpu.VMEM((4, 8, 128), jnp.int32),
            pltpu.SMEM((4, 8, 128), jnp.int32),
            pltpu.VMEM((4, 2, NL, DE), BF16),
            pltpu.VMEM((4, 2, NL, DE), BF16),
            pltpu.VMEM((128, 512), BF16),
            pltpu.VMEM((128, 512), BF16),
            pltpu.VMEM((128, 256), BF16),
            pltpu.VMEM((32, 2048), BF16),
            pltpu.VMEM((32, 2048), BF16),
            pltpu.VMEM(wide, BF16),
            pltpu.VMEM(wide, BF16),
            pltpu.VMEM(slim, BF16),
            pltpu.VMEM((512, 1024), BF16),
            pltpu.VMEM((4, 128, 2048), BF16),
            pltpu.VMEM((4, 128, 2048), BF16),
            pltpu.VMEM((8, 1024), F32),
            pltpu.VMEM((4, 128, 2048), BF16),
            pltpu.VMEM((4, 128, 2048), BF16),
            pltpu.VMEM((8, 2, 1024), F32),
            DMA((2, 4)), DMA((2, 4)),
            DMA((4,)), DMA((4,)),
            DMA((3,)), DMA((3,)),
            DMA((4, 2, 11)), DMA((4, 2, 11)),
            DMA((2, 4)), DMA((2, 4)),
            DMA((3, 4)), DMA((3, 4)),
            DMA((1,)),
            DMA((3,)),
        ],
        compiler_params=pltpu.CompilerParams(
            collective_id=0, has_side_effects=True, vmem_limit_bytes=52 << 20
        ),
        name="forward",
    )(ids, sq, gain, xs, og, sm, store, wq, wo, wc, wk, wv)


def ring_kernel(
    att, qag, cd, kp, vp,
    att_all, qag_all, cd_all, ko, vo,
    b_k, b_v, t_k, t_v, u_k, u_v, w_k, w_v, x_k, x_v, p_k, p_v,
    s_y, r_y, s_d, r_d, s_c, r_c, s_1, r_1, s_2, r_2, s_3, r_3, s_loc,
):
    x, z, c, y = place()
    yp = [at(x, z, c, around(y, k)) for k in (1, 2, 3)]
    xp = [at(around(x, k), z, c, y) for k in (1, 2, 3)]
    zp = [at(x, around(z, k), c, y) for k in (1, 2, 3)]
    sib = at(x, z, 1 - c, y)
    meet(yp + xp + zp + [sib])
    swaps = [
        remote(p.at[:, :, 1 - c], b, s_c.at[n], r_c.at[n], sib)
        for n, (p, b) in enumerate(((kp, b_k), (vp, b_v)))
    ]
    keep = []
    small, ring = [], []
    for k in (1, 2, 3):
        small.append(remote(cd, cd_all.at[y], s_d.at[k], r_d.at[k], yp[k - 1]))
    for n, (src, dst) in enumerate(((att, att_all), (qag, qag_all))):
        local = pltpu.make_async_copy(src, dst.at[y], s_loc.at[n])
        local.start()
        keep.append(local)
        ring.append(remote(src, dst.at[y], s_y.at[n, 0], r_y.at[n, 0], yp[0]))
        ring.append(remote(src, dst.at[y], s_y.at[n, 1], r_y.at[n, 1], yp[2]))
    cd_all[y] = cd[...]

    sent = []
    halves = ((kp, b_k, t_k, u_k), (vp, b_v, t_v, u_v))
    for n, (p, b, t, u) in enumerate(halves):
        swaps[n].wait_recv()

        def fold(i, carry, p=p, b=b, t=t):
            t[i // 4, i % 4] = (
                p[i // 4, i % 4, c].astype(F32) + b[i // 4, i % 4].astype(F32)
            ).astype(BF16)
            return carry

        lax.fori_loop(0, 16, fold, 0)
        for k in (2, 1, 3):
            if n:
                src, peer = t.at[around(x, k)], xp[k - 1]
            else:
                src, peer = t.at[:, around(z, k)], zp[k - 1]
            sent.append(remote(src, u.at[k], s_1.at[n, k], r_1.at[n, k], peer))

    passed = []
    for n, dst in enumerate((att_all, qag_all)):
        left, right = around(y, 3), around(y, 1)
        ring[2 * n].wait_recv()
        block = dst.at[left, pl.ds(0, 64)]
        passed.append(remote(block, block, s_y.at[n, 2], r_y.at[n, 2], yp[0]))
        ring[2 * n + 1].wait_recv()
        block = dst.at[right, pl.ds(64, 64)]
        passed.append(remote(block, block, s_y.at[n, 3], r_y.at[n, 3], yp[2]))

    sent2 = []
    for n, (t, u, w, v) in enumerate(((t_k, u_k, w_k, x_k), (t_v, u_v, w_v, x_v))):
        for copy in sent[3 * n : 3 * n + 3]:
            copy.wait_recv()

        def fold(i, carry, t=t, u=u, w=w, n=n):
            own = t[x, i] if n else t[i, z]
            w[i] = (
                own.astype(F32) + u[1, i].astype(F32) + u[2, i].astype(F32) + u[3, i].astype(F32)
            ).astype(BF16)
            return carry

        lax.fori_loop(0, 4, fold, 0)
        for k in (2, 1, 3):
            if n:
                src, peer = w.at[around(z, k)], zp[k - 1]
            else:
                src, peer = w.at[around(x, k)], xp[k - 1]
            sent2.append(remote(src, v.at[k], s_2.at[n, k], r_2.at[n, k], peer))
    sent3 = []
    ends = ((w_k, x_k, p_k), (w_v, x_v, p_v))
    for n, (w, v, p) in enumerate(ends):
        for copy in sent2[3 * n : 3 * n + 3]:
            copy.wait_recv()
        own = w[z] if n else w[x]
        p[0] = (
            own.astype(F32) + v[1].astype(F32) + v[2].astype(F32) + v[3].astype(F32)
        ).astype(BF16)
        for k in (2, 1, 3):
            sent3.append(
                remote(
                    p.at[0, :, cols(around(y, k), 512)],
                    p.at[k, :, pl.ds(0, 512)],
                    s_3.at[n, k],
                    r_3.at[n, k],
                    yp[k - 1],
                )
            )
    for n, (out, p) in enumerate(((ko, p_k), (vo, p_v))):
        for copy in sent3[3 * n : 3 * n + 3]:
            copy.wait_recv()
        out[...] = (
            p[0, :, cols(y, 512)].astype(F32)
            + p[1, :, pl.ds(0, 512)].astype(F32)
            + p[2, :, pl.ds(0, 512)].astype(F32)
            + p[3, :, pl.ds(0, 512)].astype(F32)
        )
    for copy in keep:
        copy.wait()
    for copy in small + passed:
        copy.wait_recv()
    for copy in swaps + small + ring + sent + passed + sent2 + sent3:
        copy.wait_send()


def ring_gather(att, qag, cd, kp, vp):
    return pl.pallas_call(
        ring_kernel,
        out_shape=(
            jax.ShapeDtypeStruct((4, 128, 2048), BF16),
            jax.ShapeDtypeStruct((4, 128, 2048), BF16),
            jax.ShapeDtypeStruct((4, 2, 1024), F32),
            jax.ShapeDtypeStruct((32, 512), F32),
            jax.ShapeDtypeStruct((32, 512), F32),
        ),
        in_specs=[VM] * 5,
        out_specs=(VM,) * 5,
        scratch_shapes=[pltpu.VMEM((4, 4, 32, 2048), BF16)] * 4
        + [pltpu.VMEM((4, 4, 32, 2048), BF16)] * 2
        + [pltpu.VMEM((4, 32, 2048), BF16)] * 6
        + [
            DMA((2, 4)), DMA((2, 4)),
            DMA((4,)), DMA((4,)),
            DMA((2,)), DMA((2,)),
            DMA((2, 4)), DMA((2, 4)),
            DMA((2, 4)), DMA((2, 4)),
            DMA((2, 4)), DMA((2, 4)),
            DMA((2,)),
        ],
        compiler_params=pltpu.CompilerParams(
            collective_id=2, has_side_effects=True, vmem_limit_bytes=56 << 20
        ),
        name="ring_gather",
    )(att, qag, cd, kp, vp)


def reduce_kernel(
    qp, op, cp, rs,
    qo, oo, co, rs_all,
    b_q, b_o, b_c, u_q, u_o, u_c, w_q, w_o, w_c, v_q, v_o, v_c, f_q, f_o, f_c,
    s_d, r_d, s_c, r_c, s_1, r_1, s_2, r_2, s_t, r_t,
):
    x, z, c, y = place()
    yp = [at(x, z, c, around(y, k)) for k in (1, 2, 3)]
    xp = [at(around(x, k), z, c, y) for k in (1, 2, 3)]
    zp = [at(x, around(z, k), c, y) for k in (1, 2, 3)]
    sib = at(x, z, 1 - c, y)
    partner = at(y, z, c, x)
    meet(yp + xp + zp + [sib], partner, x != y)
    parts = (qp, op, cp)
    swaps = [
        remote(p.at[:, 1 - c], b, s_c.at[n], r_c.at[n], sib)
        for n, (p, b) in enumerate(zip(parts, (b_q, b_o, b_c)))
    ]
    small = [
        remote(rs, rs_all.at[y], s_d.at[k], r_d.at[k], yp[k - 1]) for k in (1, 2, 3)
    ]
    rs_all[y] = rs[...]
    widths = (512, 512, 256)
    sent = []
    for n, (p, b, u, wd) in enumerate(zip(parts, (b_q, b_o, b_c), (u_q, u_o, u_c), widths)):
        swaps[n].wait_recv()

        def fold(i, carry, p=p, b=b):
            r = pl.ds(pl.multiple_of((i % 8) * 16, 16), 16)
            b[i // 8, r] = (p[i // 8, c, r].astype(F32) + b[i // 8, r].astype(F32)).astype(BF16)
            return carry

        lax.fori_loop(0, 32, fold, 0)
        for k in (2, 1, 3):
            if n == 1:
                src, peer = b.at[:, :, cols(around(x, k), wd)], xp[k - 1]
            else:
                src, peer = b.at[around(z, k)], zp[k - 1]
            sent.append(remote(src, u.at[k], s_1.at[n, k], r_1.at[n, k], peer))
    sent2 = []
    for n, (b, u, w, v, wd) in enumerate(
        zip((b_q, b_o, b_c), (u_q, u_o, u_c), (w_q, w_o, w_c), (v_q, v_o, v_c), widths)
    ):
        for copy in sent[3 * n : 3 * n + 3]:
            copy.wait_recv()

        if n == 1:

            def fold(i, carry, b=b, u=u, w=w, wd=wd):
                r = pl.ds(pl.multiple_of((i % 8) * 16, 16), 16)
                w[i // 8, r] = (
                    b[i // 8, r, cols(x, wd)].astype(F32)
                    + u[1, i // 8, r].astype(F32)
                    + u[2, i // 8, r].astype(F32)
                    + u[3, i // 8, r].astype(F32)
                ).astype(BF16)
                return carry

            lax.fori_loop(0, 32, fold, 0)
        else:
            sum_rows(w, [b.at[z], u.at[1], u.at[2], u.at[3]])
        for k in (2, 1, 3):
            if n == 1:
                src, peer = w.at[around(z, k)], zp[k - 1]
            else:
                src, peer = w.at[:, cols(around(x, k), wd)], xp[k - 1]
            sent2.append(remote(src, v.at[k], s_2.at[n, k], r_2.at[n, k], peer))
    lasts = tuple(zip((w_q, w_o, w_c), (v_q, v_o, v_c), (f_q, f_o, f_c), (qo, oo, co), widths))
    for n, (w, v, f, out, wd) in enumerate(lasts):
        for copy in sent2[3 * n : 3 * n + 3]:
            copy.wait_recv()
        own = w.at[z] if n == 1 else w.at[:, cols(x, wd)]
        sum_rows(f, [own, v.at[1], v.at[2], v.at[3]])

        @pl.when(x != y)
        def _(f=f, out=out, n=n):
            remote(f, out, s_t.at[n], r_t.at[n], partner)

        @pl.when(x == y)
        def _(f=f, out=out, n=n):
            pltpu.make_async_copy(f, out, r_t.at[n]).start()

    for n, (w, v, f, out, wd) in enumerate(lasts):
        pltpu.make_async_copy(f, out, r_t.at[n]).wait()
    for copy in small:
        copy.wait_recv()
    for copy in swaps + small + sent + sent2:
        copy.wait_send()

    @pl.when(x != y)
    def _():
        for n, (w, v, f, out, wd) in enumerate(lasts):
            pltpu.make_async_copy(f, out, s_t.at[n]).wait()


def reduce_weights(qp, op, cp, rs):
    wide, slim = (4, 128, 2048), (4, 128, 1024)
    return pl.pallas_call(
        reduce_kernel,
        out_shape=(
            jax.ShapeDtypeStruct((128, 512), BF16),
            jax.ShapeDtypeStruct((128, 512), BF16),
            jax.ShapeDtypeStruct((128, 256), BF16),
            jax.ShapeDtypeStruct((4, 8, 128), F32),
        ),
        in_specs=[VM] * 4,
        out_specs=(VM,) * 4,
        scratch_shapes=[
            pltpu.VMEM(wide, BF16), pltpu.VMEM(wide, BF16), pltpu.VMEM(slim, BF16),
            pltpu.VMEM(wide, BF16), pltpu.VMEM((4, 4, 128, 512), BF16), pltpu.VMEM(slim, BF16),
            pltpu.VMEM((128, 2048), BF16), pltpu.VMEM((4, 128, 512), BF16),
            pltpu.VMEM((128, 1024), BF16),
            pltpu.VMEM((4, 128, 512), BF16), pltpu.VMEM((4, 128, 512), BF16),
            pltpu.VMEM((4, 128, 256), BF16),
            pltpu.VMEM((128, 512), BF16), pltpu.VMEM((128, 512), BF16),
            pltpu.VMEM((128, 256), BF16),
            DMA((4,)), DMA((4,)),
            DMA((3,)), DMA((3,)),
            DMA((3, 4)), DMA((3, 4)),
            DMA((3, 4)), DMA((3, 4)),
            DMA((3,)), DMA((3,)),
        ],
        compiler_params=pltpu.CompilerParams(
            collective_id=3, has_side_effects=True, vmem_limit_bytes=56 << 20
        ),
        name="reduce_weights",
    )(qp, op, cp, rs)


def dot_nn(a, b):
    return jnp.dot(a, b, preferred_element_type=F32)


def dot_nt(a, b):
    return lax.dot_general(a, b, (((1,), (1,)), ((), ())), preferred_element_type=F32)


def dot_tn(a, b):
    return lax.dot_general(a, b, (((0,), (0,)), ((), ())), preferred_element_type=F32)


def attention_kernel(q_ref, g_ref, k_ref, v_ref, att_ref, qag_ref, kag_ref, vag_ref):
    scale = HSZ ** (-0.5)
    for h in range(q_ref.shape[1] // HSZ):
        lanes = slice(h * HSZ, (h + 1) * HSZ)
        for s in range(2):
            rows, keys = slice(s * SPAN, (s + 1) * SPAN), slice(s * 2 * NL, (s + 1) * 2 * NL)
            q, g = q_ref[rows, lanes], g_ref[rows, lanes]
            k, v = k_ref[keys, lanes], v_ref[keys, lanes]
            score = dot_nt(q, k) * scale
            e = jnp.exp(score - jnp.max(score, axis=-1, keepdims=True))
            full = e / jnp.sum(e, axis=-1, keepdims=True)
            weights = full.astype(BF16)
            att_ref[rows, lanes] = dot_nn(weights, v).astype(BF16)
            pg = dot_nt(g, v)
            sg = (full * (pg - jnp.sum(full * pg, axis=-1, keepdims=True)) * scale).astype(BF16)
            qag_ref[rows, lanes] = dot_nn(sg, k).astype(BF16)
            kag_ref[keys, lanes] = dot_tn(sg, q).astype(BF16)
            vag_ref[keys, lanes] = dot_tn(weights, g).astype(BF16)


def attention(q, g, k, v):
    few = pl.BlockSpec((128, 256), lambda h: (0, h))
    many = pl.BlockSpec((512, 256), lambda h: (0, h))
    return pl.pallas_call(
        attention_kernel,
        grid=(8,),
        out_shape=(
            jax.ShapeDtypeStruct((128, 2048), BF16),
            jax.ShapeDtypeStruct((128, 2048), BF16),
            jax.ShapeDtypeStruct((512, 2048), BF16),
            jax.ShapeDtypeStruct((512, 2048), BF16),
        ),
        in_specs=[few, few, many, many],
        out_specs=(few, few, many, many),
        name="attention",
    )(q, g, k, v)


def wide_columns(n):
    r = lax.broadcasted_iota(jnp.int32, (28 * n, 32 * n), 0)
    s = lax.broadcasted_iota(jnp.int32, (28 * n, 32 * n), 1)
    return ((r // 28 == s // 32) & (r % 28 == s % 32)).astype(BF16)


def lines(v):
    return jnp.pad(v.reshape(4, 128), ((0, 4), (0, 0)))


def shards(
    hidden, norm_gain, w_query, w_key, w_value, w_out, w_cond, enc_gain, store, neighbour_ids,
    out_grad,
):
    y = lax.axis_index("enc")
    xf = hidden.astype(F32)
    gain = lax.dynamic_slice_in_dim(norm_gain, y * 1024, 1024)
    sq = lines(jnp.sum(xf * xf, axis=-1))
    summary = jnp.mean(xf.reshape(8, SPAN, 1024), axis=1).astype(BF16)
    ids = jnp.pad(neighbour_ids.reshape(1, 4), ((0, 7), (0, 124)))
    wc = dot_nn(w_cond, wide_columns(8)).astype(BF16)
    wk = jnp.pad(w_key, ((0, 4), (0, 0)))
    wv = jnp.pad(w_value, ((0, 4), (0, 0)))
    raw, sq_all, q, ag, cond, normed_t, out_grad_t, gq, go, gc, gk, gv = forward(
        ids, sq, gain.reshape(1, 1024), hidden, out_grad, summary, store,
        w_query, w_out.T, wc, wk, wv,
    )
    gq, go, gc = gq.reshape(1024, 2048), go.reshape(1024, 2048), gc.reshape(1024, 1024)
    gk, gv = gk.reshape(PE, 2048), gv.reshape(PE, 2048)
    rstd = lax.rsqrt(jnp.sum(sq_all, axis=0)[:4].reshape(512, 1) / 4096 + EPS)

    egain = jnp.pad(enc_gain.reshape(32, 28), ((0, 0), (0, 4))).reshape(PE)
    rawp = dot_nn(raw.reshape(512, DE), wide_columns(32))
    cond_rows = cond.astype(BF16).astype(F32)
    enc_in = (rawp.reshape(2, 256, PE) + cond_rows[:, None, :]).reshape(512, PE)
    enc_rstd = lax.rsqrt(jnp.sum(enc_in * enc_in, axis=-1, keepdims=True) / DE + EPS)
    encoded = (enc_in * enc_rstd * egain).astype(BF16)
    keys = dot_nn(encoded, gk).astype(BF16)
    values = dot_nn(encoded, gv).astype(BF16)
    att, qag, kag, vag = attention(q, ag, keys, values)
    kp = dot_tn(encoded, kag).astype(BF16).reshape(4, 4, 2, 32, 2048)
    vp = dot_tn(encoded, vag).astype(BF16).reshape(4, 4, 2, 32, 2048)
    eg = (dot_nt(kag, gk) + dot_nt(vag, gv)).astype(BF16).astype(F32)
    ey = egain * eg
    emean = jnp.sum(enc_in * ey, axis=-1, keepdims=True) / DE
    slot = jnp.sum(
        (enc_rstd * ey - enc_in * enc_rstd**3 * emean).reshape(2, 256, PE), axis=1
    )
    cd = slot.astype(BF16).astype(F32)
    att_all, qag_all, cd_all, kg, vg = ring_gather(att, qag, cd, kp, vp)
    att_all, qag_all = att_all.reshape(512, 2048), qag_all.reshape(512, 2048)
    cd_all = cd_all.reshape(8, PE).astype(BF16)

    layer_out = (xf + dot_nt(att_all, go)).astype(BF16)
    op = dot_nn(out_grad_t, att_all).astype(BF16).reshape(4, 2, 128, 2048)
    gp = dot_nn(normed_t, qag_all).astype(BF16).reshape(4, 2, 128, 2048)
    hp = dot_tn(summary, cd_all).astype(BF16).reshape(4, 2, 128, 1024)
    scaled = dot_nt(qag_all, gq) * gain
    rs = lines(jnp.sum(xf * scaled, axis=-1))
    summary_grad = dot_nt(cd_all, gc)
    qo, oo, co, rs_all = reduce_weights(gp, op, hp, rs)

    row_mean = jnp.sum(rs_all, axis=0)[:4].reshape(512, 1) / 4096
    hidden_grad = (
        out_grad.astype(F32)
        + (rstd * scaled - xf * rstd**3 * row_mean)
        + jnp.repeat(summary_grad / SPAN, SPAN, axis=0)
    )
    cond_grad = co.astype(F32).reshape(128, 8, 32)[:, :, :28].reshape(128, 224)
    return (
        layer_out,
        hidden_grad,
        qo.astype(F32),
        kg[:28],
        vg[:28],
        oo.T.astype(F32),
        cond_grad,
    )


def solution(mesh):
    placed = (
        P("dp", "enc"), P(), P("dp", "enc"), P("dp", "enc"), P("dp", "enc"), P("enc", "dp"),
        P("dp", "enc"), P(), P(("dp", "enc"), None, None), P(("dp", "enc")), P("dp", "enc"),
    )
    return jax.shard_map(
        shards,
        mesh=mesh,
        in_specs=placed,
        out_specs=(
            P("dp", "enc"), P("dp", "enc"), P("dp", "enc"), P("dp", "enc"), P("dp", "enc"),
            P("enc", "dp"), P("dp", "enc"),
        ),
        check_vma=False,
    )
```

```python
import functools

import jax
import jax.numpy as jnp
from jax import lax
from jax.experimental import pallas as pl
from jax.experimental.pallas import tpu as pltpu
from jax.sharding import PartitionSpec as P

MESH = pl.DeviceIdType.MESH
F32 = jnp.float32
BF16 = jnp.bfloat16
HSZ = 128
SPAN = 64
NL = 128
DE = 896
PE = 1024
EPS = 1e-05
ANY = pl.BlockSpec(memory_space=pl.ANY)
VM = pl.BlockSpec(memory_space=pltpu.VMEM)
DMA = pltpu.SemaphoreType.DMA


def place():
    d = lax.axis_index("dp")
    return d // 8, (d // 2) % 4, d % 2, lax.axis_index("enc")


def at(x, z, c, y):
    return ((x * 4 + z) * 2 + c, y)


def around(v, k):
    return (v + k) % 4


def remote(src, dst, send, recv, device):
    copy = pltpu.make_async_remote_copy(
        src, dst, send, recv, device_id=device, device_id_type=MESH
    )
    copy.start()
    return copy


def meet(peers, partner=None, has_partner=None):
    barrier = pltpu.get_barrier_semaphore()
    for peer in peers:
        pl.semaphore_signal(barrier, inc=1, device_id=peer, device_id_type=MESH)
    if partner is not None:

        @pl.when(has_partner)
        def _():
            pl.semaphore_signal(barrier, inc=1, device_id=partner, device_id_type=MESH)

        pl.semaphore_wait(barrier, jnp.where(has_partner, len(peers) + 1, len(peers)))
    else:
        pl.semaphore_wait(barrier, len(peers))


def sum_rows(out, terms, step=16):
    rows = out.shape[0]

    def body(i, carry):
        at_row = pl.ds(pl.multiple_of(i * step, step), step)
        total = terms[0][at_row].astype(F32)
        for t in terms[1:]:
            total = total + t[at_row].astype(F32)
        out[at_row] = total.astype(out.dtype)
        return carry

    lax.fori_loop(0, rows // step, body, 0)


def cols(i, n):
    return pl.ds(pl.multiple_of(i * n, n), n)


def pick_rows(ids_s, r):
    every = [ids_s[r, 0, k] for k in range(4)]
    owner = [(v // 8) % 4 for v in every]
    row = [v % 8 for v in every]
    rank = []
    for k in range(4):
        n = jnp.int32(0)
        for j in range(k):
            n = n + jnp.where(owner[j] == owner[k], 1, 0)
        rank.append(n)
    return owner, row, rank


class Plane:
    def __init__(self, put, line, cut, whole, axes, sems):
        self.put, self.line, self.cut, self.whole = put, line, cut, whole
        self.x, self.z, self.xp, self.zp, self.sib = axes
        self.s, self.r = sems
        self.one, self.two, self.on, self.last = [[], []], [[], []], [[], []], None

    def first(self):
        for h in range(2):
            src, dst, keep = self.put(h)
            for k in (2, 1, 3):
                peer = (self.zp if h else self.xp)[k - 1]
                self.one[h].append(remote(src, dst, self.s.at[h, k], self.r.at[h, k], peer))
            if keep is not None:
                copy = pltpu.make_async_copy(src, dst, self.s.at[h, 0])
                copy.start()
                copy.wait()

    def second(self):
        for h in range(2):
            for copy in self.one[h]:
                copy.wait_recv()
            block = self.line(h, self.x if h else self.z)
            for k in (1, 3):
                peer = (self.xp if h else self.zp)[k - 1]
                self.two[h].append(
                    remote(block, block, self.s.at[h, 3 + k], self.r.at[h, 3 + k], peer)
                )

    def relay(self):
        for h in range(2):
            place = self.x if h else self.z
            for j, k in ((0, 1), (1, 3)):
                self.two[h][j].wait_recv()
                block = self.cut(h, around(place, 4 - k), j)
                peer = (self.xp if h else self.zp)[k - 1]
                self.on[h].append(
                    remote(block, block, self.s.at[h, 7 + k], self.r.at[h, 7 + k], peer)
                )

    def swap(self):
        for copy in self.on[0] + self.on[1]:
            copy.wait_recv()
        self.last = remote(self.whole, self.whole, self.s.at[0, 5], self.r.at[0, 5], self.sib)

    def sent(self):
        every = self.one[0] + self.one[1] + self.two[0] + self.two[1]
        for copy in every + self.on[0] + self.on[1] + [self.last]:
            copy.wait_send()


def forward_kernel(
    ids, sq, gain, xs, og, sm, store, wq, wo, wc, wk, wv,
    raw, sq_all, q, a, cond, nt, ogt, hq, ho, hc, gk, gv,
    ids_all, ids_s, out_rows, in_rows, tq, to, tc, yk, yv, gq, go, gc,
    normed, qp, ap, cp, rq, ra, rc,
    s_small, r_small, s_row, r_row, s_t, r_t, s_p, r_p, s_w, r_w, s_y, r_y, s_loc, s_out,
):
    x, z, c, y = place()
    yp = [at(x, z, c, around(y, k)) for k in (1, 2, 3)]
    xp = [at(around(x, k), z, c, y) for k in (1, 2, 3)]
    zp = [at(x, around(z, k), c, y) for k in (1, 2, 3)]
    sib = at(x, z, 1 - c, y)
    partner = at(y, z, c, x)
    axes = (x, z, xp, zp, sib)
    meet(yp + xp + zp + [sib], partner, x != y)

    moves = ((wq, tq), (wo, to), (wc, tc))

    @pl.when(x != y)
    def _():
        for n, (w, t) in enumerate(moves):
            remote(w, t, s_t.at[n], r_t.at[n], partner)

    @pl.when(x == y)
    def _():
        for n, (w, t) in enumerate(moves):
            pltpu.make_async_copy(w, t, r_t.at[n]).start()

    small = []
    for k in (1, 2, 3):
        small.append(remote(ids, ids_all.at[y], s_small.at[0, k], r_small.at[0, k], yp[k - 1]))
    for k in (1, 2, 3):
        small.append(remote(sq, sq_all.at[y], s_small.at[1, k], r_small.at[1, k], yp[k - 1]))
    across = []
    for n, (w, t) in enumerate(((wk, yk), (wv, yv))):
        for k in (2, 1, 3):
            across.append(
                remote(w, t.at[:, cols(y, 512)], s_w.at[n, k], r_w.at[n, k], yp[k - 1])
            )
        t[:, cols(y, 512)] = w[...]
    ids_all[y] = ids[...]
    sq_all[y] = sq[...]
    for copy in small[:3]:
        copy.wait_recv()
    to_s = pltpu.make_async_copy(ids_all, ids_s, s_loc.at[0])
    to_s.start()
    to_s.wait()

    row_copies = []
    for k in (2, 1, 3, 0):
        owner, row, rank = pick_rows(ids_s, around(y, k))
        for n in range(2):
            pick = jnp.int32(0)
            for j in range(4):
                pick = pick + jnp.where((owner[j] == y) & (rank[j] == n), row[j], 0)
            if k:
                out_rows[k, n] = store[pick]
            else:
                in_rows[y, n] = store[pick]
        if k:
            row_copies.append(
                remote(out_rows.at[k], in_rows.at[y], s_row.at[k], r_row.at[k], yp[k - 1])
            )

    def weight(n, t, g, w):
        def put(h):
            rows = pl.ds(64 * h, 64)
            return t.at[rows], g.at[z, c, rows, cols(x, w)], True

        def line(h, i):
            if h:
                return g.at[:, c, pl.ds(64, 64), cols(i, w)]
            return g.at[i, c, pl.ds(0, 64)]

        def cut(h, i, j):
            if h:
                return g.at[:, c, pl.ds(64 + 32 * j, 32), cols(i, w)]
            return g.at[i, c, pl.ds(32 * j, 32)]

        return Plane(put, line, cut, g.at[:, c], axes, (s_p.at[n], r_p.at[n]))

    pq, po, pc = weight(0, tq, gq, 512), weight(1, to, go, 512), weight(2, tc, gc, 256)

    def kv_put(h):
        return (yv, gv.at[x, z, c], True) if h else (yk, gk.at[x, z, c], True)

    def kv_line(h, i):
        return gv.at[i, :, c] if h else gk.at[:, i, c]

    def kv_cut(h, i, j):
        if h:
            return gv.at[i, pl.ds(2 * j, 2), c]
        return gk.at[pl.ds(2 * j, 2), i, c]

    def arrived(n, w, t):
        pltpu.make_async_copy(w, t, r_t.at[n]).wait()

    arrived(0, wq, tq)
    pq.first()
    arrived(1, wo, to)
    po.first()
    pq.second()
    arrived(2, wc, tc)
    pc.first()
    for copy in small[3:]:
        copy.wait_recv()
    total = sq_all[0] + sq_all[1] + sq_all[2] + sq_all[3]
    rstd = lax.rsqrt(total / 4096 + EPS).T
    for j in range(4):
        rows = slice(128 * j, 128 * (j + 1))
        normed[rows] = (xs[rows].astype(F32) * rstd[:, j : j + 1] * gain[...]).astype(BF16)
    po.second()
    pq.relay()
    for copy in across:
        copy.wait_recv()
    pk = KeyPlane(kv_put, kv_line, kv_cut, (gk.at[:, :, c], gv.at[:, :, c]), axes, (s_p.at[3], r_p.at[3]))
    pk.first()
    pc.second()
    pq.swap()
    po.relay()

    parts, outs = [], []

    def partial(n, act, g, h, p, r, plane):
        plane.last.wait_recv()
        keep = pltpu.make_async_copy(g, h, s_out.at[n])
        keep.start()
        outs.append(keep)

        def tile(i, carry):
            lanes = cols(i, 256)
            w = g[:, :, :, lanes].reshape(1024, 256)
            p[:, :, lanes] = dot_nn(act[...], w).astype(BF16).reshape(4, 128, 256)
            return carry

        lax.fori_loop(0, 8, tile, 0)
        for k in (2, 1, 3):
            parts.append(
                remote(p.at[around(y, k)], r.at[k], s_y.at[n, k], r_y.at[n, k], yp[k - 1])
            )

    partial(0, normed, gq, hq, qp, rq, pq)
    pk.second()
    po.swap()
    pc.relay()
    partial(1, og, go, ho, ap, ra, po)
    pk.relay()
    pc.swap()
    for j in range(4):
        rows = slice(128 * j, 128 * (j + 1))
        nt[:, rows] = normed[rows].T
        ogt[:, rows] = og[rows].T
    pc.last.wait_recv()
    keep = pltpu.make_async_copy(gc, hc, s_out.at[2])
    keep.start()
    outs.append(keep)
    for i in range(4):
        lanes = slice(256 * i, 256 * (i + 1))
        w = gc[:, :, :, lanes].reshape(1024, 256)
        cp[:, lanes] = dot_nn(sm[...], w)
    for j in range(4):
        rc[j + 4] = cp[2 * j : 2 * j + 2]
    for k in (2, 1, 3):
        parts.append(
            remote(rc.at[4 + around(y, k)], rc.at[k], s_y.at[2, k], r_y.at[2, k], yp[k - 1])
        )
    for copy in row_copies:
        copy.wait_recv()
    owner, row, rank = pick_rows(ids_s, y)
    for k in range(4):
        raw[k] = in_rows[owner[k], jnp.minimum(rank[k], 1)]
    pk.swap()
    for copy in parts[:3]:
        copy.wait_recv()
    sum_rows(q, [qp.at[y], rq.at[1], rq.at[2], rq.at[3]])
    for copy in parts[3:]:
        copy.wait_recv()
    sum_rows(a, [ap.at[y], ra.at[1], ra.at[2], ra.at[3]])
    cond[...] = rc[4 + y] + rc[1] + rc[2] + rc[3]
    for copy in pk.last:
        copy.wait_recv()
    for copy in outs:
        copy.wait()
    for copy in small + across + row_copies + parts:
        copy.wait_send()
    for plane in (pq, po, pc, pk):
        plane.sent()

    @pl.when(x != y)
    def _():
        for n, (w, t) in enumerate(moves):
            pltpu.make_async_copy(w, t, s_t.at[n]).wait()


class KeyPlane(Plane):
    def swap(self):
        for copy in self.on[0] + self.on[1]:
            copy.wait_recv()
        self.last = [
            remote(ref, ref, self.s.at[n, 5], self.r.at[n, 5], self.sib)
            for n, ref in enumerate(self.whole)
        ]

    def sent(self):
        every = self.one[0] + self.one[1] + self.two[0] + self.two[1]
        for copy in every + self.on[0] + self.on[1] + self.last:
            copy.wait_send()


def forward(ids, sq, gain, xs, og, sm, store, wq, wo, wc, wk, wv):
    wide, slim, keys = (4, 2, 128, 2048), (4, 2, 128, 1024), (4, 4, 2, 32, 2048)
    shape = jax.ShapeDtypeStruct
    return pl.pallas_call(
        forward_kernel,
        out_shape=(
            shape((4, NL, DE), BF16),
            shape((4, 8, 128), F32),
            shape((128, 2048), BF16),
            shape((128, 2048), BF16),
            shape((2, 1024), F32),
            shape((1024, 512), BF16),
            shape((1024, 512), BF16),
            shape(wide, BF16),
            shape(wide, BF16),
            shape(slim, BF16),
            shape(keys, BF16),
            shape(keys, BF16),
        ),
        in_specs=[VM] * 12,
        out_specs=(VM,) * 7 + (ANY,) * 5,
        scratch_shapes=[
            pltpu.VMEM((4, 8, 128), jnp.int32),
            pltpu.SMEM((4, 8, 128), jnp.int32),
            pltpu.VMEM((4, 2, NL, DE), BF16),
            pltpu.VMEM((4, 2, NL, DE), BF16),
            pltpu.VMEM((128, 512), BF16),
            pltpu.VMEM((128, 512), BF16),
            pltpu.VMEM((128, 256), BF16),
            pltpu.VMEM((32, 2048), BF16),
            pltpu.VMEM((32, 2048), BF16),
            pltpu.VMEM(wide, BF16),
            pltpu.VMEM(wide, BF16),
            pltpu.VMEM(slim, BF16),
            pltpu.VMEM((512, 1024), BF16),
            pltpu.VMEM((4, 128, 2048), BF16),
            pltpu.VMEM((4, 128, 2048), BF16),
            pltpu.VMEM((8, 1024), F32),
            pltpu.VMEM((4, 128, 2048), BF16),
            pltpu.VMEM((4, 128, 2048), BF16),
            pltpu.VMEM((8, 2, 1024), F32),
            DMA((2, 4)), DMA((2, 4)),
            DMA((4,)), DMA((4,)),
            DMA((3,)), DMA((3,)),
            DMA((4, 2, 11)), DMA((4, 2, 11)),
            DMA((2, 4)), DMA((2, 4)),
            DMA((3, 4)), DMA((3, 4)),
            DMA((1,)),
            DMA((3,)),
        ],
        compiler_params=pltpu.CompilerParams(
            collective_id=0, has_side_effects=True, vmem_limit_bytes=52 << 20
        ),
        name="forward",
    )(ids, sq, gain, xs, og, sm, store, wq, wo, wc, wk, wv)


def dot_nn(a, b):
    return jnp.dot(a, b, preferred_element_type=F32)


def dot_nt(a, b):
    return lax.dot_general(a, b, (((1,), (1,)), ((), ())), preferred_element_type=F32)


def dot_tn(a, b):
    return lax.dot_general(a, b, (((0,), (0,)), ((), ())), preferred_element_type=F32)


class Halves:
    def __init__(self, p, bufs, out, w, spots, sems):
        self.p, self.out, self.w = p, out, w
        self.b, self.ua, self.ub, self.wa, self.wb, self.va, self.vb, self.f = bufs
        self.x, self.z, self.c, self.y, self.xp, self.zp, self.sib = spots
        self.s, self.r = sems
        self.one, self.two, self.swapped = [[], []], [[], []], None

    def swap(self):
        src = self.p.at[:, pl.ds(2 * (1 - self.c), 2)]
        self.swapped = remote(src, self.b, self.s.at[0], self.r.at[0], self.sib)

    def first(self):
        self.swapped.wait_recv()
        p, b, c = self.p, self.b, self.c

        def fold(i, carry):
            j, h, k = i // 4, (i // 2) % 2, i % 2
            b[j, h, k] = (p[j, 2 * c + h, k].astype(F32) + b[j, h, k].astype(F32)).astype(BF16)
            return carry

        lax.fori_loop(0, 16, fold, 0)
        for k in (2, 1, 3):
            self.one[0].append(
                remote(b.at[around(self.z, k), 0], self.ua.at[k - 1], self.s.at[k], self.r.at[k], self.zp[k - 1])
            )
            lanes = cols(around(self.x, k), self.w)
            self.one[1].append(
                remote(b.at[:, 1, :, :, lanes], self.ub.at[k - 1], self.s.at[3 + k], self.r.at[3 + k], self.xp[k - 1])
            )

    def second(self):
        b, ua, ub, wa, wb = self.b, self.ua, self.ub, self.wa, self.wb
        for copy in self.one[0]:
            copy.wait_recv()
        for i in range(2):
            wa[i] = (
                b[self.z, 0, i].astype(F32) + ua[0, i].astype(F32)
                + ua[1, i].astype(F32) + ua[2, i].astype(F32)
            ).astype(BF16)
        for k in (2, 1, 3):
            lanes = cols(around(self.x, k), self.w)
            self.two[0].append(
                remote(wa.at[:, :, lanes], self.va.at[k - 1], self.s.at[6 + k], self.r.at[6 + k], self.xp[k - 1])
            )
        for copy in self.one[1]:
            copy.wait_recv()

        def fold(i, carry):
            j, k = i // 2, i % 2
            wb[j, k] = (
                b[j, 1, k, :, cols(self.x, self.w)].astype(F32) + ub[0, j, k].astype(F32)
                + ub[1, j, k].astype(F32) + ub[2, j, k].astype(F32)
            ).astype(BF16)
            return carry

        lax.fori_loop(0, 8, fold, 0)
        for k in (2, 1, 3):
            self.two[1].append(
                remote(wb.at[around(self.z, k)], self.vb.at[k - 1], self.s.at[9 + k], self.r.at[9 + k], self.zp[k - 1])
            )

    def third(self):
        x, y, z, f, va, vb = self.x, self.y, self.z, self.f, self.va, self.vb
        for copy in self.two[0] + self.two[1]:
            copy.wait_recv()
        for i in range(2):
            f[0, i] = (
                self.wa[i, :, cols(x, self.w)].astype(F32) + va[0, i].astype(F32)
                + va[1, i].astype(F32) + va[2, i].astype(F32)
            ).astype(BF16)
            f[1, i] = (
                self.wb[z, i].astype(F32) + vb[0, i].astype(F32)
                + vb[1, i].astype(F32) + vb[2, i].astype(F32)
            ).astype(BF16)

        @pl.when(x != y)
        def _():
            remote(f, self.out, self.s.at[13], self.r.at[13], at(y, z, self.c, x))

        @pl.when(x == y)
        def _():
            pltpu.make_async_copy(f, self.out, self.r.at[13]).start()

    def end(self):
        pltpu.make_async_copy(self.f, self.out, self.r.at[13]).wait()
        for copy in self.one[0] + self.one[1] + self.two[0] + self.two[1]:
            copy.wait_send()

        @pl.when(self.x != self.y)
        def _():
            pltpu.make_async_copy(self.f, self.out, self.s.at[13]).wait()


def backward_kernel(
    att, qag, kag, vag, enc, ein, egain, xs, og, gain, nt, ogt, sm, sq, gc, gq, go, gk, gv,
    layer, hidden, qo, oo, co, ko, vo,
    tile, et, att_all, qag_all, cd_all, rs_all, p1, p2, p3, line_up, erstd, emean, rsum, sgrad, slot,
    b_k, b_v, u_k, u_v, w_k, w_v, x_k, x_v, f_k, f_v,
    bq0, bq1, bq2, bq3, bq4, bq5, bq6, bq7,
    bo0, bo1, bo2, bo3, bo4, bo5, bo6, bo7,
    bc0, bc1, bc2, bc3, bc4, bc5, bc6, bc7,
    s_y, r_y, s_d, r_d, s_c, r_c, s_1, r_1, s_2, r_2, s_3, r_3, s_h, r_h, s_tile,
):
    x, z, c, y = place()
    yp = [at(x, z, c, around(y, k)) for k in (1, 2, 3)]
    xp = [at(around(x, k), z, c, y) for k in (1, 2, 3)]
    zp = [at(x, around(z, k), c, y) for k in (1, 2, 3)]
    sib = at(x, z, 1 - c, y)
    meet(yp + xp + zp + [sib], at(y, z, c, x), x != y)
    spots = (x, z, c, y, xp, zp, sib)
    rq = Halves(p1, (bq0, bq1, bq2, bq3, bq4, bq5, bq6, bq7), qo, 512, spots, (s_h.at[0], r_h.at[0]))
    ro = Halves(p2, (bo0, bo1, bo2, bo3, bo4, bo5, bo6, bo7), oo, 512, spots, (s_h.at[1], r_h.at[1]))
    rc = Halves(p3, (bc0, bc1, bc2, bc3, bc4, bc5, bc6, bc7), co, 256, spots, (s_h.at[2], r_h.at[2]))

    ring = []
    for n, (src, dst) in enumerate(((att, att_all), (qag, qag_all))):
        for j, k in ((0, 1), (1, 3)):
            ring.append(remote(src, dst.at[y], s_y.at[n, j], r_y.at[n, j], yp[k - 1]))
    et[...] = enc[...].T

    def product(left, right, p, width=256):
        def step(i, carry):
            lanes = cols(i, width)
            r = right[..., lanes].reshape(left.shape[1], width)
            p[..., lanes] = dot_nn(left[...], r).astype(BF16).reshape(4, 4, 2, 32, width)
            return carry

        lax.fori_loop(0, p.shape[-1] // width, step, 0)

    swaps = []
    for n, (act, p, b) in enumerate(((kag, p1, b_k), (vag, p2, b_v))):
        product(et, act, p)
        swaps.append(remote(p.at[:, :, 1 - c], b, s_c.at[n], r_c.at[n], sib))
    att_all[y] = att[...]
    qag_all[y] = qag[...]

    passed = []

    def relay(n, dst):
        for j, k in ((0, 1), (1, 3)):
            ring[2 * n + j].wait_recv()
            block = dst.at[around(y, 4 - k), pl.ds(64 * j, 64)]
            passed.append(remote(block, block, s_y.at[n, 2 + j], r_y.at[n, 2 + j], yp[k - 1]))

    sent = []
    for n, (p, b, u) in enumerate(((p1, b_k, u_k), (p2, b_v, u_v))):
        swaps[n].wait_recv()

        def fold(i, carry, p=p, b=b):
            b[i // 4, i % 4] = (
                p[i // 4, i % 4, c].astype(F32) + b[i // 4, i % 4].astype(F32)
            ).astype(BF16)
            return carry

        lax.fori_loop(0, 16, fold, 0)
        for k in (2, 1, 3):
            if n:
                src, peer = b.at[around(x, k)], xp[k - 1]
            else:
                src, peer = b.at[:, around(z, k)], zp[k - 1]
            sent.append(remote(src, u.at[k - 1], s_1.at[n, k], r_1.at[n, k], peer))
    for copy in swaps:
        copy.wait_send()
    relay(0, att_all)

    def fetch(h, i, j):
        return pltpu.make_async_copy(h.at[i], tile.at[j], s_tile.at[j])

    ee = ein[...]
    erstd[...] = lax.rsqrt(jnp.sum(ee * ee, axis=-1, keepdims=True) / DE + EPS)
    emean[...] = jnp.zeros_like(emean)
    fetch(gk, 0, 0).start()
    fetch(gv, 0, 1).start()

    def encoder(i, carry):
        lanes = cols(i, 256)
        fetch(gk, i, 0).wait()
        part = dot_nt(kag[...], tile[0])

        @pl.when(i < 3)
        def _():
            fetch(gk, i + 1, 0).start()

        fetch(gv, i, 1).wait()
        part = part + dot_nt(vag[...], tile[1])

        @pl.when(i < 3)
        def _():
            fetch(gv, i + 1, 1).start()

        ey = part.astype(BF16).astype(F32) * egain[:, lanes]
        emean[...] += jnp.sum(ein[:, lanes] * ey, axis=-1, keepdims=True)
        ry = ey * erstd[...]
        for s in range(2):
            slot[s : s + 1, lanes] = jnp.sum(ry[256 * s : 256 * s + 256], axis=0, keepdims=True)
        return carry

    lax.fori_loop(0, 4, encoder, 0)
    relay(1, qag_all)
    for s in range(2):
        rows = slice(256 * s, 256 * s + 256)
        weight = erstd[rows] ** 3 * (emean[rows] / DE)
        row = slot[s : s + 1] - jnp.sum(ein[rows] * weight, axis=0, keepdims=True)
        slot[s : s + 1] = row.astype(BF16).astype(F32)
    cd_all[y] = slot[...]
    small = [remote(slot, cd_all.at[y], s_d.at[0, k], r_d.at[0, k], yp[k - 1]) for k in (1, 2, 3)]

    for copy in passed[:2]:
        copy.wait_recv()
    product(ogt, att_all, p2)
    ro.swap()

    def streamed(h, act, use):
        fetch(h, 0, 0).start()

        def step(i, carry):
            fetch(h, i, i % 2).wait()

            @pl.when(i < 3)
            def _():
                fetch(h, i + 1, (i + 1) % 2).start()

            use(cols(i, 256), dot_nt(act[...].reshape(512, 2048), tile[i % 2]))
            return carry

        lax.fori_loop(0, 4, step, 0)

    sent2 = []
    for n, (b, u, w, v) in enumerate(((b_k, u_k, w_k, x_k), (b_v, u_v, w_v, x_v))):
        for copy in sent[3 * n : 3 * n + 3]:
            copy.wait_recv()

        def fold(i, carry, b=b, u=u, w=w, n=n):
            own = b[x, i] if n else b[i, z]
            w[i] = (
                own.astype(F32) + u[0, i].astype(F32) + u[1, i].astype(F32) + u[2, i].astype(F32)
            ).astype(BF16)
            return carry

        lax.fori_loop(0, 4, fold, 0)
        for k in (2, 1, 3):
            if n:
                src, peer = w.at[around(z, k)], zp[k - 1]
            else:
                src, peer = w.at[around(x, k)], xp[k - 1]
            sent2.append(remote(src, v.at[k - 1], s_2.at[n, k], r_2.at[n, k], peer))
    ro.first()
    for copy in passed[2:]:
        copy.wait_recv()
    product(nt, qag_all, p1)
    rq.swap()

    def add_out(lanes, value):
        layer[:, lanes] = (xs[:, lanes].astype(F32) + value).astype(BF16)

    streamed(go, att_all, add_out)
    rq.first()
    sent3 = []
    for n, (w, v, f) in enumerate(((w_k, x_k, f_k), (w_v, x_v, f_v))):
        for copy in sent2[3 * n : 3 * n + 3]:
            copy.wait_recv()
        own = w[z] if n else w[x]
        f[0] = (
            own.astype(F32) + v[0].astype(F32) + v[1].astype(F32) + v[2].astype(F32)
        ).astype(BF16)
        for k in (2, 1, 3):
            src, dst = f.at[0, :, cols(around(y, k), 512)], f.at[k, :, pl.ds(0, 512)]
            sent3.append(remote(src, dst, s_3.at[n, k], r_3.at[n, k], yp[k - 1]))
    for copy in small:
        copy.wait_recv()
    cd = cd_all[...].reshape(8, 1024).astype(BF16)
    for i in range(4):
        lanes = slice(256 * i, 256 * i + 256)
        p3[..., lanes] = dot_tn(sm[...], cd[:, lanes]).astype(BF16).reshape(4, 4, 2, 32, 256)
    rc.swap()
    for i in range(4):
        sgrad[:, 256 * i : 256 * i + 256] = dot_nt(cd, gc[i].reshape(256, 1024)) / SPAN
    rsum[...] = jnp.zeros_like(rsum)

    def add_scaled(lanes, value):
        scaled = value * gain[:, lanes]
        hidden[:, lanes] = scaled
        rsum[...] += jnp.sum(xs[:, lanes].astype(F32) * scaled, axis=-1, keepdims=True)

    streamed(gq, qag_all, add_scaled)
    line_up[...] = jnp.zeros_like(line_up)
    for j in range(4):
        line_up[:, j : j + 1] = rsum[128 * j : 128 * j + 128]
    rs_all[4] = line_up[...].T[:8]
    for k in (1, 2, 3):
        small.append(
            remote(rs_all.at[4], rs_all.at[y], s_d.at[1, k], r_d.at[1, k], yp[k - 1])
        )
    rs_all[y] = rs_all[4]
    rc.first()
    ro.second()
    for n, (out, f) in enumerate(((ko, f_k), (vo, f_v))):
        for copy in sent3[3 * n : 3 * n + 3]:
            copy.wait_recv()
        out[...] = (
            f[0, :, cols(y, 512)].astype(F32)
            + f[1, :, pl.ds(0, 512)].astype(F32)
            + f[2, :, pl.ds(0, 512)].astype(F32)
            + f[3, :, pl.ds(0, 512)].astype(F32)
        )
    rq.second()
    ro.third()
    rc.second()
    for copy in small[3:]:
        copy.wait_recv()
    total = rs_all[0] + rs_all[1] + rs_all[2] + rs_all[3]
    mean = (total / 4096).T
    rstd = lax.rsqrt((sq[0] + sq[1] + sq[2] + sq[3]) / 4096 + EPS).T
    for s in range(8):
        rows, half, j = slice(64 * s, 64 * s + 64), slice(64 * (s % 2), 64 * (s % 2) + 64), s // 2
        r, m = rstd[half, j : j + 1], mean[half, j : j + 1]
        hidden[rows] = (
            og[rows].astype(F32)
            + (r * hidden[rows] - xs[rows].astype(F32) * (r * r * r * m))
            + sgrad[s : s + 1]
        )
    rq.third()
    rc.third()
    for r in (ro, rq, rc):
        r.swapped.wait_send()
        r.end()
    for copy in small + ring + sent + passed + sent2 + sent3:
        copy.wait_send()


def halves_scratch(w):
    return [
        pltpu.VMEM((4, 2, 2, 32, 4 * w), BF16),
        pltpu.VMEM((3, 2, 32, 4 * w), BF16),
        pltpu.VMEM((3, 4, 2, 32, w), BF16),
        pltpu.VMEM((2, 32, 4 * w), BF16),
        pltpu.VMEM((4, 2, 32, w), BF16),
        pltpu.VMEM((3, 2, 32, w), BF16),
        pltpu.VMEM((3, 2, 32, w), BF16),
        pltpu.VMEM((2, 2, 32, w), BF16),
    ]


def backward(*operands):
    shape = jax.ShapeDtypeStruct
    rows = (4, 4, 2, 32)
    return pl.pallas_call(
        backward_kernel,
        out_shape=(
            shape((512, 1024), BF16),
            shape((512, 1024), F32),
            shape((2, 2, 32, 512), BF16),
            shape((2, 2, 32, 512), BF16),
            shape((2, 2, 32, 256), BF16),
            shape((32, 512), F32),
            shape((32, 512), F32),
        ),
        in_specs=[VM] * 15 + [ANY] * 4,
        out_specs=(VM,) * 7,
        scratch_shapes=[
            pltpu.VMEM((2, 256, 2048), BF16),
            pltpu.VMEM((1024, 512), BF16),
            pltpu.VMEM((4, 128, 2048), BF16),
            pltpu.VMEM((4, 128, 2048), BF16),
            pltpu.VMEM((4, 2, 1024), F32),
            pltpu.VMEM((5, 8, 128), F32),
            pltpu.VMEM(rows + (2048,), BF16),
            pltpu.VMEM(rows + (2048,), BF16),
            pltpu.VMEM(rows + (1024,), BF16),
            pltpu.VMEM((128, 128), F32),
            pltpu.VMEM((512, 1), F32),
            pltpu.VMEM((512, 1), F32),
            pltpu.VMEM((512, 1), F32),
            pltpu.VMEM((8, 1024), F32),
            pltpu.VMEM((2, 1024), F32),
            pltpu.VMEM((4, 4, 32, 2048), BF16),
            pltpu.VMEM((4, 4, 32, 2048), BF16),
            pltpu.VMEM((3, 4, 32, 2048), BF16),
            pltpu.VMEM((3, 4, 32, 2048), BF16),
            pltpu.VMEM((4, 32, 2048), BF16),
            pltpu.VMEM((4, 32, 2048), BF16),
            pltpu.VMEM((3, 32, 2048), BF16),
            pltpu.VMEM((3, 32, 2048), BF16),
            pltpu.VMEM((4, 32, 2048), BF16),
            pltpu.VMEM((4, 32, 2048), BF16),
        ]
        + halves_scratch(512)
        + halves_scratch(512)
        + halves_scratch(256)
        + [
            DMA((2, 4)), DMA((2, 4)),
            DMA((2, 4)), DMA((2, 4)),
            DMA((2,)), DMA((2,)),
            DMA((2, 4)), DMA((2, 4)),
            DMA((2, 4)), DMA((2, 4)),
            DMA((2, 4)), DMA((2, 4)),
            DMA((3, 14)), DMA((3, 14)),
            DMA((2,)),
        ],
        compiler_params=pltpu.CompilerParams(
            collective_id=1, has_side_effects=True, vmem_limit_bytes=60 << 20
        ),
        name="backward",
    )(*operands)


def attention_kernel(q_ref, g_ref, k_ref, v_ref, att_ref, qag_ref, kag_ref, vag_ref):
    scale = HSZ ** (-0.5)
    for h in range(q_ref.shape[1] // HSZ):
        lanes = slice(h * HSZ, (h + 1) * HSZ)
        for s in range(2):
            rows, keys = slice(s * SPAN, (s + 1) * SPAN), slice(s * 2 * NL, (s + 1) * 2 * NL)
            q, g = q_ref[rows, lanes], g_ref[rows, lanes]
            k, v = k_ref[keys, lanes], v_ref[keys, lanes]
            score = dot_nt(q, k) * scale
            e = jnp.exp(score - jnp.max(score, axis=-1, keepdims=True))
            full = e / jnp.sum(e, axis=-1, keepdims=True)
            weights = full.astype(BF16)
            att_ref[rows, lanes] = dot_nn(weights, v).astype(BF16)
            pg = dot_nt(g, v)
            sg = (full * (pg - jnp.sum(full * pg, axis=-1, keepdims=True)) * scale).astype(BF16)
            qag_ref[rows, lanes] = dot_nn(sg, k).astype(BF16)
            kag_ref[keys, lanes] = dot_tn(sg, q).astype(BF16)
            vag_ref[keys, lanes] = dot_tn(weights, g).astype(BF16)


def attention(q, g, k, v):
    few = pl.BlockSpec((128, 256), lambda h: (0, h))
    many = pl.BlockSpec((512, 256), lambda h: (0, h))
    return pl.pallas_call(
        attention_kernel,
        grid=(8,),
        out_shape=(
            jax.ShapeDtypeStruct((128, 2048), BF16),
            jax.ShapeDtypeStruct((128, 2048), BF16),
            jax.ShapeDtypeStruct((512, 2048), BF16),
            jax.ShapeDtypeStruct((512, 2048), BF16),
        ),
        in_specs=[few, few, many, many],
        out_specs=(few, few, many, many),
        name="attention",
    )(q, g, k, v)


def wide_columns(n):
    r = lax.broadcasted_iota(jnp.int32, (28 * n, 32 * n), 0)
    s = lax.broadcasted_iota(jnp.int32, (28 * n, 32 * n), 1)
    return ((r // 28 == s // 32) & (r % 28 == s % 32)).astype(BF16)


def lines(v):
    return jnp.pad(v.reshape(4, 128), ((0, 4), (0, 0)))


def shards(
    hidden, norm_gain, w_query, w_key, w_value, w_out, w_cond, enc_gain, store, neighbour_ids,
    out_grad,
):
    y = lax.axis_index("enc")
    xf = hidden.astype(F32)
    gain = lax.dynamic_slice_in_dim(norm_gain, y * 1024, 1024)
    sq = lines(jnp.sum(xf * xf, axis=-1))
    summary = jnp.mean(xf.reshape(8, SPAN, 1024), axis=1).astype(BF16)
    ids = jnp.pad(neighbour_ids.reshape(1, 4), ((0, 7), (0, 124)))
    wc = dot_nn(w_cond, wide_columns(8)).astype(BF16)
    wk = jnp.pad(w_key, ((0, 4), (0, 0)))
    wv = jnp.pad(w_value, ((0, 4), (0, 0)))
    raw, sq_all, q, ag, cond, normed_t, out_grad_t, gq, go, gc, gk, gv = forward(
        ids, sq, gain.reshape(1, 1024), hidden, out_grad, summary, store,
        w_query, w_out.T, wc, wk, wv,
    )
    gk, gv = gk.reshape(PE, 2048), gv.reshape(PE, 2048)

    egain = jnp.pad(enc_gain.reshape(32, 28), ((0, 0), (0, 4))).reshape(PE)
    rawp = dot_nn(raw.reshape(512, DE), wide_columns(32))
    cond_rows = cond.astype(BF16).astype(F32)
    enc_in = (rawp.reshape(2, 256, PE) + cond_rows[:, None, :]).reshape(512, PE)
    enc_rstd = lax.rsqrt(jnp.sum(enc_in * enc_in, axis=-1, keepdims=True) / DE + EPS)
    encoded = (enc_in * enc_rstd * egain).astype(BF16)
    keys = dot_nn(encoded, gk).astype(BF16)
    values = dot_nn(encoded, gv).astype(BF16)
    att, qag, kag, vag = attention(q, ag, keys, values)
    layer_out, hidden_grad, qo, oo, co, kg, vg = backward(
        att, qag, kag, vag, encoded, enc_in, egain.reshape(1, PE), hidden, out_grad,
        gain.reshape(1, 1024), normed_t, out_grad_t, summary, sq_all, gc,
        gq.reshape(4, 256, 2048), go.reshape(4, 256, 2048),
        gk.reshape(4, 256, 2048), gv.reshape(4, 256, 2048),
    )
    cond_grad = co.astype(F32).reshape(128, 8, 32)[:, :, :28].reshape(128, 224)
    return (
        layer_out,
        hidden_grad,
        qo.reshape(128, 512).astype(F32),
        kg[:28],
        vg[:28],
        oo.reshape(128, 512).T.astype(F32),
        cond_grad,
    )


def solution(mesh):
    placed = (
        P("dp", "enc"), P(), P("dp", "enc"), P("dp", "enc"), P("dp", "enc"), P("enc", "dp"),
        P("dp", "enc"), P(), P(("dp", "enc"), None, None), P(("dp", "enc")), P("dp", "enc"),
    )
    return jax.shard_map(
        shards,
        mesh=mesh,
        in_specs=placed,
        out_specs=(
            P("dp", "enc"), P("dp", "enc"), P("dp", "enc"), P("dp", "enc"), P("dp", "enc"),
            P("enc", "dp"), P("dp", "enc"),
        ),
        check_vma=False,
    )
```

```python
import functools

import jax
import jax.numpy as jnp
from jax import lax
from jax.experimental import pallas as pl
from jax.experimental.pallas import tpu as pltpu
from jax.sharding import PartitionSpec as P

MESH = pl.DeviceIdType.MESH
F32 = jnp.float32
BF16 = jnp.bfloat16
HSZ = 128
SPAN = 64
NL = 128
DE = 896
PE = 1024
EPS = 1e-05
ANY = pl.BlockSpec(memory_space=pl.ANY)
VM = pl.BlockSpec(memory_space=pltpu.VMEM)
DMA = pltpu.SemaphoreType.DMA


def place():
    d = lax.axis_index("dp")
    return d // 8, (d // 2) % 4, d % 2, lax.axis_index("enc")


def at(x, z, c, y):
    return ((x * 4 + z) * 2 + c, y)


def around(v, k):
    return (v + k) % 4


def remote(src, dst, send, recv, device):
    copy = pltpu.make_async_remote_copy(
        src, dst, send, recv, device_id=device, device_id_type=MESH
    )
    copy.start()
    return copy


def meet(peers, partner=None, has_partner=None):
    barrier = pltpu.get_barrier_semaphore()
    for peer in peers:
        pl.semaphore_signal(barrier, inc=1, device_id=peer, device_id_type=MESH)
    if partner is not None:

        @pl.when(has_partner)
        def _():
            pl.semaphore_signal(barrier, inc=1, device_id=partner, device_id_type=MESH)

        pl.semaphore_wait(barrier, jnp.where(has_partner, len(peers) + 1, len(peers)))
    else:
        pl.semaphore_wait(barrier, len(peers))


def sum_rows(out, terms, step=16):
    rows = out.shape[0]

    def body(i, carry):
        at_row = pl.ds(pl.multiple_of(i * step, step), step)
        total = terms[0][at_row].astype(F32)
        for t in terms[1:]:
            total = total + t[at_row].astype(F32)
        out[at_row] = total.astype(out.dtype)
        return carry

    lax.fori_loop(0, rows // step, body, 0)


def cols(i, n):
    return pl.ds(pl.multiple_of(i * n, n), n)


def pick_rows(ids_s, r):
    every = [ids_s[r, 0, k] for k in range(4)]
    owner = [(v // 8) % 4 for v in every]
    row = [v % 8 for v in every]
    rank = []
    for k in range(4):
        n = jnp.int32(0)
        for j in range(k):
            n = n + jnp.where(owner[j] == owner[k], 1, 0)
        rank.append(n)
    return owner, row, rank


class Plane:
    def __init__(self, put, line, cut, whole, axes, sems):
        self.put, self.line, self.cut, self.whole = put, line, cut, whole
        self.x, self.z, self.xp, self.zp, self.sib = axes
        self.s, self.r = sems
        self.one, self.two, self.on, self.last = [[], []], [[], []], [[], []], None

    def first(self):
        for h in range(2):
            src, dst, keep = self.put(h)
            for k in (2, 1, 3):
                peer = (self.zp if h else self.xp)[k - 1]
                self.one[h].append(remote(src, dst, self.s.at[h, k], self.r.at[h, k], peer))
            if keep is not None:
                copy = pltpu.make_async_copy(src, dst, self.s.at[h, 0])
                copy.start()
                copy.wait()

    def second(self):
        for h in range(2):
            for copy in self.one[h]:
                copy.wait_recv()
            block = self.line(h, self.x if h else self.z)
            for k in (1, 3):
                peer = (self.xp if h else self.zp)[k - 1]
                self.two[h].append(
                    remote(block, block, self.s.at[h, 3 + k], self.r.at[h, 3 + k], peer)
                )

    def relay(self):
        for h in range(2):
            place = self.x if h else self.z
            for j, k in ((0, 1), (1, 3)):
                self.two[h][j].wait_recv()
                block = self.cut(h, around(place, 4 - k), j)
                peer = (self.xp if h else self.zp)[k - 1]
                self.on[h].append(
                    remote(block, block, self.s.at[h, 7 + k], self.r.at[h, 7 + k], peer)
                )

    def swap(self):
        for copy in self.on[0] + self.on[1]:
            copy.wait_recv()
        self.last = remote(self.whole, self.whole, self.s.at[0, 5], self.r.at[0, 5], self.sib)

    def sent(self):
        every = self.one[0] + self.one[1] + self.two[0] + self.two[1]
        for copy in every + self.on[0] + self.on[1] + [self.last]:
            copy.wait_send()


class Sums:
    def __init__(self, p, bufs, y, right, left, sems):
        self.p, self.y, self.right, self.left = p, y, right, left
        self.far_a, self.far_b, self.from_left, self.from_right = bufs
        self.s, self.r = sems
        self.far, self.near, self.late = [], [], []

    def send(self, n, src, dst, peer):
        return remote(src, dst, self.s.at[n], self.r.at[n], peer)

    def first(self):
        p, y = self.p, self.y
        a, b = pl.ds(0, 64), pl.ds(64, 64)
        self.far = [
            self.send(0, p.at[around(y, 2), a], self.far_a, self.right),
            self.send(1, p.at[around(y, 2), b], self.far_b, self.left),
        ]
        self.near = [
            self.send(2, p.at[around(y, 1), b], self.from_left.at[b], self.right),
            self.send(3, p.at[around(y, 3), a], self.from_right.at[a], self.left),
        ]

    def second(self):
        p, y = self.p, self.y
        moves = (
            (0, self.far_a, around(y, 1), 0, self.from_left, self.right),
            (1, self.far_b, around(y, 3), 64, self.from_right, self.left),
        )
        for n, far, target, low, dst, peer in moves:
            self.far[n].wait_recv()

            def fold(i, carry, far=far, target=target, low=low):
                rows = pl.ds(pl.multiple_of(low + i * 16, 16), 16)
                more = far[pl.ds(pl.multiple_of(i * 16, 16), 16)].astype(F32)
                p[target, rows] = (p[target, rows].astype(F32) + more).astype(BF16)
                return carry

            lax.fori_loop(0, 4, fold, 0)
            half = pl.ds(low, 64)
            self.late.append(self.send(4 + n, p.at[target, half], dst.at[half], peer))

    def third(self, out):
        for copy in self.near + self.late:
            copy.wait_recv()
        sum_rows(out, [self.p.at[self.y], self.from_left, self.from_right])

    def sent(self):
        for copy in self.far + self.near + self.late:
            copy.wait_send()


def forward_kernel(
    ids_in, gain, xs, og, egain, store, wq, wo_in, wc_in, wk_in, wv_in,
    sq_all, sm, q, a, keys, values, enc, ein, nt, ogt, hq, ho, hc, hk, hv,
    ids_all, ids_s, out_rows, in_rows, tq, to, tc, yk, yv, gq, go, gc, gk, gv,
    normed, qp, ap, cp, q0, q1, q2, q3, a0, a1, a2, a3, rc,
    ids, sq, line_up, means, pick_cols, wo, wc, wk, wv,
    s_small, r_small, s_row, r_row, s_t, r_t, s_p, r_p, s_w, r_w, s_y, r_y, s_q, r_q, s_a, r_a,
    s_loc, s_out,
):
    x, z, c, y = place()
    yp = [at(x, z, c, around(y, k)) for k in (1, 2, 3)]
    xp = [at(around(x, k), z, c, y) for k in (1, 2, 3)]
    zp = [at(x, around(z, k), c, y) for k in (1, 2, 3)]
    sib = at(x, z, 1 - c, y)
    partner = at(y, z, c, x)
    axes = (x, z, xp, zp, sib)
    meet(yp + xp + zp + [sib], partner, x != y)

    moves = ((wq, tq), (wo, to), (wc, tc))

    def cross(n):
        w, t = moves[n]

        @pl.when(x != y)
        def _():
            remote(w, t, s_t.at[n], r_t.at[n], partner)

        @pl.when(x == y)
        def _():
            pltpu.make_async_copy(w, t, r_t.at[n]).start()

    def arrived(n):
        w, t = moves[n]
        pltpu.make_async_copy(w, t, r_t.at[n]).wait()

    cross(0)
    ids[...] = jnp.zeros_like(ids)
    ids[0:1, 0:4] = ids_in[...]
    small = []
    for k in (1, 2, 3):
        small.append(remote(ids, ids_all.at[y], s_small.at[0, k], r_small.at[0, k], yp[k - 1]))
    ids_all[y] = ids[...]
    line_up[...] = jnp.zeros_like(line_up)
    for j in range(4):
        part = xs[128 * j : 128 * (j + 1)].astype(F32)
        line_up[:, j : j + 1] = jnp.sum(part * part, axis=-1, keepdims=True)
        for i in range(2):
            row = jnp.sum(part[64 * i : 64 * i + 64], axis=0, keepdims=True) / SPAN
            means[2 * j + i : 2 * j + i + 1] = row
    sm[...] = means[...].astype(BF16)
    sq[...] = line_up[...].T[:8]
    sq_all[y] = sq[...]
    for k in (1, 2, 3):
        small.append(remote(sq, sq_all.at[y], s_small.at[1, k], r_small.at[1, k], yp[k - 1]))
    wo[...] = wo_in[...].T
    spot = lax.broadcasted_iota(jnp.int32, (1, PE), 1)
    source = jnp.where(spot % 32 < 28, spot // 32 * 28 + spot % 32, -1)
    for i in range(7):
        row = lax.broadcasted_iota(jnp.int32, (128, PE), 0) + 128 * i
        pick_cols[128 * i : 128 * (i + 1)] = jnp.where(row == source, 1.0, 0.0).astype(BF16)
    wc[...] = dot_nn(wc_in[...], pick_cols[0:224, 0:256]).astype(BF16)
    for w, v in ((wk, wk_in), (wv, wv_in)):
        w[...] = jnp.zeros_like(w)
        w[0:28] = v[...]
    for copy in small[:3]:
        copy.wait_recv()
    to_s = pltpu.make_async_copy(ids_all, ids_s, s_loc.at[0])
    to_s.start()
    to_s.wait()

    row_copies = []
    for k in (2, 1, 3, 0):
        owner, row, rank = pick_rows(ids_s, around(y, k))
        for n in range(2):
            pick = jnp.int32(0)
            for j in range(4):
                pick = pick + jnp.where((owner[j] == y) & (rank[j] == n), row[j], 0)
            if k:
                out_rows[k, n] = store[pick]
            else:
                in_rows[y, n] = store[pick]
        if k:
            row_copies.append(
                remote(out_rows.at[k], in_rows.at[y], s_row.at[k], r_row.at[k], yp[k - 1])
            )

    def weight(n, t, g, w):
        def put(h):
            rows = pl.ds(64 * h, 64)
            return t.at[rows], g.at[z, c, rows, cols(x, w)], True

        def line(h, i):
            if h:
                return g.at[:, c, pl.ds(64, 64), cols(i, w)]
            return g.at[i, c, pl.ds(0, 64)]

        def cut(h, i, j):
            if h:
                return g.at[:, c, pl.ds(64 + 32 * j, 32), cols(i, w)]
            return g.at[i, c, pl.ds(32 * j, 32)]

        return Plane(put, line, cut, g.at[:, c], axes, (s_p.at[n], r_p.at[n]))

    pq, po, pc = weight(0, tq, gq, 512), weight(1, to, go, 512), weight(2, tc, gc, 256)

    def kv_put(h):
        return (yv, gv.at[x, z, c], True) if h else (yk, gk.at[x, z, c], True)

    def kv_line(h, i):
        return gv.at[i, :, c] if h else gk.at[:, i, c]

    def kv_cut(h, i, j):
        if h:
            return gv.at[i, pl.ds(2 * j, 2), c]
        return gk.at[pl.ds(2 * j, 2), i, c]

    pk = KeyPlane(
        kv_put, kv_line, kv_cut, (gk.at[:, :, c], gv.at[:, :, c]), axes, (s_p.at[3], r_p.at[3])
    )
    rq = Sums(qp, (q0, q1, q2, q3), y, yp[0], yp[2], (s_q, r_q))
    ra = Sums(ap, (a0, a1, a2, a3), y, yp[0], yp[2], (s_a, r_a))

    arrived(0)
    cross(2)
    cross(1)
    pq.first()
    across = []
    for n, (w, t) in enumerate(((wk, yk), (wv, yv))):
        for k in (2, 1, 3):
            across.append(
                remote(w, t.at[:, cols(y, 512)], s_w.at[n, k], r_w.at[n, k], yp[k - 1])
            )
        t[:, cols(y, 512)] = w[...]
    pq.second()
    arrived(2)
    pc.first()
    for copy in small[3:]:
        copy.wait_recv()
    total = sq_all[0] + sq_all[1] + sq_all[2] + sq_all[3]
    rstd = lax.rsqrt(total / 4096 + EPS).T
    for j in range(4):
        rows = slice(128 * j, 128 * (j + 1))
        normed[rows] = (xs[rows].astype(F32) * rstd[:, j : j + 1] * gain[:, cols(y, 1024)]).astype(BF16)
    arrived(1)
    po.first()
    pq.relay()
    pc.second()
    po.second()
    pq.swap()
    pc.relay()
    outs = []

    def keep(n, g, h):
        copy = pltpu.make_async_copy(g, h, s_out.at[n])
        copy.start()
        outs.append(copy)

    def product(act, g, put):
        def tile(i, carry):
            lanes = cols(i, 256)
            put(lanes, dot_nn(act[...], g[..., lanes].reshape(1024, 256)).astype(BF16))
            return carry

        lax.fori_loop(0, 8, tile, 0)

    def into(p):
        def put(lanes, value):
            p[:, :, lanes] = value.reshape(4, 128, 256)

        return put

    pq.last.wait_recv()
    product(normed, gq, into(qp))
    rq.first()
    keep(0, gq, hq)
    pc.swap()
    po.relay()
    for copy in across:
        copy.wait_recv()
    pk.first()
    pc.last.wait_recv()
    keep(2, gc, hc)
    for i in range(4):
        lanes = slice(256 * i, 256 * (i + 1))
        w = gc[:, :, :, lanes].reshape(1024, 256)
        cp[:, lanes] = dot_nn(sm[...], w)
    for j in range(4):
        rc[j + 4] = cp[2 * j : 2 * j + 2]
    parts = []
    for k in (2, 1, 3):
        parts.append(
            remote(rc.at[4 + around(y, k)], rc.at[k], s_y.at[k], r_y.at[k], yp[k - 1])
        )
    rq.second()
    po.swap()
    pk.second()
    po.last.wait_recv()
    product(og, go, into(ap))
    ra.first()
    keep(1, go, ho)
    for copy in row_copies:
        copy.wait_recv()
    owner, row, rank = pick_rows(ids_s, y)
    for k in range(4):
        rows = slice(128 * k, 128 * (k + 1))
        ein[rows] = dot_nn(in_rows[owner[k], jnp.minimum(rank[k], 1)], pick_cols[...])
    pk.relay()
    for copy in parts:
        copy.wait_recv()
    cond = (rc[4 + y] + rc[1] + rc[2] + rc[3]).astype(BF16).astype(F32)
    for k in range(4):
        rows = slice(128 * k, 128 * (k + 1))
        row = ein[rows] + cond[k // 2 : k // 2 + 1]
        ein[rows] = row
        scale = lax.rsqrt(jnp.sum(row * row, axis=-1, keepdims=True) / DE + EPS)
        enc[rows] = (row * scale * egain[...]).astype(BF16)
    ra.second()
    pk.swap()
    for j in range(4):
        rows = slice(128 * j, 128 * (j + 1))
        nt[:, rows] = normed[rows].T
        ogt[:, rows] = og[rows].T
    rq.third(q)
    for n, (g, h, out) in enumerate(((gk, hk, keys), (gv, hv, values))):
        pk.last[n].wait_recv()
        keep(3 + n, g, h)

        def put(lanes, value, out=out):
            out[:, lanes] = value

        product(enc, g, put)
    ra.third(a)
    for copy in outs:
        copy.wait()
    for copy in small + across + row_copies + parts:
        copy.wait_send()
    for plane in (pq, po, pc, pk, rq, ra):
        plane.sent()

    @pl.when(x != y)
    def _():
        for n, (w, t) in enumerate(moves):
            pltpu.make_async_copy(w, t, s_t.at[n]).wait()


class KeyPlane(Plane):
    def swap(self):
        for copy in self.on[0] + self.on[1]:
            copy.wait_recv()
        self.last = [
            remote(ref, ref, self.s.at[n, 5], self.r.at[n, 5], self.sib)
            for n, ref in enumerate(self.whole)
        ]

    def sent(self):
        every = self.one[0] + self.one[1] + self.two[0] + self.two[1]
        for copy in every + self.on[0] + self.on[1] + self.last:
            copy.wait_send()


def forward(*operands):
    wide, slim, keys = (4, 2, 128, 2048), (4, 2, 128, 1024), (4, 4, 2, 32, 2048)
    shape = jax.ShapeDtypeStruct
    halves = [
        pltpu.VMEM((64, 2048), BF16),
        pltpu.VMEM((64, 2048), BF16),
        pltpu.VMEM((128, 2048), BF16),
        pltpu.VMEM((128, 2048), BF16),
    ]
    return pl.pallas_call(
        forward_kernel,
        out_shape=(
            shape((4, 8, 128), F32),
            shape((8, 1024), BF16),
            shape((128, 2048), BF16),
            shape((128, 2048), BF16),
            shape((512, 2048), BF16),
            shape((512, 2048), BF16),
            shape((512, PE), BF16),
            shape((512, PE), F32),
            shape((1024, 512), BF16),
            shape((1024, 512), BF16),
            shape(wide, BF16),
            shape(wide, BF16),
            shape(slim, BF16),
            shape(keys, BF16),
            shape(keys, BF16),
        ),
        in_specs=[VM] * 11,
        out_specs=(VM,) * 10 + (ANY,) * 5,
        scratch_shapes=[
            pltpu.VMEM((4, 8, 128), jnp.int32),
            pltpu.SMEM((4, 8, 128), jnp.int32),
            pltpu.VMEM((4, 2, NL, DE), BF16),
            pltpu.VMEM((4, 2, NL, DE), BF16),
            pltpu.VMEM((128, 512), BF16),
            pltpu.VMEM((128, 512), BF16),
            pltpu.VMEM((128, 256), BF16),
            pltpu.VMEM((32, 2048), BF16),
            pltpu.VMEM((32, 2048), BF16),
            pltpu.VMEM(wide, BF16),
            pltpu.VMEM(wide, BF16),
            pltpu.VMEM(slim, BF16),
            pltpu.VMEM(keys, BF16),
            pltpu.VMEM(keys, BF16),
            pltpu.VMEM((512, 1024), BF16),
            pltpu.VMEM((4, 128, 2048), BF16),
            pltpu.VMEM((4, 128, 2048), BF16),
            pltpu.VMEM((8, 1024), F32),
        ]
        + halves
        + halves
        + [
            pltpu.VMEM((8, 2, 1024), F32),
            pltpu.VMEM((8, 128), jnp.int32),
            pltpu.VMEM((8, 128), F32),
            pltpu.VMEM((128, 128), F32),
            pltpu.VMEM((8, 1024), F32),
            pltpu.VMEM((DE, PE), BF16),
            pltpu.VMEM((128, 512), BF16),
            pltpu.VMEM((128, 256), BF16),
            pltpu.VMEM((32, 512), BF16),
            pltpu.VMEM((32, 512), BF16),
            DMA((2, 4)), DMA((2, 4)),
            DMA((4,)), DMA((4,)),
            DMA((3,)), DMA((3,)),
            DMA((4, 2, 11)), DMA((4, 2, 11)),
            DMA((2, 4)), DMA((2, 4)),
            DMA((4,)), DMA((4,)),
            DMA((6,)), DMA((6,)),
            DMA((6,)), DMA((6,)),
            DMA((1,)),
            DMA((5,)),
        ],
        compiler_params=pltpu.CompilerParams(
            collective_id=0, has_side_effects=True, vmem_limit_bytes=58 << 20
        ),
        name="forward",
    )(*operands)


def dot_nn(a, b):
    return jnp.dot(a, b, preferred_element_type=F32)


def dot_nt(a, b):
    return lax.dot_general(a, b, (((1,), (1,)), ((), ())), preferred_element_type=F32)


def dot_tn(a, b):
    return lax.dot_general(a, b, (((0,), (0,)), ((), ())), preferred_element_type=F32)


class Around:
    def __init__(self, half, bufs, place, right, left, sems, base):
        self.half, self.place, self.right, self.left = half, place, right, left
        self.far, self.from_left, self.from_right = bufs
        self.s, self.r, self.base = sems[0], sems[1], base
        self.sends = []

    def send(self, n, src, dst, peer):
        n = self.base + n
        self.sends.append(remote(src, dst, self.s.at[n], self.r.at[n], peer))

    def first(self):
        half, p = self.half, self.place
        self.send(0, half(around(p, 2), 0), self.far.at[0], self.right)
        self.send(1, half(around(p, 2), 1), self.far.at[1], self.left)
        self.send(2, half(around(p, 1), 1), self.from_left.at[1], self.right)
        self.send(3, half(around(p, 3), 0), self.from_right.at[0], self.left)

    def mid(self):
        moves = ((0, 1, self.from_left, self.right), (1, 3, self.from_right, self.left))
        for n, k, dst, peer in moves:
            self.sends[n].wait_recv()
            own = self.half(around(self.place, k), n)
            own[...] = (own[...].astype(F32) + self.far[n].astype(F32)).astype(BF16)
            self.send(4 + n, own, dst.at[n], peer)

    def here(self):
        for copy in self.sends[2:]:
            copy.wait_recv()

    def total(self, i):
        own = self.half(self.place, i)[...].astype(F32)
        return (own + self.from_left[i].astype(F32) + self.from_right[i].astype(F32)).astype(BF16)

    def sent(self):
        for copy in self.sends:
            copy.wait_send()


class Halves:
    def __init__(self, p, bufs, out, w, spots, sems):
        self.p, self.out, self.w = p, out, w
        self.b, fa, la, ra, fb, lb, rb, self.wa, self.wb, self.va, self.vb, self.f = bufs
        self.x, self.z, self.c, self.y, self.xp, self.zp, self.sib = spots
        self.s, self.r = sems
        self.two, self.swapped = [[], []], None
        b = self.b
        self.ringa = Around(
            lambda t, i: b.at[t, 0, i], (fa, la, ra), self.z, self.zp[0], self.zp[2], sems, 14
        )
        self.ringb = Around(
            lambda t, i: b.at[:, 1, i, :, cols(t, w)], (fb, lb, rb), self.x, self.xp[0],
            self.xp[2], sems, 20,
        )

    def swap(self):
        src = self.p.at[:, pl.ds(2 * (1 - self.c), 2)]
        self.swapped = remote(src, self.b, self.s.at[0], self.r.at[0], self.sib)

    def first(self):
        self.swapped.wait_recv()
        p, b, c = self.p, self.b, self.c

        def fold(i, carry):
            j, h, k = i // 4, (i // 2) % 2, i % 2
            b[j, h, k] = (p[j, 2 * c + h, k].astype(F32) + b[j, h, k].astype(F32)).astype(BF16)
            return carry

        lax.fori_loop(0, 16, fold, 0)
        self.ringa.first()
        self.ringb.first()

    def mid(self):
        self.ringa.mid()
        self.ringb.mid()

    def second(self):
        wa, wb = self.wa, self.wb
        self.ringa.here()
        for i in range(2):
            wa[i] = self.ringa.total(i)
        for k in (2, 1, 3):
            lanes = cols(around(self.x, k), self.w)
            self.two[0].append(
                remote(wa.at[:, :, lanes], self.va.at[k - 1], self.s.at[6 + k], self.r.at[6 + k], self.xp[k - 1])
            )
        self.ringb.here()
        for i in range(2):
            wb[:, i] = self.ringb.total(i)
        for k in (2, 1, 3):
            self.two[1].append(
                remote(wb.at[around(self.z, k)], self.vb.at[k - 1], self.s.at[9 + k], self.r.at[9 + k], self.zp[k - 1])
            )

    def third(self):
        x, y, z, f, va, vb = self.x, self.y, self.z, self.f, self.va, self.vb
        for copy in self.two[0] + self.two[1]:
            copy.wait_recv()
        for i in range(2):
            f[0, i] = (
                self.wa[i, :, cols(x, self.w)].astype(F32) + va[0, i].astype(F32)
                + va[1, i].astype(F32) + va[2, i].astype(F32)
            ).astype(BF16)
            f[1, i] = (
                self.wb[z, i].astype(F32) + vb[0, i].astype(F32)
                + vb[1, i].astype(F32) + vb[2, i].astype(F32)
            ).astype(BF16)

        @pl.when(x != y)
        def _():
            remote(f, self.out, self.s.at[13], self.r.at[13], at(y, z, self.c, x))

        @pl.when(x == y)
        def _():
            pltpu.make_async_copy(f, self.out, self.r.at[13]).start()

    def end(self):
        pltpu.make_async_copy(self.f, self.out, self.r.at[13]).wait()
        for copy in self.two[0] + self.two[1]:
            copy.wait_send()
        self.ringa.sent()
        self.ringb.sent()

        @pl.when(self.x != self.y)
        def _():
            pltpu.make_async_copy(self.f, self.out, self.s.at[13]).wait()


def backward_kernel(
    att, qag, kag, vag, enc, ein, egain, xs, og, gain, nt, ogt, sm, sq, gc, gq, go, gk, gv,
    layer, hidden, qo, oo, co, ko, vo,
    tile, et, att_all, qag_all, cd_all, rs_all, p1, p2, p3, line_up, erstd, emean, rsum, sgrad, slot,
    *scratch,
):
    b_k, b_v, ak, lk, rk, av, lv, rv, w_k, w_v, x_k, x_v, f_k, f_v = scratch[:14]
    bq, bo, bc = scratch[14:26], scratch[26:38], scratch[38:50]
    s_y, r_y, s_d, r_d, s_c, r_c, s_1, r_1, s_2, r_2, s_3, r_3, s_h, r_h, s_tile = scratch[50:]
    x, z, c, y = place()
    yp = [at(x, z, c, around(y, k)) for k in (1, 2, 3)]
    xp = [at(around(x, k), z, c, y) for k in (1, 2, 3)]
    zp = [at(x, around(z, k), c, y) for k in (1, 2, 3)]
    sib = at(x, z, 1 - c, y)
    meet(yp + xp + zp + [sib], at(y, z, c, x), x != y)
    spots = (x, z, c, y, xp, zp, sib)
    rq = Halves(p1, bq, qo, 512, spots, (s_h.at[0], r_h.at[0]))
    ro = Halves(p2, bo, oo, 512, spots, (s_h.at[1], r_h.at[1]))
    rc = Halves(p3, bc, co, 256, spots, (s_h.at[2], r_h.at[2]))

    ring = []
    for n, (src, dst) in enumerate(((att, att_all), (qag, qag_all))):
        for j, k in ((0, 1), (1, 3)):
            ring.append(remote(src, dst.at[y], s_y.at[n, j], r_y.at[n, j], yp[k - 1]))
    et[...] = enc[...].T

    def product(left, right, p, width=256):
        def step(i, carry):
            lanes = cols(i, width)
            r = right[..., lanes].reshape(left.shape[1], width)
            p[..., lanes] = dot_nn(left[...], r).astype(BF16).reshape(4, 4, 2, 32, width)
            return carry

        lax.fori_loop(0, p.shape[-1] // width, step, 0)

    swaps = []
    for n, (act, p, b) in enumerate(((kag, p1, b_k), (vag, p2, b_v))):
        product(et, act, p)
        swaps.append(remote(p.at[:, :, 1 - c], b, s_c.at[n], r_c.at[n], sib))
    att_all[y] = att[...]
    qag_all[y] = qag[...]

    passed = []

    def relay(n, dst):
        for j, k in ((0, 1), (1, 3)):
            ring[2 * n + j].wait_recv()
            block = dst.at[around(y, 4 - k), pl.ds(64 * j, 64)]
            passed.append(remote(block, block, s_y.at[n, 2 + j], r_y.at[n, 2 + j], yp[k - 1]))

    def pair(i):
        return pl.ds(2 * i, 2)

    kring = Around(
        lambda t, i: b_k.at[pair(i), t], (ak, lk, rk), z, zp[0], zp[2], (s_1, r_1), 0
    )
    vring = Around(
        lambda t, i: b_v.at[t, pair(i)], (av, lv, rv), x, xp[0], xp[2], (s_1, r_1), 6
    )
    rings = (kring, vring)
    for n, (p, b) in enumerate(((p1, b_k), (p2, b_v))):
        swaps[n].wait_recv()

        def fold(i, carry, p=p, b=b):
            b[i // 4, i % 4] = (
                p[i // 4, i % 4, c].astype(F32) + b[i // 4, i % 4].astype(F32)
            ).astype(BF16)
            return carry

        lax.fori_loop(0, 16, fold, 0)
        rings[n].first()
    for copy in swaps:
        copy.wait_send()
    relay(0, att_all)

    def fetch(h, i, j):
        return pltpu.make_async_copy(h.at[i], tile.at[j], s_tile.at[j])

    ee = ein[...]
    erstd[...] = lax.rsqrt(jnp.sum(ee * ee, axis=-1, keepdims=True) / DE + EPS)
    emean[...] = jnp.zeros_like(emean)
    fetch(gk, 0, 0).start()
    fetch(gv, 0, 1).start()
    kring.mid()
    vring.mid()

    def encoder(i, carry):
        lanes = cols(i, 256)
        fetch(gk, i, 0).wait()
        part = dot_nt(kag[...], tile[0])

        @pl.when(i < 3)
        def _():
            fetch(gk, i + 1, 0).start()

        fetch(gv, i, 1).wait()
        part = part + dot_nt(vag[...], tile[1])

        @pl.when(i < 3)
        def _():
            fetch(gv, i + 1, 1).start()

        ey = part.astype(BF16).astype(F32) * egain[:, lanes]
        emean[...] += jnp.sum(ein[:, lanes] * ey, axis=-1, keepdims=True)
        ry = ey * erstd[...]
        for s in range(2):
            slot[s : s + 1, lanes] = jnp.sum(ry[256 * s : 256 * s + 256], axis=0, keepdims=True)
        return carry

    lax.fori_loop(0, 4, encoder, 0)
    relay(1, qag_all)
    for s in range(2):
        rows = slice(256 * s, 256 * s + 256)
        weight = erstd[rows] ** 3 * (emean[rows] / DE)
        row = slot[s : s + 1] - jnp.sum(ein[rows] * weight, axis=0, keepdims=True)
        slot[s : s + 1] = row.astype(BF16).astype(F32)
    cd_all[y] = slot[...]
    small = [remote(slot, cd_all.at[y], s_d.at[0, k], r_d.at[0, k], yp[k - 1]) for k in (1, 2, 3)]

    for copy in passed[:2]:
        copy.wait_recv()
    product(ogt, att_all, p2)
    ro.swap()

    def streamed(h, act, use):
        fetch(h, 0, 0).start()

        def step(i, carry):
            fetch(h, i, i % 2).wait()

            @pl.when(i < 3)
            def _():
                fetch(h, i + 1, (i + 1) % 2).start()

            use(cols(i, 256), dot_nt(act[...].reshape(512, 2048), tile[i % 2]))
            return carry

        lax.fori_loop(0, 4, step, 0)

    sent2 = []
    ro.first()
    for n, (w, v) in enumerate(((w_k, x_k), (w_v, x_v))):
        rings[n].here()
        for i in range(2):
            w[pair(i)] = rings[n].total(i)
        for k in (2, 1, 3):
            if n:
                src, peer = w.at[around(z, k)], zp[k - 1]
            else:
                src, peer = w.at[around(x, k)], xp[k - 1]
            sent2.append(remote(src, v.at[k - 1], s_2.at[n, k], r_2.at[n, k], peer))
    for copy in passed[2:]:
        copy.wait_recv()
    product(nt, qag_all, p1)
    rq.swap()
    ro.mid()

    def add_out(lanes, value):
        layer[:, lanes] = (xs[:, lanes].astype(F32) + value).astype(BF16)

    streamed(go, att_all, add_out)
    rq.first()
    ro.second()
    sent3 = []
    for n, (w, v, f) in enumerate(((w_k, x_k, f_k), (w_v, x_v, f_v))):
        for copy in sent2[3 * n : 3 * n + 3]:
            copy.wait_recv()
        own = w[z] if n else w[x]
        f[0] = (
            own.astype(F32) + v[0].astype(F32) + v[1].astype(F32) + v[2].astype(F32)
        ).astype(BF16)
        for k in (2, 1, 3):
            src, dst = f.at[0, :, cols(around(y, k), 512)], f.at[k, :, pl.ds(0, 512)]
            sent3.append(remote(src, dst, s_3.at[n, k], r_3.at[n, k], yp[k - 1]))
    for copy in small:
        copy.wait_recv()
    cd = cd_all[...].reshape(8, 1024).astype(BF16)
    for i in range(4):
        lanes = slice(256 * i, 256 * i + 256)
        p3[..., lanes] = dot_tn(sm[...], cd[:, lanes]).astype(BF16).reshape(4, 4, 2, 32, 256)
    rc.swap()
    rq.mid()
    for i in range(4):
        sgrad[:, 256 * i : 256 * i + 256] = dot_nt(cd, gc[i].reshape(256, 1024)) / SPAN
    rsum[...] = jnp.zeros_like(rsum)

    def add_scaled(lanes, value):
        scaled = value * gain[:, pl.ds(pl.multiple_of(y * 1024 + lanes.start, 256), 256)]
        hidden[:, lanes] = scaled
        rsum[...] += jnp.sum(xs[:, lanes].astype(F32) * scaled, axis=-1, keepdims=True)

    streamed(gq, qag_all, add_scaled)
    line_up[...] = jnp.zeros_like(line_up)
    for j in range(4):
        line_up[:, j : j + 1] = rsum[128 * j : 128 * j + 128]
    rs_all[4] = line_up[...].T[:8]
    for k in (1, 2, 3):
        small.append(
            remote(rs_all.at[4], rs_all.at[y], s_d.at[1, k], r_d.at[1, k], yp[k - 1])
        )
    rs_all[y] = rs_all[4]
    rc.first()
    ro.third()
    rq.second()
    rc.mid()
    for n, (out, f) in enumerate(((ko, f_k), (vo, f_v))):
        for copy in sent3[3 * n : 3 * n + 3]:
            copy.wait_recv()
        out[...] = (
            f[0, :, cols(y, 512)].astype(F32)
            + f[1, :, pl.ds(0, 512)].astype(F32)
            + f[2, :, pl.ds(0, 512)].astype(F32)
            + f[3, :, pl.ds(0, 512)].astype(F32)
        )
    rc.second()
    rq.third()
    for copy in small[3:]:
        copy.wait_recv()
    total = rs_all[0] + rs_all[1] + rs_all[2] + rs_all[3]
    mean = (total / 4096).T
    rstd = lax.rsqrt((sq[0] + sq[1] + sq[2] + sq[3]) / 4096 + EPS).T
    for s in range(8):
        rows, half, j = slice(64 * s, 64 * s + 64), slice(64 * (s % 2), 64 * (s % 2) + 64), s // 2
        r, m = rstd[half, j : j + 1], mean[half, j : j + 1]
        hidden[rows] = (
            og[rows].astype(F32)
            + (r * hidden[rows] - xs[rows].astype(F32) * (r * r * r * m))
            + sgrad[s : s + 1]
        )
    rc.third()
    for r in (ro, rq, rc):
        r.swapped.wait_send()
        r.end()
    for r in rings:
        r.sent()
    for copy in small + ring + passed + sent2 + sent3:
        copy.wait_send()


def halves_scratch(w):
    return [
        pltpu.VMEM((4, 2, 2, 32, 4 * w), BF16),
        *[pltpu.VMEM((2, 32, 4 * w), BF16)] * 3,
        *[pltpu.VMEM((2, 4, 32, w), BF16)] * 3,
        pltpu.VMEM((2, 32, 4 * w), BF16),
        pltpu.VMEM((4, 2, 32, w), BF16),
        pltpu.VMEM((3, 2, 32, w), BF16),
        pltpu.VMEM((3, 2, 32, w), BF16),
        pltpu.VMEM((2, 2, 32, w), BF16),
    ]


def backward(*operands):
    shape = jax.ShapeDtypeStruct
    rows = (4, 4, 2, 32)
    return pl.pallas_call(
        backward_kernel,
        out_shape=(
            shape((512, 1024), BF16),
            shape((512, 1024), F32),
            shape((2, 2, 32, 512), BF16),
            shape((2, 2, 32, 512), BF16),
            shape((2, 2, 32, 256), BF16),
            shape((32, 512), F32),
            shape((32, 512), F32),
        ),
        in_specs=[VM] * 15 + [ANY] * 4,
        out_specs=(VM,) * 7,
        scratch_shapes=[
            pltpu.VMEM((2, 256, 2048), BF16),
            pltpu.VMEM((1024, 512), BF16),
            pltpu.VMEM((4, 128, 2048), BF16),
            pltpu.VMEM((4, 128, 2048), BF16),
            pltpu.VMEM((4, 2, 1024), F32),
            pltpu.VMEM((5, 8, 128), F32),
            pltpu.VMEM(rows + (2048,), BF16),
            pltpu.VMEM(rows + (2048,), BF16),
            pltpu.VMEM(rows + (1024,), BF16),
            pltpu.VMEM((128, 128), F32),
            pltpu.VMEM((512, 1), F32),
            pltpu.VMEM((512, 1), F32),
            pltpu.VMEM((512, 1), F32),
            pltpu.VMEM((8, 1024), F32),
            pltpu.VMEM((2, 1024), F32),
            pltpu.VMEM((4, 4, 32, 2048), BF16),
            pltpu.VMEM((4, 4, 32, 2048), BF16),
            *[pltpu.VMEM((2, 2, 32, 2048), BF16)] * 6,
            pltpu.VMEM((4, 32, 2048), BF16),
            pltpu.VMEM((4, 32, 2048), BF16),
            pltpu.VMEM((3, 32, 2048), BF16),
            pltpu.VMEM((3, 32, 2048), BF16),
            pltpu.VMEM((4, 32, 2048), BF16),
            pltpu.VMEM((4, 32, 2048), BF16),
        ]
        + halves_scratch(512)
        + halves_scratch(512)
        + halves_scratch(256)
        + [
            DMA((2, 4)), DMA((2, 4)),
            DMA((2, 4)), DMA((2, 4)),
            DMA((2,)), DMA((2,)),
            DMA((12,)), DMA((12,)),
            DMA((2, 4)), DMA((2, 4)),
            DMA((2, 4)), DMA((2, 4)),
            DMA((3, 26)), DMA((3, 26)),
            DMA((2,)),
        ],
        compiler_params=pltpu.CompilerParams(
            collective_id=1, has_side_effects=True, vmem_limit_bytes=60 << 20
        ),
        name="backward",
    )(*operands)


def attention_kernel(q_ref, g_ref, k_ref, v_ref, att_ref, qag_ref, kag_ref, vag_ref):
    scale = HSZ ** (-0.5)
    spots = []
    for h in range(q_ref.shape[1] // HSZ):
        lanes = slice(h * HSZ, (h + 1) * HSZ)
        for s in range(2):
            rows, keys = slice(s * SPAN, (s + 1) * SPAN), slice(s * 2 * NL, (s + 1) * 2 * NL)
            spots.append(((rows, lanes), (keys, lanes)))
    scores = [dot_nt(q_ref[r], k_ref[k]) * scale for r, k in spots]
    pgs = [dot_nt(g_ref[r], v_ref[k]) for r, k in spots]
    tops = [jnp.max(s, axis=-1, keepdims=True) for s in scores]
    es = [jnp.exp(s - m) for s, m in zip(scores, tops)]
    sums = [jnp.sum(e, axis=-1, keepdims=True) for e in es]
    fulls = [e / t for e, t in zip(es, sums)]
    weights = [f.astype(BF16) for f in fulls]
    dots = [jnp.sum(f * p, axis=-1, keepdims=True) for f, p in zip(fulls, pgs)]
    sgs = [(f * (p - d) * scale).astype(BF16) for f, p, d in zip(fulls, pgs, dots)]
    for (r, k), w in zip(spots, weights):
        att_ref[r] = dot_nn(w, v_ref[k]).astype(BF16)
    for (r, k), sg in zip(spots, sgs):
        qag_ref[r] = dot_nn(sg, k_ref[k]).astype(BF16)
    for (r, k), sg in zip(spots, sgs):
        kag_ref[k] = dot_tn(sg, q_ref[r]).astype(BF16)
    for (r, k), w in zip(spots, weights):
        vag_ref[k] = dot_tn(w, g_ref[r]).astype(BF16)


def attention(q, g, k, v):
    few = pl.BlockSpec((128, 256), lambda h: (0, h))
    many = pl.BlockSpec((512, 256), lambda h: (0, h))
    return pl.pallas_call(
        attention_kernel,
        grid=(8,),
        out_shape=(
            jax.ShapeDtypeStruct((128, 2048), BF16),
            jax.ShapeDtypeStruct((128, 2048), BF16),
            jax.ShapeDtypeStruct((512, 2048), BF16),
            jax.ShapeDtypeStruct((512, 2048), BF16),
        ),
        in_specs=[few, few, many, many],
        out_specs=(few, few, many, many),
        name="attention",
    )(q, g, k, v)


def shards(
    hidden, norm_gain, w_query, w_key, w_value, w_out, w_cond, enc_gain, store, neighbour_ids,
    out_grad,
):
    egain = jnp.pad(enc_gain.reshape(32, 28), ((0, 0), (0, 4))).reshape(1, PE)
    gain = norm_gain.reshape(1, 4096)
    (
        sq_all, summary, q, ag, keys, values, encoded, enc_in, normed_t, out_grad_t,
        gq, go, gc, gk, gv,
    ) = forward(
        neighbour_ids.reshape(1, 4), gain, hidden, out_grad, egain, store,
        w_query, w_out, w_cond, w_key, w_value,
    )
    att, qag, kag, vag = attention(q, ag, keys, values)
    layer_out, hidden_grad, qo, oo, co, kg, vg = backward(
        att, qag, kag, vag, encoded, enc_in, egain, hidden, out_grad,
        gain, normed_t, out_grad_t, summary, sq_all, gc,
        gq.reshape(4, 256, 2048), go.reshape(4, 256, 2048),
        gk.reshape(4, 256, 2048), gv.reshape(4, 256, 2048),
    )
    cond_grad = co.astype(F32).reshape(128, 8, 32)[:, :, :28].reshape(128, 224)
    return (
        layer_out,
        hidden_grad,
        qo.reshape(128, 512).astype(F32),
        kg[:28],
        vg[:28],
        oo.reshape(128, 512).T.astype(F32),
        cond_grad,
    )


def solution(mesh):
    placed = (
        P("dp", "enc"), P(), P("dp", "enc"), P("dp", "enc"), P("dp", "enc"), P("enc", "dp"),
        P("dp", "enc"), P(), P(("dp", "enc"), None, None), P(("dp", "enc")), P("dp", "enc"),
    )
    return jax.shard_map(
        shards,
        mesh=mesh,
        in_specs=placed,
        out_specs=(
            P("dp", "enc"), P("dp", "enc"), P("dp", "enc"), P("dp", "enc"), P("dp", "enc"),
            P("enc", "dp"), P("dp", "enc"),
        ),
        check_vma=False,
    )
```

```python
import functools

import jax
import jax.numpy as jnp
from jax import lax
from jax.experimental import pallas as pl
from jax.experimental.pallas import tpu as pltpu
from jax.sharding import PartitionSpec as P

MESH = pl.DeviceIdType.MESH
F32 = jnp.float32
BF16 = jnp.bfloat16
HSZ = 128
SPAN = 64
NL = 128
DE = 896
PE = 1024
EPS = 1e-05
ANY = pl.BlockSpec(memory_space=pl.ANY)
VM = pl.BlockSpec(memory_space=pltpu.VMEM)
DMA = pltpu.SemaphoreType.DMA


def place():
    d = lax.axis_index("dp")
    return d // 8, (d // 2) % 4, d % 2, lax.axis_index("enc")


def at(x, z, c, y):
    return ((x * 4 + z) * 2 + c, y)


def around(v, k):
    return (v + k) % 4


def remote(src, dst, send, recv, device):
    copy = pltpu.make_async_remote_copy(
        src, dst, send, recv, device_id=device, device_id_type=MESH
    )
    copy.start()
    return copy


def meet(peers, partner=None, has_partner=None):
    barrier = pltpu.get_barrier_semaphore()
    for peer in peers:
        pl.semaphore_signal(barrier, inc=1, device_id=peer, device_id_type=MESH)
    if partner is not None:

        @pl.when(has_partner)
        def _():
            pl.semaphore_signal(barrier, inc=1, device_id=partner, device_id_type=MESH)

        pl.semaphore_wait(barrier, jnp.where(has_partner, len(peers) + 1, len(peers)))
    else:
        pl.semaphore_wait(barrier, len(peers))


def sum_rows(out, terms, step=16):
    rows = out.shape[0]

    def body(i, carry):
        at_row = pl.ds(pl.multiple_of(i * step, step), step)
        total = terms[0][at_row].astype(F32)
        for t in terms[1:]:
            total = total + t[at_row].astype(F32)
        out[at_row] = total.astype(out.dtype)
        return carry

    lax.fori_loop(0, rows // step, body, 0)


def cols(i, n):
    return pl.ds(pl.multiple_of(i * n, n), n)


def pick_rows(ids_s, r):
    every = [ids_s[r, 0, k] for k in range(4)]
    owner = [(v // 8) % 4 for v in every]
    row = [v % 8 for v in every]
    rank = []
    for k in range(4):
        n = jnp.int32(0)
        for j in range(k):
            n = n + jnp.where(owner[j] == owner[k], 1, 0)
        rank.append(n)
    return owner, row, rank


class Plane:
    def __init__(self, put, line, cut, whole, axes, sems):
        self.put, self.line, self.cut, self.whole = put, line, cut, whole
        self.x, self.z, self.xp, self.zp, self.sib = axes
        self.s, self.r = sems
        self.one, self.two, self.on, self.last = [[], []], [[], []], [[], []], None

    def first(self):
        for h in range(2):
            src, dst, keep = self.put(h)
            for k in (2, 1, 3):
                peer = (self.zp if h else self.xp)[k - 1]
                self.one[h].append(remote(src, dst, self.s.at[h, k], self.r.at[h, k], peer))
            if keep is not None:
                copy = pltpu.make_async_copy(src, dst, self.s.at[h, 0])
                copy.start()
                copy.wait()

    def second(self):
        for h in range(2):
            for copy in self.one[h]:
                copy.wait_recv()
            block = self.line(h, self.x if h else self.z)
            for k in (1, 3):
                peer = (self.xp if h else self.zp)[k - 1]
                self.two[h].append(
                    remote(block, block, self.s.at[h, 3 + k], self.r.at[h, 3 + k], peer)
                )

    def relay(self):
        for h in range(2):
            place = self.x if h else self.z
            for j, k in ((0, 1), (1, 3)):
                self.two[h][j].wait_recv()
                block = self.cut(h, around(place, 4 - k), j)
                peer = (self.xp if h else self.zp)[k - 1]
                self.on[h].append(
                    remote(block, block, self.s.at[h, 7 + k], self.r.at[h, 7 + k], peer)
                )

    def swap(self):
        for copy in self.on[0] + self.on[1]:
            copy.wait_recv()
        self.last = remote(self.whole, self.whole, self.s.at[0, 5], self.r.at[0, 5], self.sib)

    def sent(self):
        every = self.one[0] + self.one[1] + self.two[0] + self.two[1]
        for copy in every + self.on[0] + self.on[1] + [self.last]:
            copy.wait_send()


class Sums:
    def __init__(self, p, bufs, y, right, left, sems):
        self.p, self.y, self.right, self.left = p, y, right, left
        self.far_a, self.far_b, self.from_left, self.from_right = bufs
        self.s, self.r = sems
        self.far, self.near, self.late = [], [], []

    def send(self, n, src, dst, peer):
        return remote(src, dst, self.s.at[n], self.r.at[n], peer)

    def first(self):
        p, y = self.p, self.y
        a, b = pl.ds(0, 64), pl.ds(64, 64)
        self.far = [
            self.send(0, p.at[around(y, 2), a], self.far_a, self.right),
            self.send(1, p.at[around(y, 2), b], self.far_b, self.left),
        ]
        self.near = [
            self.send(2, p.at[around(y, 1), b], self.from_left.at[b], self.right),
            self.send(3, p.at[around(y, 3), a], self.from_right.at[a], self.left),
        ]

    def second(self):
        p, y = self.p, self.y
        moves = (
            (0, self.far_a, around(y, 1), 0, self.from_left, self.right),
            (1, self.far_b, around(y, 3), 64, self.from_right, self.left),
        )
        for n, far, target, low, dst, peer in moves:
            self.far[n].wait_recv()

            def fold(i, carry, far=far, target=target, low=low):
                rows = pl.ds(pl.multiple_of(low + i * 16, 16), 16)
                more = far[pl.ds(pl.multiple_of(i * 16, 16), 16)].astype(F32)
                p[target, rows] = (p[target, rows].astype(F32) + more).astype(BF16)
                return carry

            lax.fori_loop(0, 4, fold, 0)
            half = pl.ds(low, 64)
            self.late.append(self.send(4 + n, p.at[target, half], dst.at[half], peer))

    def third(self, out):
        for copy in self.near + self.late:
            copy.wait_recv()
        sum_rows(out, [self.p.at[self.y], self.from_left, self.from_right])

    def sent(self):
        for copy in self.far + self.near + self.late:
            copy.wait_send()


def forward_kernel(
    ids_in, gain, xs, og_h, egain, store, wq, wo_in, wc_in, wk_in, wv_in,
    sq_all, sm, q, a, keys, values, enc_h, ein_h, nt_h, ogt_h, hq, ho, hc, hk, hv,
    ids_all, ids_s, out_rows, in_rows, tq, to, tc, yk, yv, gq, go, gc, gk, gv,
    normed, qp, ap, cp, q0, q1, q2, q3, a0, a1, a2, a3, rc,
    ids, sq, line_up, means, pick_cols, wo, wc, wk, wv,
    s_small, r_small, s_row, r_row, s_t, r_t, s_p, r_p, s_w, r_w, s_y, r_y, s_q, r_q, s_a, r_a,
    s_loc, s_out, og, enc, ein, nt, ogt,
):
    load = pltpu.make_async_copy(og_h, og, s_loc.at[1])
    load.start()
    x, z, c, y = place()
    yp = [at(x, z, c, around(y, k)) for k in (1, 2, 3)]
    xp = [at(around(x, k), z, c, y) for k in (1, 2, 3)]
    zp = [at(x, around(z, k), c, y) for k in (1, 2, 3)]
    sib = at(x, z, 1 - c, y)
    partner = at(y, z, c, x)
    axes = (x, z, xp, zp, sib)
    meet(yp + xp + zp + [sib], partner, x != y)

    moves = ((wq, tq), (wo, to), (wc, tc))

    def cross(n):
        w, t = moves[n]

        @pl.when(x != y)
        def _():
            remote(w, t, s_t.at[n], r_t.at[n], partner)

        @pl.when(x == y)
        def _():
            pltpu.make_async_copy(w, t, r_t.at[n]).start()

    def arrived(n):
        w, t = moves[n]
        pltpu.make_async_copy(w, t, r_t.at[n]).wait()

    cross(0)
    ids[...] = jnp.zeros_like(ids)
    ids[0:1, 0:4] = ids_in[...]
    small = []
    for k in (1, 2, 3):
        small.append(remote(ids, ids_all.at[y], s_small.at[0, k], r_small.at[0, k], yp[k - 1]))
    ids_all[y] = ids[...]
    line_up[...] = jnp.zeros_like(line_up)
    for j in range(4):
        part = xs[128 * j : 128 * (j + 1)].astype(F32)
        line_up[:, j : j + 1] = jnp.sum(part * part, axis=-1, keepdims=True)
        for i in range(2):
            row = jnp.sum(part[64 * i : 64 * i + 64], axis=0, keepdims=True) / SPAN
            means[2 * j + i : 2 * j + i + 1] = row
    sm[...] = means[...].astype(BF16)
    sq[...] = line_up[...].T[:8]
    sq_all[y] = sq[...]
    for k in (1, 2, 3):
        small.append(remote(sq, sq_all.at[y], s_small.at[1, k], r_small.at[1, k], yp[k - 1]))
    wo[...] = wo_in[...].T
    spot = lax.broadcasted_iota(jnp.int32, (1, PE), 1)
    source = jnp.where(spot % 32 < 28, spot // 32 * 28 + spot % 32, -1)
    for i in range(7):
        row = lax.broadcasted_iota(jnp.int32, (128, PE), 0) + 128 * i
        pick_cols[128 * i : 128 * (i + 1)] = jnp.where(row == source, 1.0, 0.0).astype(BF16)
    wc[...] = dot_nn(wc_in[...], pick_cols[0:224, 0:256]).astype(BF16)
    for w, v in ((wk, wk_in), (wv, wv_in)):
        w[...] = jnp.zeros_like(w)
        w[0:28] = v[...]
    for copy in small[:3]:
        copy.wait_recv()
    to_s = pltpu.make_async_copy(ids_all, ids_s, s_loc.at[0])
    to_s.start()
    to_s.wait()

    row_copies = []
    for k in (2, 1, 3, 0):
        owner, row, rank = pick_rows(ids_s, around(y, k))
        for n in range(2):
            pick = jnp.int32(0)
            for j in range(4):
                pick = pick + jnp.where((owner[j] == y) & (rank[j] == n), row[j], 0)
            if k:
                out_rows[k, n] = store[pick]
            else:
                in_rows[y, n] = store[pick]
        if k:
            row_copies.append(
                remote(out_rows.at[k], in_rows.at[y], s_row.at[k], r_row.at[k], yp[k - 1])
            )

    def weight(n, t, g, w):
        def put(h):
            rows = pl.ds(64 * h, 64)
            return t.at[rows], g.at[z, c, rows, cols(x, w)], True

        def line(h, i):
            if h:
                return g.at[:, c, pl.ds(64, 64), cols(i, w)]
            return g.at[i, c, pl.ds(0, 64)]

        def cut(h, i, j):
            if h:
                return g.at[:, c, pl.ds(64 + 32 * j, 32), cols(i, w)]
            return g.at[i, c, pl.ds(32 * j, 32)]

        return Plane(put, line, cut, g.at[:, c], axes, (s_p.at[n], r_p.at[n]))

    pq, po, pc = weight(0, tq, gq, 512), weight(1, to, go, 512), weight(2, tc, gc, 256)

    def kv_put(h):
        return (yv, gv.at[x, z, c], True) if h else (yk, gk.at[x, z, c], True)

    def kv_line(h, i):
        return gv.at[i, :, c] if h else gk.at[:, i, c]

    def kv_cut(h, i, j):
        if h:
            return gv.at[i, pl.ds(2 * j, 2), c]
        return gk.at[pl.ds(2 * j, 2), i, c]

    pk = KeyPlane(
        kv_put, kv_line, kv_cut, (gk.at[:, :, c], gv.at[:, :, c]), axes, (s_p.at[3], r_p.at[3])
    )
    rq = Sums(qp, (q0, q1, q2, q3), y, yp[0], yp[2], (s_q, r_q))
    ra = Sums(ap, (a0, a1, a2, a3), y, yp[0], yp[2], (s_a, r_a))

    arrived(0)
    cross(2)
    cross(1)
    pq.first()
    across = []
    for n, (w, t) in enumerate(((wk, yk), (wv, yv))):
        for k in (2, 1, 3):
            across.append(
                remote(w, t.at[:, cols(y, 512)], s_w.at[n, k], r_w.at[n, k], yp[k - 1])
            )
        t[:, cols(y, 512)] = w[...]
    pq.second()
    arrived(2)
    pc.first()
    for copy in small[3:]:
        copy.wait_recv()
    total = sq_all[0] + sq_all[1] + sq_all[2] + sq_all[3]
    rstd = lax.rsqrt(total / 4096 + EPS).T
    for j in range(4):
        rows = slice(128 * j, 128 * (j + 1))
        normed[rows] = (xs[rows].astype(F32) * rstd[:, j : j + 1] * gain[:, cols(y, 1024)]).astype(BF16)
    arrived(1)
    po.first()
    pq.relay()
    pc.second()
    po.second()
    pq.swap()
    outs = []

    def keep(n, g, h):
        copy = pltpu.make_async_copy(g, h, s_out.at[n])
        copy.start()
        outs.append(copy)

    def product(act, g, put):
        def tile(i, carry):
            lanes = cols(i, 256)
            put(lanes, dot_nn(act[...], g[..., lanes].reshape(1024, 256)).astype(BF16))
            return carry

        lax.fori_loop(0, 8, tile, 0)

    def into(p):
        def put(lanes, value):
            p[:, :, lanes] = value.reshape(4, 128, 256)

        return put

    pq.last.wait_recv()
    product(normed, gq, into(qp))
    rq.first()
    keep(0, gq, hq)
    pc.relay()
    po.relay()
    for copy in across:
        copy.wait_recv()
    pk.first()
    pc.swap()
    pc.last.wait_recv()
    keep(2, gc, hc)
    for i in range(4):
        lanes = slice(256 * i, 256 * (i + 1))
        w = gc[:, :, :, lanes].reshape(1024, 256)
        cp[:, lanes] = dot_nn(sm[...], w)
    for j in range(4):
        rc[j + 4] = cp[2 * j : 2 * j + 2]
    parts = []
    for k in (2, 1, 3):
        parts.append(
            remote(rc.at[4 + around(y, k)], rc.at[k], s_y.at[k], r_y.at[k], yp[k - 1])
        )
    rq.second()
    po.swap()
    pk.second()
    po.last.wait_recv()
    load.wait()
    product(og, go, into(ap))
    ra.first()
    keep(1, go, ho)
    for copy in row_copies:
        copy.wait_recv()
    owner, row, rank = pick_rows(ids_s, y)
    for k in range(4):
        rows = slice(128 * k, 128 * (k + 1))
        ein[rows] = dot_nn(in_rows[owner[k], jnp.minimum(rank[k], 1)], pick_cols[...])
    pk.relay()
    for copy in parts:
        copy.wait_recv()
    cond = (rc[4 + y] + rc[1] + rc[2] + rc[3]).astype(BF16).astype(F32)
    for k in range(4):
        rows = slice(128 * k, 128 * (k + 1))
        row = ein[rows] + cond[k // 2 : k // 2 + 1]
        ein[rows] = row
        scale = lax.rsqrt(jnp.sum(row * row, axis=-1, keepdims=True) / DE + EPS)
        enc[rows] = (row * scale * egain[...]).astype(BF16)
    keep(5, enc, enc_h)
    keep(6, ein, ein_h)
    ra.second()
    pk.swap()
    for j in range(4):
        rows = slice(128 * j, 128 * (j + 1))
        nt[:, rows] = normed[rows].T
        ogt[:, rows] = og[rows].T
    keep(7, nt, nt_h)
    keep(8, ogt, ogt_h)
    rq.third(q)
    for n, (g, h, out) in enumerate(((gk, hk, keys), (gv, hv, values))):
        pk.last[n].wait_recv()
        keep(3 + n, g, h)

        def put(lanes, value, out=out):
            out[:, lanes] = value

        product(enc, g, put)
    ra.third(a)
    for copy in outs:
        copy.wait()
    for copy in small + across + row_copies + parts:
        copy.wait_send()
    for plane in (pq, po, pc, pk, rq, ra):
        plane.sent()

    @pl.when(x != y)
    def _():
        for n, (w, t) in enumerate(moves):
            pltpu.make_async_copy(w, t, s_t.at[n]).wait()


class KeyPlane(Plane):
    def swap(self):
        for copy in self.on[0] + self.on[1]:
            copy.wait_recv()
        self.last = [
            remote(ref, ref, self.s.at[n, 5], self.r.at[n, 5], self.sib)
            for n, ref in enumerate(self.whole)
        ]

    def sent(self):
        every = self.one[0] + self.one[1] + self.two[0] + self.two[1]
        for copy in every + self.on[0] + self.on[1] + self.last:
            copy.wait_send()


def forward(*operands):
    wide, slim, keys = (4, 2, 128, 2048), (4, 2, 128, 1024), (4, 4, 2, 32, 2048)
    shape = jax.ShapeDtypeStruct
    halves = [
        pltpu.VMEM((64, 2048), BF16),
        pltpu.VMEM((64, 2048), BF16),
        pltpu.VMEM((128, 2048), BF16),
        pltpu.VMEM((128, 2048), BF16),
    ]
    return pl.pallas_call(
        forward_kernel,
        out_shape=(
            shape((4, 8, 128), F32),
            shape((8, 1024), BF16),
            shape((128, 2048), BF16),
            shape((128, 2048), BF16),
            shape((512, 2048), BF16),
            shape((512, 2048), BF16),
            shape((512, PE), BF16),
            shape((512, PE), F32),
            shape((1024, 512), BF16),
            shape((1024, 512), BF16),
            shape(wide, BF16),
            shape(wide, BF16),
            shape(slim, BF16),
            shape(keys, BF16),
            shape(keys, BF16),
        ),
        in_specs=[VM] * 3 + [ANY] + [VM] * 7,
        out_specs=(VM,) * 6 + (ANY,) * 9,
        scratch_shapes=[
            pltpu.VMEM((4, 8, 128), jnp.int32),
            pltpu.SMEM((4, 8, 128), jnp.int32),
            pltpu.VMEM((4, 2, NL, DE), BF16),
            pltpu.VMEM((4, 2, NL, DE), BF16),
            pltpu.VMEM((128, 512), BF16),
            pltpu.VMEM((128, 512), BF16),
            pltpu.VMEM((128, 256), BF16),
            pltpu.VMEM((32, 2048), BF16),
            pltpu.VMEM((32, 2048), BF16),
            pltpu.VMEM(wide, BF16),
            pltpu.VMEM(wide, BF16),
            pltpu.VMEM(slim, BF16),
            pltpu.VMEM(keys, BF16),
            pltpu.VMEM(keys, BF16),
            pltpu.VMEM((512, 1024), BF16),
            pltpu.VMEM((4, 128, 2048), BF16),
            pltpu.VMEM((4, 128, 2048), BF16),
            pltpu.VMEM((8, 1024), F32),
        ]
        + halves
        + halves
        + [
            pltpu.VMEM((8, 2, 1024), F32),
            pltpu.VMEM((8, 128), jnp.int32),
            pltpu.VMEM((8, 128), F32),
            pltpu.VMEM((128, 128), F32),
            pltpu.VMEM((8, 1024), F32),
            pltpu.VMEM((DE, PE), BF16),
            pltpu.VMEM((128, 512), BF16),
            pltpu.VMEM((128, 256), BF16),
            pltpu.VMEM((32, 512), BF16),
            pltpu.VMEM((32, 512), BF16),
            DMA((2, 4)), DMA((2, 4)),
            DMA((4,)), DMA((4,)),
            DMA((3,)), DMA((3,)),
            DMA((4, 2, 11)), DMA((4, 2, 11)),
            DMA((2, 4)), DMA((2, 4)),
            DMA((4,)), DMA((4,)),
            DMA((6,)), DMA((6,)),
            DMA((6,)), DMA((6,)),
            DMA((2,)),
            DMA((9,)),
            pltpu.VMEM((512, 1024), BF16),
            pltpu.VMEM((512, PE), BF16),
            pltpu.VMEM((512, PE), F32),
            pltpu.VMEM((1024, 512), BF16),
            pltpu.VMEM((1024, 512), BF16),
        ],
        compiler_params=pltpu.CompilerParams(
            collective_id=0, has_side_effects=True, vmem_limit_bytes=58 << 20
        ),
        name="forward",
    )(*operands)


def dot_nn(a, b):
    return jnp.dot(a, b, preferred_element_type=F32)


def dot_nt(a, b):
    return lax.dot_general(a, b, (((1,), (1,)), ((), ())), preferred_element_type=F32)


def dot_tn(a, b):
    return lax.dot_general(a, b, (((0,), (0,)), ((), ())), preferred_element_type=F32)


class Around:
    def __init__(self, half, bufs, place, right, left, sems, base):
        self.half, self.place, self.right, self.left = half, place, right, left
        self.far, self.from_left, self.from_right = bufs
        self.s, self.r, self.base = sems[0], sems[1], base
        self.sends = []

    def send(self, n, src, dst, peer):
        n = self.base + n
        self.sends.append(remote(src, dst, self.s.at[n], self.r.at[n], peer))

    def first(self):
        half, p = self.half, self.place
        self.send(0, half(around(p, 2), 0), self.far.at[0], self.right)
        self.send(1, half(around(p, 2), 1), self.far.at[1], self.left)
        self.send(2, half(around(p, 1), 1), self.from_left.at[1], self.right)
        self.send(3, half(around(p, 3), 0), self.from_right.at[0], self.left)

    def mid(self):
        moves = ((0, 1, self.from_left, self.right), (1, 3, self.from_right, self.left))
        for n, k, dst, peer in moves:
            self.sends[n].wait_recv()
            own = self.half(around(self.place, k), n)
            own[...] = (own[...].astype(F32) + self.far[n].astype(F32)).astype(BF16)
            self.send(4 + n, own, dst.at[n], peer)

    def here(self):
        for copy in self.sends[2:]:
            copy.wait_recv()

    def total(self, i):
        own = self.half(self.place, i)[...].astype(F32)
        return (own + self.from_left[i].astype(F32) + self.from_right[i].astype(F32)).astype(BF16)

    def sent(self):
        for copy in self.sends:
            copy.wait_send()


class Halves:
    def __init__(self, p, bufs, out, w, spots, sems):
        self.p, self.out, self.w = p, out, w
        self.b, fa, la, ra, fb, lb, rb, self.wa, self.wb, self.va, self.vb, self.f = bufs
        self.x, self.z, self.c, self.y, self.xp, self.zp, self.sib = spots
        self.s, self.r = sems
        self.two, self.swapped = [[], []], None
        b = self.b
        self.ringa = Around(
            lambda t, i: b.at[t, 0, i], (fa, la, ra), self.z, self.zp[0], self.zp[2], sems, 14
        )
        self.ringb = Around(
            lambda t, i: b.at[:, 1, i, :, cols(t, w)], (fb, lb, rb), self.x, self.xp[0],
            self.xp[2], sems, 20,
        )

    def swap(self):
        src = self.p.at[:, pl.ds(2 * (1 - self.c), 2)]
        self.swapped = remote(src, self.b, self.s.at[0], self.r.at[0], self.sib)

    def first(self):
        self.swapped.wait_recv()
        p, b, c = self.p, self.b, self.c

        def fold(i, carry):
            j, h, k = i // 4, (i // 2) % 2, i % 2
            b[j, h, k] = (p[j, 2 * c + h, k].astype(F32) + b[j, h, k].astype(F32)).astype(BF16)
            return carry

        lax.fori_loop(0, 16, fold, 0)
        self.ringa.first()
        self.ringb.first()

    def mid(self):
        self.ringa.mid()
        self.ringb.mid()

    def second(self):
        wa, wb = self.wa, self.wb
        self.ringa.here()
        for i in range(2):
            wa[i] = self.ringa.total(i)
        for k in (2, 1, 3):
            lanes = cols(around(self.x, k), self.w)
            self.two[0].append(
                remote(wa.at[:, :, lanes], self.va.at[k - 1], self.s.at[6 + k], self.r.at[6 + k], self.xp[k - 1])
            )
        self.ringb.here()
        for i in range(2):
            wb[:, i] = self.ringb.total(i)
        for k in (2, 1, 3):
            self.two[1].append(
                remote(wb.at[around(self.z, k)], self.vb.at[k - 1], self.s.at[9 + k], self.r.at[9 + k], self.zp[k - 1])
            )

    def third(self):
        x, y, z, f, va, vb = self.x, self.y, self.z, self.f, self.va, self.vb
        for copy in self.two[0] + self.two[1]:
            copy.wait_recv()
        for i in range(2):
            f[0, i] = (
                self.wa[i, :, cols(x, self.w)].astype(F32) + va[0, i].astype(F32)
                + va[1, i].astype(F32) + va[2, i].astype(F32)
            ).astype(BF16)
            f[1, i] = (
                self.wb[z, i].astype(F32) + vb[0, i].astype(F32)
                + vb[1, i].astype(F32) + vb[2, i].astype(F32)
            ).astype(BF16)

        @pl.when(x != y)
        def _():
            remote(f, self.out, self.s.at[13], self.r.at[13], at(y, z, self.c, x))

        @pl.when(x == y)
        def _():
            pltpu.make_async_copy(f, self.out, self.r.at[13]).start()

    def end(self):
        pltpu.make_async_copy(self.f, self.out, self.r.at[13]).wait()
        for copy in self.two[0] + self.two[1]:
            copy.wait_send()
        self.ringa.sent()
        self.ringb.sent()

        @pl.when(self.x != self.y)
        def _():
            pltpu.make_async_copy(self.f, self.out, self.s.at[13]).wait()


def backward_kernel(
    att, qag, kag, vag, enc, ein_h, egain, xs_h, og_h, gain, nt_h, ogt_h, sm, sq, gc_h,
    gq, go, gk, gv,
    layer, hidden, qo, oo, co, ko, vo,
    tile, et, att_all, qag_all, cd_all, rs_all, p1, p2, p3, line_up, erstd, emean, rsum, sgrad, slot,
    *scratch,
):
    b_k, b_v, ak, lk, rk, av, lv, rv, w_k, w_v, x_k, x_v, f_k, f_v = scratch[:14]
    bq, bo, bc = scratch[14:26], scratch[26:38], scratch[38:50]
    s_y, r_y, s_d, r_d, s_c, r_c, s_1, r_1, s_2, r_2, s_3, r_3, s_h, r_h, s_tile = scratch[50:65]
    ein, xs, og, ogt, gc, s_in = scratch[65:]
    nt = et
    loads = [
        pltpu.make_async_copy(h, v, s_in.at[n])
        for n, (h, v) in enumerate(
            ((ein_h, ein), (xs_h, xs), (og_h, og), (ogt_h, ogt), (gc_h, gc), (nt_h, nt))
        )
    ]
    for copy in loads[:5]:
        copy.start()
    x, z, c, y = place()
    yp = [at(x, z, c, around(y, k)) for k in (1, 2, 3)]
    xp = [at(around(x, k), z, c, y) for k in (1, 2, 3)]
    zp = [at(x, around(z, k), c, y) for k in (1, 2, 3)]
    sib = at(x, z, 1 - c, y)
    meet(yp + xp + zp + [sib], at(y, z, c, x), x != y)
    spots = (x, z, c, y, xp, zp, sib)
    rq = Halves(p1, bq, qo, 512, spots, (s_h.at[0], r_h.at[0]))
    ro = Halves(p2, bo, oo, 512, spots, (s_h.at[1], r_h.at[1]))
    rc = Halves(p3, bc, co, 256, spots, (s_h.at[2], r_h.at[2]))

    ring = []
    for n, (src, dst) in enumerate(((att, att_all), (qag, qag_all))):
        for j, k in ((0, 1), (1, 3)):
            ring.append(remote(src, dst.at[y], s_y.at[n, j], r_y.at[n, j], yp[k - 1]))
    et[...] = enc[...].T

    def product(left, right, p, width=256):
        def step(i, carry):
            lanes = cols(i, width)
            r = right[..., lanes].reshape(left.shape[1], width)
            p[..., lanes] = dot_nn(left[...], r).astype(BF16).reshape(4, 4, 2, 32, width)
            return carry

        lax.fori_loop(0, p.shape[-1] // width, step, 0)

    swaps = []
    for n, (act, p, b) in enumerate(((kag, p1, b_k), (vag, p2, b_v))):
        product(et, act, p)
        swaps.append(remote(p.at[:, :, 1 - c], b, s_c.at[n], r_c.at[n], sib))
    loads[5].start()
    att_all[y] = att[...]
    qag_all[y] = qag[...]

    passed = []

    def relay(n, dst):
        for j, k in ((0, 1), (1, 3)):
            ring[2 * n + j].wait_recv()
            block = dst.at[around(y, 4 - k), pl.ds(64 * j, 64)]
            passed.append(remote(block, block, s_y.at[n, 2 + j], r_y.at[n, 2 + j], yp[k - 1]))

    def pair(i):
        return pl.ds(2 * i, 2)

    kring = Around(
        lambda t, i: b_k.at[pair(i), t], (ak, lk, rk), z, zp[0], zp[2], (s_1, r_1), 0
    )
    vring = Around(
        lambda t, i: b_v.at[t, pair(i)], (av, lv, rv), x, xp[0], xp[2], (s_1, r_1), 6
    )
    rings = (kring, vring)
    for n, (p, b) in enumerate(((p1, b_k), (p2, b_v))):
        swaps[n].wait_recv()

        def fold(i, carry, p=p, b=b):
            b[i // 4, i % 4] = (
                p[i // 4, i % 4, c].astype(F32) + b[i // 4, i % 4].astype(F32)
            ).astype(BF16)
            return carry

        lax.fori_loop(0, 16, fold, 0)
        rings[n].first()
    for copy in swaps:
        copy.wait_send()
    relay(0, att_all)

    def fetch(h, i, j):
        return pltpu.make_async_copy(h.at[i], tile.at[j], s_tile.at[j])

    for copy in loads:
        copy.wait()
    ee = ein[...]
    erstd[...] = lax.rsqrt(jnp.sum(ee * ee, axis=-1, keepdims=True) / DE + EPS)
    emean[...] = jnp.zeros_like(emean)
    fetch(gk, 0, 0).start()
    fetch(gv, 0, 1).start()

    def encoder(i, carry):
        lanes = cols(i, 256)
        fetch(gk, i, 0).wait()
        part = dot_nt(kag[...], tile[0])

        @pl.when(i < 3)
        def _():
            fetch(gk, i + 1, 0).start()

        fetch(gv, i, 1).wait()
        part = part + dot_nt(vag[...], tile[1])

        @pl.when(i < 3)
        def _():
            fetch(gv, i + 1, 1).start()

        ey = part.astype(BF16).astype(F32) * egain[:, lanes]
        emean[...] += jnp.sum(ein[:, lanes] * ey, axis=-1, keepdims=True)
        ry = ey * erstd[...]
        for s in range(2):
            slot[s : s + 1, lanes] = jnp.sum(ry[256 * s : 256 * s + 256], axis=0, keepdims=True)
        return carry

    lax.fori_loop(0, 4, encoder, 0)
    relay(1, qag_all)
    kring.mid()
    vring.mid()
    for copy in passed[:2]:
        copy.wait_recv()
    product(ogt, att_all, p2)
    ro.swap()
    for s in range(2):
        rows = slice(256 * s, 256 * s + 256)
        weight = erstd[rows] ** 3 * (emean[rows] / DE)
        row = slot[s : s + 1] - jnp.sum(ein[rows] * weight, axis=0, keepdims=True)
        slot[s : s + 1] = row.astype(BF16).astype(F32)
    cd_all[y] = slot[...]
    small = [remote(slot, cd_all.at[y], s_d.at[0, k], r_d.at[0, k], yp[k - 1]) for k in (1, 2, 3)]


    def streamed(h, act, use):
        fetch(h, 0, 0).start()

        def step(i, carry):
            fetch(h, i, i % 2).wait()

            @pl.when(i < 3)
            def _():
                fetch(h, i + 1, (i + 1) % 2).start()

            use(cols(i, 256), dot_nt(act[...].reshape(512, 2048), tile[i % 2]))
            return carry

        lax.fori_loop(0, 4, step, 0)

    ro.first()
    for copy in passed[2:]:
        copy.wait_recv()
    product(nt, qag_all, p1)
    rq.swap()
    sent2 = []
    for n, (w, v) in enumerate(((w_k, x_k), (w_v, x_v))):
        rings[n].here()
        for i in range(2):
            w[pair(i)] = rings[n].total(i)
        for k in (2, 1, 3):
            if n:
                src, peer = w.at[around(z, k)], zp[k - 1]
            else:
                src, peer = w.at[around(x, k)], xp[k - 1]
            sent2.append(remote(src, v.at[k - 1], s_2.at[n, k], r_2.at[n, k], peer))
    ro.mid()

    def add_out(lanes, value):
        layer[:, lanes] = (xs[:, lanes].astype(F32) + value).astype(BF16)

    streamed(go, att_all, add_out)
    rq.first()
    for copy in small:
        copy.wait_recv()
    cd = cd_all[...].reshape(8, 1024).astype(BF16)
    for i in range(4):
        lanes = slice(256 * i, 256 * i + 256)
        p3[..., lanes] = dot_tn(sm[...], cd[:, lanes]).astype(BF16).reshape(4, 4, 2, 32, 256)
    rc.swap()
    ro.second()
    sent3 = []
    for n, (w, v, f) in enumerate(((w_k, x_k, f_k), (w_v, x_v, f_v))):
        for copy in sent2[3 * n : 3 * n + 3]:
            copy.wait_recv()
        own = w[z] if n else w[x]
        f[0] = (
            own.astype(F32) + v[0].astype(F32) + v[1].astype(F32) + v[2].astype(F32)
        ).astype(BF16)
        for k in (2, 1, 3):
            src, dst = f.at[0, :, cols(around(y, k), 512)], f.at[k, :, pl.ds(0, 512)]
            sent3.append(remote(src, dst, s_3.at[n, k], r_3.at[n, k], yp[k - 1]))
    rq.mid()
    rc.first()
    for i in range(4):
        sgrad[:, 256 * i : 256 * i + 256] = dot_nt(cd, gc[i].reshape(256, 1024)) / SPAN
    rsum[...] = jnp.zeros_like(rsum)

    def add_scaled(lanes, value):
        scaled = value * gain[:, pl.ds(pl.multiple_of(y * 1024 + lanes.start, 256), 256)]
        hidden[:, lanes] = scaled
        rsum[...] += jnp.sum(xs[:, lanes].astype(F32) * scaled, axis=-1, keepdims=True)

    streamed(gq, qag_all, add_scaled)
    line_up[...] = jnp.zeros_like(line_up)
    for j in range(4):
        line_up[:, j : j + 1] = rsum[128 * j : 128 * j + 128]
    rs_all[4] = line_up[...].T[:8]
    for k in (1, 2, 3):
        small.append(
            remote(rs_all.at[4], rs_all.at[y], s_d.at[1, k], r_d.at[1, k], yp[k - 1])
        )
    rs_all[y] = rs_all[4]
    ro.third()
    rq.second()
    rc.mid()
    for n, (out, f) in enumerate(((ko, f_k), (vo, f_v))):
        for copy in sent3[3 * n : 3 * n + 3]:
            copy.wait_recv()
        out[...] = (
            f[0, :, cols(y, 512)].astype(F32)
            + f[1, :, pl.ds(0, 512)].astype(F32)
            + f[2, :, pl.ds(0, 512)].astype(F32)
            + f[3, :, pl.ds(0, 512)].astype(F32)
        )
    rq.third()
    rc.second()
    for copy in small[3:]:
        copy.wait_recv()
    total = rs_all[0] + rs_all[1] + rs_all[2] + rs_all[3]
    mean = (total / 4096).T
    rstd = lax.rsqrt((sq[0] + sq[1] + sq[2] + sq[3]) / 4096 + EPS).T
    for s in range(8):
        rows, half, j = slice(64 * s, 64 * s + 64), slice(64 * (s % 2), 64 * (s % 2) + 64), s // 2
        r, m = rstd[half, j : j + 1], mean[half, j : j + 1]
        hidden[rows] = (
            og[rows].astype(F32)
            + (r * hidden[rows] - xs[rows].astype(F32) * (r * r * r * m))
            + sgrad[s : s + 1]
        )
    rc.third()
    for r in (ro, rq, rc):
        r.swapped.wait_send()
        r.end()
    for r in rings:
        r.sent()
    for copy in small + ring + passed + sent2 + sent3:
        copy.wait_send()


def halves_scratch(w):
    return [
        pltpu.VMEM((4, 2, 2, 32, 4 * w), BF16),
        *[pltpu.VMEM((2, 32, 4 * w), BF16)] * 3,
        *[pltpu.VMEM((2, 4, 32, w), BF16)] * 3,
        pltpu.VMEM((2, 32, 4 * w), BF16),
        pltpu.VMEM((4, 2, 32, w), BF16),
        pltpu.VMEM((3, 2, 32, w), BF16),
        pltpu.VMEM((3, 2, 32, w), BF16),
        pltpu.VMEM((2, 2, 32, w), BF16),
    ]


def backward(*operands):
    shape = jax.ShapeDtypeStruct
    rows = (4, 4, 2, 32)
    return pl.pallas_call(
        backward_kernel,
        out_shape=(
            shape((512, 1024), BF16),
            shape((512, 1024), F32),
            shape((2, 2, 32, 512), BF16),
            shape((2, 2, 32, 512), BF16),
            shape((2, 2, 32, 256), BF16),
            shape((32, 512), F32),
            shape((32, 512), F32),
        ),
        in_specs=[VM] * 5 + [ANY, VM, ANY, ANY, VM, ANY, ANY, VM, VM] + [ANY] * 5,
        out_specs=(VM,) * 7,
        scratch_shapes=[
            pltpu.VMEM((2, 256, 2048), BF16),
            pltpu.VMEM((1024, 512), BF16),
            pltpu.VMEM((4, 128, 2048), BF16),
            pltpu.VMEM((4, 128, 2048), BF16),
            pltpu.VMEM((4, 2, 1024), F32),
            pltpu.VMEM((5, 8, 128), F32),
            pltpu.VMEM(rows + (2048,), BF16),
            pltpu.VMEM(rows + (2048,), BF16),
            pltpu.VMEM(rows + (1024,), BF16),
            pltpu.VMEM((128, 128), F32),
            pltpu.VMEM((512, 1), F32),
            pltpu.VMEM((512, 1), F32),
            pltpu.VMEM((512, 1), F32),
            pltpu.VMEM((8, 1024), F32),
            pltpu.VMEM((2, 1024), F32),
            pltpu.VMEM((4, 4, 32, 2048), BF16),
            pltpu.VMEM((4, 4, 32, 2048), BF16),
            *[pltpu.VMEM((2, 2, 32, 2048), BF16)] * 6,
            pltpu.VMEM((4, 32, 2048), BF16),
            pltpu.VMEM((4, 32, 2048), BF16),
            pltpu.VMEM((3, 32, 2048), BF16),
            pltpu.VMEM((3, 32, 2048), BF16),
            pltpu.VMEM((4, 32, 2048), BF16),
            pltpu.VMEM((4, 32, 2048), BF16),
        ]
        + halves_scratch(512)
        + halves_scratch(512)
        + halves_scratch(256)
        + [
            DMA((2, 4)), DMA((2, 4)),
            DMA((2, 4)), DMA((2, 4)),
            DMA((2,)), DMA((2,)),
            DMA((12,)), DMA((12,)),
            DMA((2, 4)), DMA((2, 4)),
            DMA((2, 4)), DMA((2, 4)),
            DMA((3, 26)), DMA((3, 26)),
            DMA((2,)),
            pltpu.VMEM((512, PE), F32),
            pltpu.VMEM((512, 1024), BF16),
            pltpu.VMEM((512, 1024), BF16),
            pltpu.VMEM((1024, 512), BF16),
            pltpu.VMEM((4, 2, 128, 1024), BF16),
            DMA((6,)),
        ],
        compiler_params=pltpu.CompilerParams(
            collective_id=1, has_side_effects=True, vmem_limit_bytes=60 << 20
        ),
        name="backward",
    )(*operands)


def attention_kernel(q_ref, g_ref, k_ref, v_ref, att_ref, qag_ref, kag_ref, vag_ref):
    scale = HSZ ** (-0.5)
    spots = []
    for h in range(q_ref.shape[1] // HSZ):
        lanes = slice(h * HSZ, (h + 1) * HSZ)
        for s in range(2):
            rows, keys = slice(s * SPAN, (s + 1) * SPAN), slice(s * 2 * NL, (s + 1) * 2 * NL)
            spots.append(((rows, lanes), (keys, lanes)))
    scores = [dot_nt(q_ref[r], k_ref[k]) * scale for r, k in spots]
    pgs = [dot_nt(g_ref[r], v_ref[k]) for r, k in spots]
    tops = [jnp.max(s, axis=-1, keepdims=True) for s in scores]
    es = [jnp.exp(s - m) for s, m in zip(scores, tops)]
    sums = [jnp.sum(e, axis=-1, keepdims=True) for e in es]
    fulls = [e / t for e, t in zip(es, sums)]
    weights = [f.astype(BF16) for f in fulls]
    dots = [jnp.sum(f * p, axis=-1, keepdims=True) for f, p in zip(fulls, pgs)]
    sgs = [(f * (p - d) * scale).astype(BF16) for f, p, d in zip(fulls, pgs, dots)]
    for (r, k), w in zip(spots, weights):
        att_ref[r] = dot_nn(w, v_ref[k]).astype(BF16)
    for (r, k), sg in zip(spots, sgs):
        qag_ref[r] = dot_nn(sg, k_ref[k]).astype(BF16)
    for (r, k), sg in zip(spots, sgs):
        kag_ref[k] = dot_tn(sg, q_ref[r]).astype(BF16)
    for (r, k), w in zip(spots, weights):
        vag_ref[k] = dot_tn(w, g_ref[r]).astype(BF16)


def attention(q, g, k, v):
    few = pl.BlockSpec((128, 256), lambda h: (0, h))
    many = pl.BlockSpec((512, 256), lambda h: (0, h))
    return pl.pallas_call(
        attention_kernel,
        grid=(8,),
        out_shape=(
            jax.ShapeDtypeStruct((128, 2048), BF16),
            jax.ShapeDtypeStruct((128, 2048), BF16),
            jax.ShapeDtypeStruct((512, 2048), BF16),
            jax.ShapeDtypeStruct((512, 2048), BF16),
        ),
        in_specs=[few, few, many, many],
        out_specs=(few, few, many, many),
        name="attention",
    )(q, g, k, v)


def shards(
    hidden, norm_gain, w_query, w_key, w_value, w_out, w_cond, enc_gain, store, neighbour_ids,
    out_grad,
):
    egain = jnp.pad(enc_gain.reshape(32, 28), ((0, 0), (0, 4))).reshape(1, PE)
    gain = norm_gain.reshape(1, 4096)
    (
        sq_all, summary, q, ag, keys, values, encoded, enc_in, normed_t, out_grad_t,
        gq, go, gc, gk, gv,
    ) = forward(
        neighbour_ids.reshape(1, 4), gain, hidden, out_grad, egain, store,
        w_query, w_out, w_cond, w_key, w_value,
    )
    att, qag, kag, vag = attention(q, ag, keys, values)
    layer_out, hidden_grad, qo, oo, co, kg, vg = backward(
        att, qag, kag, vag, encoded, enc_in, egain, hidden, out_grad,
        gain, normed_t, out_grad_t, summary, sq_all, gc,
        gq.reshape(4, 256, 2048), go.reshape(4, 256, 2048),
        gk.reshape(4, 256, 2048), gv.reshape(4, 256, 2048),
    )
    cond_grad = co.astype(F32).reshape(128, 8, 32)[:, :, :28].reshape(128, 224)
    return (
        layer_out,
        hidden_grad,
        qo.reshape(128, 512).astype(F32),
        kg[:28],
        vg[:28],
        oo.reshape(128, 512).T.astype(F32),
        cond_grad,
    )


def solution(mesh):
    placed = (
        P("dp", "enc"), P(), P("dp", "enc"), P("dp", "enc"), P("dp", "enc"), P("enc", "dp"),
        P("dp", "enc"), P(), P(("dp", "enc"), None, None), P(("dp", "enc")), P("dp", "enc"),
    )
    return jax.shard_map(
        shards,
        mesh=mesh,
        in_specs=placed,
        out_specs=(
            P("dp", "enc"), P("dp", "enc"), P("dp", "enc"), P("dp", "enc"), P("dp", "enc"),
            P("enc", "dp"), P("dp", "enc"),
        ),
        check_vma=False,
    )
```

```python
import functools

import jax
import jax.numpy as jnp
from jax import lax
from jax.experimental import pallas as pl
from jax.experimental.pallas import tpu as pltpu
from jax.sharding import PartitionSpec as P

MESH = pl.DeviceIdType.MESH
F32 = jnp.float32
BF16 = jnp.bfloat16
HSZ = 128
SPAN = 64
NL = 128
DE = 896
PE = 1024
EPS = 1e-05
ANY = pl.BlockSpec(memory_space=pl.ANY)
VM = pl.BlockSpec(memory_space=pltpu.VMEM)
DMA = pltpu.SemaphoreType.DMA


def place():
    d = lax.axis_index("dp")
    return d // 8, (d // 2) % 4, d % 2, lax.axis_index("enc")


def at(x, z, c, y):
    return ((x * 4 + z) * 2 + c, y)


def around(v, k):
    return (v + k) % 4


def remote(src, dst, send, recv, device):
    copy = pltpu.make_async_remote_copy(
        src, dst, send, recv, device_id=device, device_id_type=MESH
    )
    copy.start()
    return copy


def meet(peers, partner=None, has_partner=None):
    barrier = pltpu.get_barrier_semaphore()
    for peer in peers:
        pl.semaphore_signal(barrier, inc=1, device_id=peer, device_id_type=MESH)
    if partner is not None:

        @pl.when(has_partner)
        def _():
            pl.semaphore_signal(barrier, inc=1, device_id=partner, device_id_type=MESH)

        pl.semaphore_wait(barrier, jnp.where(has_partner, len(peers) + 1, len(peers)))
    else:
        pl.semaphore_wait(barrier, len(peers))


def sum_rows(out, terms, step=16):
    rows = out.shape[0]

    def body(i, carry):
        at_row = pl.ds(pl.multiple_of(i * step, step), step)
        total = terms[0][at_row].astype(F32)
        for t in terms[1:]:
            total = total + t[at_row].astype(F32)
        out[at_row] = total.astype(out.dtype)
        return carry

    lax.fori_loop(0, rows // step, body, 0)


def cols(i, n):
    return pl.ds(pl.multiple_of(i * n, n), n)


def pick_rows(ids_s, r):
    every = [ids_s[r, 0, k] for k in range(4)]
    owner = [(v // 8) % 4 for v in every]
    row = [v % 8 for v in every]
    rank = []
    for k in range(4):
        n = jnp.int32(0)
        for j in range(k):
            n = n + jnp.where(owner[j] == owner[k], 1, 0)
        rank.append(n)
    return owner, row, rank


class Plane:
    def __init__(self, put, line, cut, whole, axes, sems):
        self.put, self.line, self.cut, self.whole = put, line, cut, whole
        self.x, self.z, self.xp, self.zp, self.sib = axes
        self.s, self.r = sems
        self.one, self.two, self.on, self.last = [[], []], [[], []], [[], []], None

    def first(self):
        for h in range(2):
            src, dst, keep = self.put(h)
            for k in (2, 1, 3):
                peer = (self.zp if h else self.xp)[k - 1]
                self.one[h].append(remote(src, dst, self.s.at[h, k], self.r.at[h, k], peer))
            if keep is not None:
                copy = pltpu.make_async_copy(src, dst, self.s.at[h, 0])
                copy.start()
                copy.wait()

    def second(self):
        for h in range(2):
            for copy in self.one[h]:
                copy.wait_recv()
            block = self.line(h, self.x if h else self.z)
            for k in (1, 3):
                peer = (self.xp if h else self.zp)[k - 1]
                self.two[h].append(
                    remote(block, block, self.s.at[h, 3 + k], self.r.at[h, 3 + k], peer)
                )

    def relay(self):
        for h in range(2):
            place = self.x if h else self.z
            for j, k in ((0, 1), (1, 3)):
                self.two[h][j].wait_recv()
                block = self.cut(h, around(place, 4 - k), j)
                peer = (self.xp if h else self.zp)[k - 1]
                self.on[h].append(
                    remote(block, block, self.s.at[h, 7 + k], self.r.at[h, 7 + k], peer)
                )

    def swap(self):
        for copy in self.on[0] + self.on[1]:
            copy.wait_recv()
        self.last = remote(self.whole, self.whole, self.s.at[0, 5], self.r.at[0, 5], self.sib)

    def sent(self):
        every = self.one[0] + self.one[1] + self.two[0] + self.two[1]
        for copy in every + self.on[0] + self.on[1] + [self.last]:
            copy.wait_send()


class Sums:
    def __init__(self, p, bufs, y, right, left, sems):
        self.p, self.y, self.right, self.left = p, y, right, left
        self.far_a, self.far_b, self.from_left, self.from_right = bufs
        self.s, self.r = sems
        self.far, self.near, self.late = [], [], []

    def send(self, n, src, dst, peer):
        return remote(src, dst, self.s.at[n], self.r.at[n], peer)

    def first(self):
        p, y = self.p, self.y
        a, b = pl.ds(0, 64), pl.ds(64, 64)
        self.far = [
            self.send(0, p.at[around(y, 2), a], self.far_a, self.right),
            self.send(1, p.at[around(y, 2), b], self.far_b, self.left),
        ]
        self.near = [
            self.send(2, p.at[around(y, 1), b], self.from_left.at[b], self.right),
            self.send(3, p.at[around(y, 3), a], self.from_right.at[a], self.left),
        ]

    def second(self):
        p, y = self.p, self.y
        moves = (
            (0, self.far_a, around(y, 1), 0, self.from_left, self.right),
            (1, self.far_b, around(y, 3), 64, self.from_right, self.left),
        )
        for n, far, target, low, dst, peer in moves:
            self.far[n].wait_recv()

            def fold(i, carry, far=far, target=target, low=low):
                rows = pl.ds(pl.multiple_of(low + i * 16, 16), 16)
                more = far[pl.ds(pl.multiple_of(i * 16, 16), 16)].astype(F32)
                p[target, rows] = (p[target, rows].astype(F32) + more).astype(BF16)
                return carry

            lax.fori_loop(0, 4, fold, 0)
            half = pl.ds(low, 64)
            self.late.append(self.send(4 + n, p.at[target, half], dst.at[half], peer))

    def third(self, out):
        for copy in self.near + self.late:
            copy.wait_recv()
        sum_rows(out, [self.p.at[self.y], self.from_left, self.from_right])

    def sent(self):
        for copy in self.far + self.near + self.late:
            copy.wait_send()


def forward_kernel(
    ids_in, gain, xs, og_h, egain, store, wq, wo_in, wc_in, wk_in, wv_in,
    sq_all, sm, q, a, keys, values, enc_h, ein_h, nt_h, ogt_h, hq, ho, hc, hk, hv,
    ids_all, ids_s, out_rows, in_rows, tq, to, tc, yk, yv, gq, go, gc, gk, gv,
    normed, qp, ap, cp, q0, q1, q2, q3, a0, a1, a2, a3, rc,
    ids, sq, line_up, means, pick_cols, wo, wc, wk, wv,
    s_small, r_small, s_row, r_row, s_t, r_t, s_p, r_p, s_w, r_w, s_y, r_y, s_q, r_q, s_a, r_a,
    s_loc, s_out, og, enc, ein, nt, ogt,
):
    load = pltpu.make_async_copy(og_h, og, s_loc.at[1])
    load.start()
    x, z, c, y = place()
    yp = [at(x, z, c, around(y, k)) for k in (1, 2, 3)]
    xp = [at(around(x, k), z, c, y) for k in (1, 2, 3)]
    zp = [at(x, around(z, k), c, y) for k in (1, 2, 3)]
    sib = at(x, z, 1 - c, y)
    partner = at(y, z, c, x)
    axes = (x, z, xp, zp, sib)
    meet(yp + xp + zp + [sib], partner, x != y)

    moves = ((wq, tq), (wo, to), (wc, tc))

    def cross(n):
        w, t = moves[n]

        @pl.when(x != y)
        def _():
            remote(w, t, s_t.at[n], r_t.at[n], partner)

        @pl.when(x == y)
        def _():
            pltpu.make_async_copy(w, t, r_t.at[n]).start()

    def arrived(n):
        w, t = moves[n]
        pltpu.make_async_copy(w, t, r_t.at[n]).wait()

    cross(0)
    ids[...] = jnp.zeros_like(ids)
    ids[0:1, 0:4] = ids_in[...]
    small = []
    for k in (1, 2, 3):
        small.append(remote(ids, ids_all.at[y], s_small.at[0, k], r_small.at[0, k], yp[k - 1]))
    ids_all[y] = ids[...]
    line_up[...] = jnp.zeros_like(line_up)
    for j in range(4):
        part = xs[128 * j : 128 * (j + 1)].astype(F32)
        line_up[:, j : j + 1] = jnp.sum(part * part, axis=-1, keepdims=True)
        for i in range(2):
            row = jnp.sum(part[64 * i : 64 * i + 64], axis=0, keepdims=True) / SPAN
            means[2 * j + i : 2 * j + i + 1] = row
    sm[...] = means[...].astype(BF16)
    sq[...] = line_up[...].T[:8]
    sq_all[y] = sq[...]
    for k in (1, 2, 3):
        small.append(remote(sq, sq_all.at[y], s_small.at[1, k], r_small.at[1, k], yp[k - 1]))
    wo[...] = wo_in[...].T
    spot = lax.broadcasted_iota(jnp.int32, (1, PE), 1)
    source = jnp.where(spot % 32 < 28, spot // 32 * 28 + spot % 32, -1)
    for i in range(7):
        row = lax.broadcasted_iota(jnp.int32, (128, PE), 0) + 128 * i
        pick_cols[128 * i : 128 * (i + 1)] = jnp.where(row == source, 1.0, 0.0).astype(BF16)
    wc[...] = dot_nn(wc_in[...], pick_cols[0:224, 0:256]).astype(BF16)
    for w, v in ((wk, wk_in), (wv, wv_in)):
        w[...] = jnp.zeros_like(w)
        w[0:28] = v[...]
    for copy in small[:3]:
        copy.wait_recv()
    to_s = pltpu.make_async_copy(ids_all, ids_s, s_loc.at[0])
    to_s.start()
    to_s.wait()

    row_copies = []
    for k in (2, 1, 3, 0):
        owner, row, rank = pick_rows(ids_s, around(y, k))
        for n in range(2):
            pick = jnp.int32(0)
            for j in range(4):
                pick = pick + jnp.where((owner[j] == y) & (rank[j] == n), row[j], 0)
            if k:
                out_rows[k, n] = store[pick]
            else:
                in_rows[y, n] = store[pick]
        if k:
            row_copies.append(
                remote(out_rows.at[k], in_rows.at[y], s_row.at[k], r_row.at[k], yp[k - 1])
            )

    def weight(n, t, g, w):
        def put(h):
            rows = pl.ds(64 * h, 64)
            return t.at[rows], g.at[z, c, rows, cols(x, w)], True

        def line(h, i):
            if h:
                return g.at[:, c, pl.ds(64, 64), cols(i, w)]
            return g.at[i, c, pl.ds(0, 64)]

        def cut(h, i, j):
            if h:
                return g.at[:, c, pl.ds(64 + 32 * j, 32), cols(i, w)]
            return g.at[i, c, pl.ds(32 * j, 32)]

        return Plane(put, line, cut, g.at[:, c], axes, (s_p.at[n], r_p.at[n]))

    pq, po, pc = weight(0, tq, gq, 512), weight(1, to, go, 512), weight(2, tc, gc, 256)

    def kv_put(h):
        return (yv, gv.at[x, z, c], True) if h else (yk, gk.at[x, z, c], True)

    def kv_line(h, i):
        return gv.at[i, :, c] if h else gk.at[:, i, c]

    def kv_cut(h, i, j):
        if h:
            return gv.at[i, pl.ds(2 * j, 2), c]
        return gk.at[pl.ds(2 * j, 2), i, c]

    pk = KeyPlane(
        kv_put, kv_line, kv_cut, (gk.at[:, :, c], gv.at[:, :, c]), axes, (s_p.at[3], r_p.at[3])
    )
    rq = Sums(qp, (q0, q1, q2, q3), y, yp[0], yp[2], (s_q, r_q))
    ra = Sums(ap, (a0, a1, a2, a3), y, yp[0], yp[2], (s_a, r_a))

    arrived(0)
    cross(2)
    cross(1)
    pq.first()
    across = []
    for n, (w, t) in enumerate(((wk, yk), (wv, yv))):
        for k in (2, 1, 3):
            across.append(
                remote(w, t.at[:, cols(y, 512)], s_w.at[n, k], r_w.at[n, k], yp[k - 1])
            )
        t[:, cols(y, 512)] = w[...]
    pq.second()
    arrived(2)
    pc.first()
    for copy in small[3:]:
        copy.wait_recv()
    total = sq_all[0] + sq_all[1] + sq_all[2] + sq_all[3]
    rstd = lax.rsqrt(total / 4096 + EPS).T
    for j in range(4):
        rows = slice(128 * j, 128 * (j + 1))
        normed[rows] = (xs[rows].astype(F32) * rstd[:, j : j + 1] * gain[:, cols(y, 1024)]).astype(BF16)
    arrived(1)
    po.first()
    pq.relay()
    pc.second()
    po.second()
    pq.swap()
    outs = []

    def keep(n, g, h):
        copy = pltpu.make_async_copy(g, h, s_out.at[n])
        copy.start()
        outs.append(copy)

    def product(act, g, put):
        def tile(i, carry):
            lanes = cols(i, 256)
            put(lanes, dot_nn(act[...], g[..., lanes].reshape(1024, 256)).astype(BF16))
            return carry

        lax.fori_loop(0, 8, tile, 0)

    def into(p):
        def put(lanes, value):
            p[:, :, lanes] = value.reshape(4, 128, 256)

        return put

    pq.last.wait_recv()
    product(normed, gq, into(qp))
    rq.first()
    keep(0, gq, hq)
    pc.relay()
    po.relay()
    for copy in across:
        copy.wait_recv()
    pk.first()
    pc.swap()
    pc.last.wait_recv()
    keep(2, gc, hc)
    for i in range(4):
        lanes = slice(256 * i, 256 * (i + 1))
        w = gc[:, :, :, lanes].reshape(1024, 256)
        cp[:, lanes] = dot_nn(sm[...], w)
    for j in range(4):
        rc[j + 4] = cp[2 * j : 2 * j + 2]
    parts = []
    for k in (2, 1, 3):
        parts.append(
            remote(rc.at[4 + around(y, k)], rc.at[k], s_y.at[k], r_y.at[k], yp[k - 1])
        )
    rq.second()
    po.swap()
    pk.second()
    po.last.wait_recv()
    load.wait()
    product(og, go, into(ap))
    ra.first()
    keep(1, go, ho)
    for copy in row_copies:
        copy.wait_recv()
    owner, row, rank = pick_rows(ids_s, y)
    for k in range(4):
        rows = slice(128 * k, 128 * (k + 1))
        ein[rows] = dot_nn(in_rows[owner[k], jnp.minimum(rank[k], 1)], pick_cols[...])
    pk.relay()
    for copy in parts:
        copy.wait_recv()
    cond = (rc[4 + y] + rc[1] + rc[2] + rc[3]).astype(BF16).astype(F32)
    for k in range(4):
        rows = slice(128 * k, 128 * (k + 1))
        row = ein[rows] + cond[k // 2 : k // 2 + 1]
        ein[rows] = row
        scale = lax.rsqrt(jnp.sum(row * row, axis=-1, keepdims=True) / DE + EPS)
        enc[rows] = (row * scale * egain[...]).astype(BF16)
    keep(5, enc, enc_h)
    keep(6, ein, ein_h)
    ra.second()
    pk.swap()
    for j in range(4):
        rows = slice(128 * j, 128 * (j + 1))
        nt[:, rows] = normed[rows].T
        ogt[:, rows] = og[rows].T
    keep(7, nt, nt_h)
    keep(8, ogt, ogt_h)
    rq.third(q)
    for n, (g, h, out) in enumerate(((gk, hk, keys), (gv, hv, values))):
        pk.last[n].wait_recv()
        keep(3 + n, g, h)

        def put(lanes, value, out=out):
            out[:, lanes] = value

        product(enc, g, put)
    ra.third(a)
    for copy in outs:
        copy.wait()
    for copy in small + across + row_copies + parts:
        copy.wait_send()
    for plane in (pq, po, pc, pk, rq, ra):
        plane.sent()

    @pl.when(x != y)
    def _():
        for n, (w, t) in enumerate(moves):
            pltpu.make_async_copy(w, t, s_t.at[n]).wait()


class KeyPlane(Plane):
    def swap(self):
        for copy in self.on[0] + self.on[1]:
            copy.wait_recv()
        self.last = [
            remote(ref, ref, self.s.at[n, 5], self.r.at[n, 5], self.sib)
            for n, ref in enumerate(self.whole)
        ]

    def sent(self):
        every = self.one[0] + self.one[1] + self.two[0] + self.two[1]
        for copy in every + self.on[0] + self.on[1] + self.last:
            copy.wait_send()


def forward(*operands):
    wide, slim, keys = (4, 2, 128, 2048), (4, 2, 128, 1024), (4, 4, 2, 32, 2048)
    shape = jax.ShapeDtypeStruct
    halves = [
        pltpu.VMEM((64, 2048), BF16),
        pltpu.VMEM((64, 2048), BF16),
        pltpu.VMEM((128, 2048), BF16),
        pltpu.VMEM((128, 2048), BF16),
    ]
    return pl.pallas_call(
        forward_kernel,
        out_shape=(
            shape((4, 8, 128), F32),
            shape((8, 1024), BF16),
            shape((128, 2048), BF16),
            shape((128, 2048), BF16),
            shape((512, 2048), BF16),
            shape((512, 2048), BF16),
            shape((512, PE), BF16),
            shape((512, PE), F32),
            shape((1024, 512), BF16),
            shape((1024, 512), BF16),
            shape(wide, BF16),
            shape(wide, BF16),
            shape(slim, BF16),
            shape(keys, BF16),
            shape(keys, BF16),
        ),
        in_specs=[VM] * 3 + [ANY] + [VM] * 7,
        out_specs=(VM,) * 6 + (ANY,) * 9,
        scratch_shapes=[
            pltpu.VMEM((4, 8, 128), jnp.int32),
            pltpu.SMEM((4, 8, 128), jnp.int32),
            pltpu.VMEM((4, 2, NL, DE), BF16),
            pltpu.VMEM((4, 2, NL, DE), BF16),
            pltpu.VMEM((128, 512), BF16),
            pltpu.VMEM((128, 512), BF16),
            pltpu.VMEM((128, 256), BF16),
            pltpu.VMEM((32, 2048), BF16),
            pltpu.VMEM((32, 2048), BF16),
            pltpu.VMEM(wide, BF16),
            pltpu.VMEM(wide, BF16),
            pltpu.VMEM(slim, BF16),
            pltpu.VMEM(keys, BF16),
            pltpu.VMEM(keys, BF16),
            pltpu.VMEM((512, 1024), BF16),
            pltpu.VMEM((4, 128, 2048), BF16),
            pltpu.VMEM((4, 128, 2048), BF16),
            pltpu.VMEM((8, 1024), F32),
        ]
        + halves
        + halves
        + [
            pltpu.VMEM((8, 2, 1024), F32),
            pltpu.VMEM((8, 128), jnp.int32),
            pltpu.VMEM((8, 128), F32),
            pltpu.VMEM((128, 128), F32),
            pltpu.VMEM((8, 1024), F32),
            pltpu.VMEM((DE, PE), BF16),
            pltpu.VMEM((128, 512), BF16),
            pltpu.VMEM((128, 256), BF16),
            pltpu.VMEM((32, 512), BF16),
            pltpu.VMEM((32, 512), BF16),
            DMA((2, 4)), DMA((2, 4)),
            DMA((4,)), DMA((4,)),
            DMA((3,)), DMA((3,)),
            DMA((4, 2, 11)), DMA((4, 2, 11)),
            DMA((2, 4)), DMA((2, 4)),
            DMA((4,)), DMA((4,)),
            DMA((6,)), DMA((6,)),
            DMA((6,)), DMA((6,)),
            DMA((2,)),
            DMA((9,)),
            pltpu.VMEM((512, 1024), BF16),
            pltpu.VMEM((512, PE), BF16),
            pltpu.VMEM((512, PE), F32),
            pltpu.VMEM((1024, 512), BF16),
            pltpu.VMEM((1024, 512), BF16),
        ],
        compiler_params=pltpu.CompilerParams(
            collective_id=0, has_side_effects=True, vmem_limit_bytes=58 << 20
        ),
        name="forward",
    )(*operands)


def dot_nn(a, b):
    return jnp.dot(a, b, preferred_element_type=F32)


def dot_nt(a, b):
    return lax.dot_general(a, b, (((1,), (1,)), ((), ())), preferred_element_type=F32)


def dot_tn(a, b):
    return lax.dot_general(a, b, (((0,), (0,)), ((), ())), preferred_element_type=F32)


class Around:
    def __init__(self, half, bufs, place, right, left, sems, base):
        self.half, self.place, self.right, self.left = half, place, right, left
        self.far, self.from_left, self.from_right = bufs
        self.s, self.r, self.base = sems[0], sems[1], base
        self.sends = []

    def send(self, n, src, dst, peer):
        n = self.base + n
        self.sends.append(remote(src, dst, self.s.at[n], self.r.at[n], peer))

    def first(self):
        half, p = self.half, self.place
        self.send(0, half(around(p, 2), 0), self.far.at[0], self.right)
        self.send(1, half(around(p, 2), 1), self.far.at[1], self.left)
        self.send(2, half(around(p, 1), 1), self.from_left.at[1], self.right)
        self.send(3, half(around(p, 3), 0), self.from_right.at[0], self.left)

    def mid(self):
        moves = ((0, 1, self.from_left, self.right), (1, 3, self.from_right, self.left))
        for n, k, dst, peer in moves:
            self.sends[n].wait_recv()
            own = self.half(around(self.place, k), n)
            own[...] = (own[...].astype(F32) + self.far[n].astype(F32)).astype(BF16)
            self.send(4 + n, own, dst.at[n], peer)

    def here(self):
        for copy in self.sends[2:]:
            copy.wait_recv()

    def total(self, i):
        own = self.half(self.place, i)[...].astype(F32)
        return (own + self.from_left[i].astype(F32) + self.from_right[i].astype(F32)).astype(BF16)

    def sent(self):
        for copy in self.sends:
            copy.wait_send()


class Halves:
    def __init__(self, p, bufs, out, w, spots, sems):
        self.p, self.out, self.w = p, out, w
        self.b, fa, la, ra, fb, lb, rb, self.wa, self.wb, self.va, self.vb, self.f = bufs
        self.x, self.z, self.c, self.y, self.xp, self.zp, self.sib = spots
        self.s, self.r = sems
        self.two, self.swapped = [[], []], None
        b = self.b
        self.ringa = Around(
            lambda t, i: b.at[t, 0, i], (fa, la, ra), self.z, self.zp[0], self.zp[2], sems, 14
        )
        self.ringb = Around(
            lambda t, i: b.at[:, 1, i, :, cols(t, w)], (fb, lb, rb), self.x, self.xp[0],
            self.xp[2], sems, 20,
        )

    def swap(self):
        src = self.p.at[:, pl.ds(2 * (1 - self.c), 2)]
        self.swapped = remote(src, self.b, self.s.at[0], self.r.at[0], self.sib)

    def first(self):
        self.swapped.wait_recv()
        p, b, c = self.p, self.b, self.c

        def fold(i, carry):
            j, h, k = i // 4, (i // 2) % 2, i % 2
            b[j, h, k] = (p[j, 2 * c + h, k].astype(F32) + b[j, h, k].astype(F32)).astype(BF16)
            return carry

        lax.fori_loop(0, 16, fold, 0)
        self.ringa.first()
        self.ringb.first()

    def mid(self):
        self.ringa.mid()
        self.ringb.mid()

    def second(self):
        wa, wb = self.wa, self.wb
        self.ringa.here()
        for i in range(2):
            wa[i] = self.ringa.total(i)
        for k in (2, 1, 3):
            lanes = cols(around(self.x, k), self.w)
            self.two[0].append(
                remote(wa.at[:, :, lanes], self.va.at[k - 1], self.s.at[6 + k], self.r.at[6 + k], self.xp[k - 1])
            )
        self.ringb.here()
        for i in range(2):
            wb[:, i] = self.ringb.total(i)
        for k in (2, 1, 3):
            self.two[1].append(
                remote(wb.at[around(self.z, k)], self.vb.at[k - 1], self.s.at[9 + k], self.r.at[9 + k], self.zp[k - 1])
            )

    def third(self):
        x, y, z, f, va, vb = self.x, self.y, self.z, self.f, self.va, self.vb
        for copy in self.two[0] + self.two[1]:
            copy.wait_recv()
        for i in range(2):
            f[0, i] = (
                self.wa[i, :, cols(x, self.w)].astype(F32) + va[0, i].astype(F32)
                + va[1, i].astype(F32) + va[2, i].astype(F32)
            ).astype(BF16)
            f[1, i] = (
                self.wb[z, i].astype(F32) + vb[0, i].astype(F32)
                + vb[1, i].astype(F32) + vb[2, i].astype(F32)
            ).astype(BF16)

        @pl.when(x != y)
        def _():
            remote(f, self.out, self.s.at[13], self.r.at[13], at(y, z, self.c, x))

        @pl.when(x == y)
        def _():
            pltpu.make_async_copy(f, self.out, self.r.at[13]).start()

    def end(self):
        pltpu.make_async_copy(self.f, self.out, self.r.at[13]).wait()
        for copy in self.two[0] + self.two[1]:
            copy.wait_send()
        self.ringa.sent()
        self.ringb.sent()

        @pl.when(self.x != self.y)
        def _():
            pltpu.make_async_copy(self.f, self.out, self.s.at[13]).wait()


def backward_kernel(
    att, qag, kag, vag, enc, ein_h, egain, xs_h, og_h, gain, nt_h, ogt_h, sm, sq, gc_h,
    gq, go, gk, gv,
    layer, hidden, qo, oo, co, ko, vo,
    tile, et, att_all, qag_all, cd_all, rs_all, p1, p2, p3, line_up, erstd, emean, rsum, sgrad, slot,
    *scratch,
):
    b_k, b_v, ak, lk, rk, av, lv, rv, w_k, w_v, x_k, x_v, f_k, f_v = scratch[:14]
    bq, bo, bc = scratch[14:26], scratch[26:38], scratch[38:50]
    s_y, r_y, s_d, r_d, s_c, r_c, s_1, r_1, s_2, r_2, s_3, r_3, s_h, r_h, s_tile = scratch[50:65]
    ein, xs, og, ogt, gc, s_in = scratch[65:]
    nt = et
    loads = [
        pltpu.make_async_copy(h, v, s_in.at[n])
        for n, (h, v) in enumerate(
            ((ein_h, ein), (xs_h, xs), (og_h, og), (ogt_h, ogt), (gc_h, gc), (nt_h, nt))
        )
    ]
    for copy in loads[:5]:
        copy.start()
    x, z, c, y = place()
    yp = [at(x, z, c, around(y, k)) for k in (1, 2, 3)]
    xp = [at(around(x, k), z, c, y) for k in (1, 2, 3)]
    zp = [at(x, around(z, k), c, y) for k in (1, 2, 3)]
    sib = at(x, z, 1 - c, y)
    meet(yp + xp + zp + [sib], at(y, z, c, x), x != y)
    spots = (x, z, c, y, xp, zp, sib)
    rq = Halves(p1, bq, qo, 512, spots, (s_h.at[0], r_h.at[0]))
    ro = Halves(p2, bo, oo, 512, spots, (s_h.at[1], r_h.at[1]))
    rc = Halves(p3, bc, co, 256, spots, (s_h.at[2], r_h.at[2]))

    ring = []
    for n, (src, dst) in enumerate(((att, att_all), (qag, qag_all))):
        for j, k in ((0, 1), (1, 3)):
            ring.append(remote(src, dst.at[y], s_y.at[n, j], r_y.at[n, j], yp[k - 1]))
    et[...] = enc[...].T

    def product(left, right, p, width=256):
        def step(i, carry):
            lanes = cols(i, width)
            r = right[..., lanes].reshape(left.shape[1], width)
            p[..., lanes] = dot_nn(left[...], r).astype(BF16).reshape(4, 4, 2, 32, width)
            return carry

        lax.fori_loop(0, p.shape[-1] // width, step, 0)

    swaps = []
    for n, (act, p, b) in enumerate(((kag, p1, b_k), (vag, p2, b_v))):
        product(et, act, p)
        swaps.append(remote(p.at[:, :, 1 - c], b, s_c.at[n], r_c.at[n], sib))
    loads[5].start()
    att_all[y] = att[...]
    qag_all[y] = qag[...]

    passed = []

    def relay(n, dst):
        for j, k in ((0, 1), (1, 3)):
            ring[2 * n + j].wait_recv()
            block = dst.at[around(y, 4 - k), pl.ds(64 * j, 64)]
            passed.append(remote(block, block, s_y.at[n, 2 + j], r_y.at[n, 2 + j], yp[k - 1]))

    def pair(i):
        return pl.ds(2 * i, 2)

    kring = Around(
        lambda t, i: b_k.at[pair(i), t], (ak, lk, rk), z, zp[0], zp[2], (s_1, r_1), 0
    )
    vring = Around(
        lambda t, i: b_v.at[t, pair(i)], (av, lv, rv), x, xp[0], xp[2], (s_1, r_1), 6
    )
    rings = (kring, vring)
    for n, (p, b) in enumerate(((p1, b_k), (p2, b_v))):
        swaps[n].wait_recv()

        def fold(i, carry, p=p, b=b):
            b[i // 4, i % 4] = (
                p[i // 4, i % 4, c].astype(F32) + b[i // 4, i % 4].astype(F32)
            ).astype(BF16)
            return carry

        lax.fori_loop(0, 16, fold, 0)
        rings[n].first()
    for copy in swaps:
        copy.wait_send()
    relay(0, att_all)

    def fetch(h, i, j):
        return pltpu.make_async_copy(h.at[i], tile.at[j], s_tile.at[j])

    for copy in loads:
        copy.wait()
    ee = ein[...]
    erstd[...] = lax.rsqrt(jnp.sum(ee * ee, axis=-1, keepdims=True) / DE + EPS)
    emean[...] = jnp.zeros_like(emean)
    fetch(gk, 0, 0).start()
    fetch(gv, 0, 1).start()

    def encoder(i, carry):
        lanes = cols(i, 256)
        fetch(gk, i, 0).wait()
        part = dot_nt(kag[...], tile[0])

        @pl.when(i < 3)
        def _():
            fetch(gk, i + 1, 0).start()

        fetch(gv, i, 1).wait()
        part = part + dot_nt(vag[...], tile[1])

        @pl.when(i < 3)
        def _():
            fetch(gv, i + 1, 1).start()

        ey = part.astype(BF16).astype(F32) * egain[:, lanes]
        emean[...] += jnp.sum(ein[:, lanes] * ey, axis=-1, keepdims=True)
        ry = ey * erstd[...]
        for s in range(2):
            slot[s : s + 1, lanes] = jnp.sum(ry[256 * s : 256 * s + 256], axis=0, keepdims=True)
        return carry

    lax.fori_loop(0, 4, encoder, 0)
    relay(1, qag_all)
    kring.mid()
    vring.mid()
    for copy in passed[:2]:
        copy.wait_recv()
    product(ogt, att_all, p2)
    ro.swap()
    for s in range(2):
        rows = slice(256 * s, 256 * s + 256)
        weight = erstd[rows] ** 3 * (emean[rows] / DE)
        row = slot[s : s + 1] - jnp.sum(ein[rows] * weight, axis=0, keepdims=True)
        slot[s : s + 1] = row.astype(BF16).astype(F32)
    cd_all[y] = slot[...]
    small = [remote(slot, cd_all.at[y], s_d.at[0, k], r_d.at[0, k], yp[k - 1]) for k in (1, 2, 3)]


    def streamed(h, act, use):
        fetch(h, 0, 0).start()

        def step(i, carry):
            fetch(h, i, i % 2).wait()

            @pl.when(i < 3)
            def _():
                fetch(h, i + 1, (i + 1) % 2).start()

            use(cols(i, 256), dot_nt(act[...].reshape(512, 2048), tile[i % 2]))
            return carry

        lax.fori_loop(0, 4, step, 0)

    ro.first()
    for copy in passed[2:]:
        copy.wait_recv()
    product(nt, qag_all, p1)
    rq.swap()
    sent2 = []
    for n, (w, v) in enumerate(((w_k, x_k), (w_v, x_v))):
        rings[n].here()
        for i in range(2):
            w[pair(i)] = rings[n].total(i)
        for k in (2, 1, 3):
            if n:
                src, peer = w.at[around(z, k)], zp[k - 1]
            else:
                src, peer = w.at[around(x, k)], xp[k - 1]
            sent2.append(remote(src, v.at[k - 1], s_2.at[n, k], r_2.at[n, k], peer))
    ro.mid()

    def add_out(lanes, value):
        layer[:, lanes] = (xs[:, lanes].astype(F32) + value).astype(BF16)

    streamed(go, att_all, add_out)
    rq.first()
    for copy in small:
        copy.wait_recv()
    cd = cd_all[...].reshape(8, 1024).astype(BF16)
    for i in range(4):
        lanes = slice(256 * i, 256 * i + 256)
        p3[..., lanes] = dot_tn(sm[...], cd[:, lanes]).astype(BF16).reshape(4, 4, 2, 32, 256)
    rc.swap()
    ro.second()
    sent3 = []
    for n, (w, v, f) in enumerate(((w_k, x_k, f_k), (w_v, x_v, f_v))):
        for copy in sent2[3 * n : 3 * n + 3]:
            copy.wait_recv()
        own = w[z] if n else w[x]
        f[0] = (
            own.astype(F32) + v[0].astype(F32) + v[1].astype(F32) + v[2].astype(F32)
        ).astype(BF16)
        for k in (2, 1, 3):
            src, dst = f.at[0, :, cols(around(y, k), 512)], f.at[k, :, pl.ds(0, 512)]
            sent3.append(remote(src, dst, s_3.at[n, k], r_3.at[n, k], yp[k - 1]))
    rq.mid()
    rc.first()
    for i in range(4):
        sgrad[:, 256 * i : 256 * i + 256] = dot_nt(cd, gc[i].reshape(256, 1024)) / SPAN
    rsum[...] = jnp.zeros_like(rsum)

    def add_scaled(lanes, value):
        scaled = value * gain[:, pl.ds(pl.multiple_of(y * 1024 + lanes.start, 256), 256)]
        hidden[:, lanes] = scaled
        rsum[...] += jnp.sum(xs[:, lanes].astype(F32) * scaled, axis=-1, keepdims=True)

    streamed(gq, qag_all, add_scaled)
    line_up[...] = jnp.zeros_like(line_up)
    for j in range(4):
        line_up[:, j : j + 1] = rsum[128 * j : 128 * j + 128]
    rs_all[4] = line_up[...].T[:8]
    for k in (1, 2, 3):
        small.append(
            remote(rs_all.at[4], rs_all.at[y], s_d.at[1, k], r_d.at[1, k], yp[k - 1])
        )
    rs_all[y] = rs_all[4]
    ro.third()
    rq.second()
    rc.mid()
    for n, (out, f) in enumerate(((ko, f_k), (vo, f_v))):
        for copy in sent3[3 * n : 3 * n + 3]:
            copy.wait_recv()
        out[...] = (
            f[0, :, cols(y, 512)].astype(F32)
            + f[1, :, pl.ds(0, 512)].astype(F32)
            + f[2, :, pl.ds(0, 512)].astype(F32)
            + f[3, :, pl.ds(0, 512)].astype(F32)
        )
    rq.third()
    rc.second()
    for copy in small[3:]:
        copy.wait_recv()
    total = rs_all[0] + rs_all[1] + rs_all[2] + rs_all[3]
    mean = (total / 4096).T
    rstd = lax.rsqrt((sq[0] + sq[1] + sq[2] + sq[3]) / 4096 + EPS).T
    for s in range(8):
        rows, half, j = slice(64 * s, 64 * s + 64), slice(64 * (s % 2), 64 * (s % 2) + 64), s // 2
        r, m = rstd[half, j : j + 1], mean[half, j : j + 1]
        hidden[rows] = (
            og[rows].astype(F32)
            + (r * hidden[rows] - xs[rows].astype(F32) * (r * r * r * m))
            + sgrad[s : s + 1]
        )
    rc.third()
    for r in (ro, rq, rc):
        r.swapped.wait_send()
        r.end()
    for r in rings:
        r.sent()
    for copy in small + ring + passed + sent2 + sent3:
        copy.wait_send()


def halves_scratch(w):
    return [
        pltpu.VMEM((4, 2, 2, 32, 4 * w), BF16),
        *[pltpu.VMEM((2, 32, 4 * w), BF16)] * 3,
        *[pltpu.VMEM((2, 4, 32, w), BF16)] * 3,
        pltpu.VMEM((2, 32, 4 * w), BF16),
        pltpu.VMEM((4, 2, 32, w), BF16),
        pltpu.VMEM((3, 2, 32, w), BF16),
        pltpu.VMEM((3, 2, 32, w), BF16),
        pltpu.VMEM((2, 2, 32, w), BF16),
    ]


def backward(*operands):
    shape = jax.ShapeDtypeStruct
    rows = (4, 4, 2, 32)
    return pl.pallas_call(
        backward_kernel,
        out_shape=(
            shape((512, 1024), BF16),
            shape((512, 1024), F32),
            shape((2, 2, 32, 512), BF16),
            shape((2, 2, 32, 512), BF16),
            shape((2, 2, 32, 256), BF16),
            shape((32, 512), F32),
            shape((32, 512), F32),
        ),
        in_specs=[VM] * 5 + [ANY, VM, ANY, ANY, VM, ANY, ANY, VM, VM] + [ANY] * 5,
        out_specs=(VM,) * 7,
        scratch_shapes=[
            pltpu.VMEM((2, 256, 2048), BF16),
            pltpu.VMEM((1024, 512), BF16),
            pltpu.VMEM((4, 128, 2048), BF16),
            pltpu.VMEM((4, 128, 2048), BF16),
            pltpu.VMEM((4, 2, 1024), F32),
            pltpu.VMEM((5, 8, 128), F32),
            pltpu.VMEM(rows + (2048,), BF16),
            pltpu.VMEM(rows + (2048,), BF16),
            pltpu.VMEM(rows + (1024,), BF16),
            pltpu.VMEM((128, 128), F32),
            pltpu.VMEM((512, 1), F32),
            pltpu.VMEM((512, 1), F32),
            pltpu.VMEM((512, 1), F32),
            pltpu.VMEM((8, 1024), F32),
            pltpu.VMEM((2, 1024), F32),
            pltpu.VMEM((4, 4, 32, 2048), BF16),
            pltpu.VMEM((4, 4, 32, 2048), BF16),
            *[pltpu.VMEM((2, 2, 32, 2048), BF16)] * 6,
            pltpu.VMEM((4, 32, 2048), BF16),
            pltpu.VMEM((4, 32, 2048), BF16),
            pltpu.VMEM((3, 32, 2048), BF16),
            pltpu.VMEM((3, 32, 2048), BF16),
            pltpu.VMEM((4, 32, 2048), BF16),
            pltpu.VMEM((4, 32, 2048), BF16),
        ]
        + halves_scratch(512)
        + halves_scratch(512)
        + halves_scratch(256)
        + [
            DMA((2, 4)), DMA((2, 4)),
            DMA((2, 4)), DMA((2, 4)),
            DMA((2,)), DMA((2,)),
            DMA((12,)), DMA((12,)),
            DMA((2, 4)), DMA((2, 4)),
            DMA((2, 4)), DMA((2, 4)),
            DMA((3, 26)), DMA((3, 26)),
            DMA((2,)),
            pltpu.VMEM((512, PE), F32),
            pltpu.VMEM((512, 1024), BF16),
            pltpu.VMEM((512, 1024), BF16),
            pltpu.VMEM((1024, 512), BF16),
            pltpu.VMEM((4, 2, 128, 1024), BF16),
            DMA((6,)),
        ],
        compiler_params=pltpu.CompilerParams(
            collective_id=1, has_side_effects=True, vmem_limit_bytes=60 << 20
        ),
        name="backward",
    )(*operands)


def attention_kernel(q_ref, g_ref, k_ref, v_ref, att_ref, qag_ref, kag_ref, vag_ref):
    scale = HSZ ** (-0.5)
    spots = []
    for h in range(q_ref.shape[1] // HSZ):
        lanes = slice(h * HSZ, (h + 1) * HSZ)
        for s in range(2):
            rows, keys = slice(s * SPAN, (s + 1) * SPAN), slice(s * 2 * NL, (s + 1) * 2 * NL)
            spots.append(((rows, lanes), (keys, lanes)))
    scores = [dot_nt(q_ref[r], k_ref[k]) * scale for r, k in spots]
    pgs = [dot_nt(g_ref[r], v_ref[k]) for r, k in spots]
    tops = [jnp.max(s, axis=-1, keepdims=True) for s in scores]
    es = [jnp.exp(s - m) for s, m in zip(scores, tops)]
    sums = [jnp.sum(e, axis=-1, keepdims=True) for e in es]
    fulls = [e / t for e, t in zip(es, sums)]
    weights = [f.astype(BF16) for f in fulls]
    dots = [jnp.sum(f * p, axis=-1, keepdims=True) for f, p in zip(fulls, pgs)]
    sgs = [(f * (p - d) * scale).astype(BF16) for f, p, d in zip(fulls, pgs, dots)]
    for (r, k), w in zip(spots, weights):
        att_ref[r] = dot_nn(w, v_ref[k]).astype(BF16)
    for (r, k), sg in zip(spots, sgs):
        qag_ref[r] = dot_nn(sg, k_ref[k]).astype(BF16)
    for (r, k), sg in zip(spots, sgs):
        kag_ref[k] = dot_tn(sg, q_ref[r]).astype(BF16)
    for (r, k), w in zip(spots, weights):
        vag_ref[k] = dot_tn(w, g_ref[r]).astype(BF16)


def attention(q, g, k, v):
    few = pl.BlockSpec((128, 512), lambda h: (0, h))
    many = pl.BlockSpec((512, 512), lambda h: (0, h))
    return pl.pallas_call(
        attention_kernel,
        grid=(4,),
        out_shape=(
            jax.ShapeDtypeStruct((128, 2048), BF16),
            jax.ShapeDtypeStruct((128, 2048), BF16),
            jax.ShapeDtypeStruct((512, 2048), BF16),
            jax.ShapeDtypeStruct((512, 2048), BF16),
        ),
        in_specs=[few, few, many, many],
        out_specs=(few, few, many, many),
        name="attention",
    )(q, g, k, v)


def shards(
    hidden, norm_gain, w_query, w_key, w_value, w_out, w_cond, enc_gain, store, neighbour_ids,
    out_grad,
):
    egain = jnp.pad(enc_gain.reshape(32, 28), ((0, 0), (0, 4))).reshape(1, PE)
    gain = norm_gain.reshape(1, 4096)
    (
        sq_all, summary, q, ag, keys, values, encoded, enc_in, normed_t, out_grad_t,
        gq, go, gc, gk, gv,
    ) = forward(
        neighbour_ids.reshape(1, 4), gain, hidden, out_grad, egain, store,
        w_query, w_out, w_cond, w_key, w_value,
    )
    att, qag, kag, vag = attention(q, ag, keys, values)
    layer_out, hidden_grad, qo, oo, co, kg, vg = backward(
        att, qag, kag, vag, encoded, enc_in, egain, hidden, out_grad,
        gain, normed_t, out_grad_t, summary, sq_all, gc,
        gq.reshape(4, 256, 2048), go.reshape(4, 256, 2048),
        gk.reshape(4, 256, 2048), gv.reshape(4, 256, 2048),
    )
    cond_grad = co.astype(F32).reshape(128, 8, 32)[:, :, :28].reshape(128, 224)
    return (
        layer_out,
        hidden_grad,
        qo.reshape(128, 512).astype(F32),
        kg[:28],
        vg[:28],
        oo.reshape(128, 512).T.astype(F32),
        cond_grad,
    )


def solution(mesh):
    placed = (
        P("dp", "enc"), P(), P("dp", "enc"), P("dp", "enc"), P("dp", "enc"), P("enc", "dp"),
        P("dp", "enc"), P(), P(("dp", "enc"), None, None), P(("dp", "enc")), P("dp", "enc"),
    )
    return jax.shard_map(
        shards,
        mesh=mesh,
        in_specs=placed,
        out_specs=(
            P("dp", "enc"), P("dp", "enc"), P("dp", "enc"), P("dp", "enc"), P("dp", "enc"),
            P("enc", "dp"), P("dp", "enc"),
        ),
        check_vma=False,
    )
```
